32 devices in a mesh: section: 2 (over y), tensor: 2 (over core), dp: 8 (over z, x).
Axes of the slice: x: 2, y: 2, z: 4, core: 2. Of those that a mesh axis runs over, the one named last changes fastest.
Arguments:
- patches: bfloat16 [18688, 768], P('dp'), may hold values from -6 to 6
- out_grad: bfloat16 [18688, 768], P('dp'), may hold values from -6 to 6
- large_place: int32 [16], P('dp'), may hold values from 0 to 3, as said below
- norm1_gain: float32 [2, 768], P('section'), may hold values from 0.5 to 1.5
- norm1_bias: float32 [2, 768], P('section'), may hold values from -1.75 to 1.75
- qkv_weight: bfloat16 [2, 3, 768, 768], P('section', None, None, 'tensor'), may hold values from -0.21875 to 0.21875
- qv_bias: float32 [2, 2, 768], P('section', None, 'tensor'), may hold values from -1.75 to 1.75
- proj_weight: bfloat16 [2, 768, 768], P('section', 'tensor'), may hold values from -1.75 to 1.75
- proj_bias: float32 [2, 768], P('section'), may hold values from -1.75 to 1.75
- norm2_gain: float32 [2, 768], P('section'), may hold values from 0.5 to 1.5
- norm2_bias: float32 [2, 768], P('section'), may hold values from -1.75 to 1.75
- up_weight: bfloat16 [2, 768, 3072], P('section', None, 'tensor'), may hold values from -0.21875 to 0.21875
- up_bias: float32 [2, 3072], P('section', 'tensor'), may hold values from -1.75 to 1.75
- down_weight: bfloat16 [2, 3072, 768], P('section', 'tensor'), may hold values from -0.109375 to 0.109375
- down_bias: float32 [2, 768], P('section'), may hold values from -1.75 to 1.75
Outputs:
- layer_outputs: bfloat16 [2, 18688, 768], P('section', 'dp')
- layer_input_grads: bfloat16 [2, 18688, 768], P('section', 'dp')
- grad_norm1_gain: float32 [2, 768], P('section')
- grad_norm1_bias: float32 [2, 768], P('section')
- grad_qkv_weight: float32 [2, 3, 768, 768], P('section', None, None, 'tensor')
- grad_qv_bias: float32 [2, 2, 768], P('section', None, 'tensor')
- grad_proj_weight: float32 [2, 768, 768], P('section', 'tensor')
- grad_proj_bias: float32 [2, 768], P('section')
- grad_norm2_gain: float32 [2, 768], P('section')
- grad_norm2_bias: float32 [2, 768], P('section')
- grad_up_weight: float32 [2, 768, 3072], P('section', None, 'tensor')
- grad_up_bias: float32 [2, 3072], P('section', 'tensor')
- grad_down_weight: float32 [2, 3072, 768], P('section', 'tensor')
- grad_down_bias: float32 [2, 768], P('section')
The draws below stay inside these ranges and needn't reach their ends.
Inputs may be any that keep to these rules, and one draw needn't show every extreme that they name: `large_place`: the large image's slot within its micro-batch of 4 images; every slot occurs.
All inputs are finite; a program needn't handle non-finite values.
Results may differ from the reference program's by a relative error of at most 0.018.
Values may be sent and summed in bfloat16 or wider, within the bound.
A program may use at most 320 MiB of HBM per device.

```python
import jax
import jax.numpy as jnp
from jax import lax

D = 768
H = 12
HD = 64
FF = 3072
LEN_SMALL = 197
LEN_LARGE = 577
SMALL_MB = 3
TMB = 1168
MBS = 16
TOKENS = 18688


def draw_large_place(key, part):
    images = SMALL_MB + 1
    base_slots = jax.random.randint(jax.random.fold_in(key, 11), (MBS,), 0, images)
    offset = jax.random.randint(jax.random.fold_in(key, 12), (), 0, images)
    leading = (jnp.arange(images, dtype=jnp.int32) + offset) % images
    return base_slots.at[:images].set(leading).astype(jnp.int32)


def block_scale(key, extent, pieces, least, top_value):
    def one(axis_at, shards_of):
        steps = jax.random.uniform(jax.random.fold_in(jax.random.fold_in(key, 6), axis_at), (shards_of,), jnp.float32, least / len(pieces), top_value / len(pieces))
        return jnp.repeat(jnp.exp(steps), extent[axis_at] // shards_of).reshape((-1,) + (1,) * (len(extent) - axis_at - 1))

    loudness = one(*pieces[0])
    for cut in pieces[1:]:
        loudness = loudness * one(*cut)
    return loudness


def noise(key, extent, spread, reach, split=(), held_as=jnp.bfloat16):
    drawn = spread * jax.random.normal(key, extent, jnp.float32)
    if split:
        drawn = drawn * block_scale(key, extent, split, -0.22, 0.18)
    return jnp.clip(drawn, -reach, reach).astype(held_as)


def setup_inputs(seed: int = 0) -> dict:
    arg_keys = jax.random.split(jax.random.key(seed), 16)
    return {
        "patches": noise(arg_keys[0], (TOKENS, D), 1.0, 6.0, ((0, 8),)),
        "out_grad": noise(arg_keys[1], (TOKENS, D), 1.0, 6.0, ((0, 8),)),
        "large_place": draw_large_place(jax.random.fold_in(arg_keys[15], 71), 0),
        "norm1_gain": jnp.clip(1.0 + 0.1 * jax.random.normal(arg_keys[3], (2, D), jnp.float32), 0.5, 1.5),
        "norm1_bias": noise(arg_keys[4], (2, D), 0.3, 1.75, ((0, 2),), jnp.float32),
        "qkv_weight": noise(arg_keys[5], (2, 3, D, D), D ** -0.5, 0.21875, ((0, 2), (3, 2))),
        "qv_bias": noise(arg_keys[6], (2, 2, D), 0.3, 1.75, ((0, 2), (2, 2)), jnp.float32),
        "proj_weight": noise(arg_keys[7], (2, D, D), (D // 64) ** -0.5, 1.75, ((0, 2), (1, 2))),
        "proj_bias": noise(arg_keys[8], (2, D), 0.3, 1.75, ((0, 2),), jnp.float32),
        "norm2_gain": jnp.clip(1.0 + 0.1 * jax.random.normal(arg_keys[9], (2, D), jnp.float32), 0.5, 1.5),
        "norm2_bias": noise(arg_keys[10], (2, D), 0.3, 1.75, ((0, 2),), jnp.float32),
        "up_weight": noise(arg_keys[11], (2, D, FF), D ** -0.5, 0.21875, ((0, 2), (2, 2))),
        "up_bias": noise(arg_keys[12], (2, FF), 0.3, 1.75, ((0, 2), (1, 2)), jnp.float32),
        "down_weight": noise(arg_keys[13], (2, FF, D), FF ** -0.5, 0.109375, ((0, 2), (1, 2))),
        "down_bias": noise(arg_keys[14], (2, D), 0.3, 1.75, ((0, 2),), jnp.float32),
    }


HIGHEST = lax.Precision.HIGHEST
EPSILON = 1e-06
MASKED = -1e+30

@jax.custom_vjp
def low(v):
    return lax.optimization_barrier(v.astype(jnp.bfloat16)).astype(jnp.float32)

@jax.custom_vjp
def low_back(v):
    return v

def low_keep(v):
    return (low(v), None)

def low_pass(kept, grad):
    return (grad,)

def back_keep(v):
    return (v, None)

def back_low(kept, grad):
    return (low(grad),)
low.defvjp(low_keep, low_pass)
low_back.defvjp(back_keep, back_low)

def layer_norm(values, scale_gain, offset):
    average = lax.optimization_barrier(jnp.mean(values, axis=-1, keepdims=True))
    centred = values - average
    variance = lax.optimization_barrier(jnp.mean(centred * centred, axis=-1, keepdims=True))
    return centred * lax.rsqrt(variance + EPSILON) * scale_gain + offset

def segment_ids(large_slot, length):
    position = jnp.arange(length, dtype=jnp.int32)
    slot_marks = jnp.arange(1, SMALL_MB + 1, dtype=jnp.int32)
    starts = slot_marks * LEN_SMALL + (LEN_LARGE - LEN_SMALL) * (slot_marks > large_slot).astype(jnp.int32)
    return lax.optimization_barrier(jnp.sum((position[:, None] >= starts[None, :]).astype(jnp.int32), axis=1))

def encoder_layer(inputs, segment, layer_params):
    gain_one, offset_one, weight_qkv, bias_qv, weight_proj, bias_proj, gain_two, offset_two, weight_up, bias_up, weight_down, bias_down = layer_params
    num_rows = inputs.shape[0]
    normed = low(layer_norm(inputs, gain_one, offset_one))
    qkv_all = jnp.einsum('td,sde->ste', normed, weight_qkv, precision=HIGHEST)
    bias_all = jnp.stack([bias_qv[0], jnp.zeros_like(bias_qv[0]), bias_qv[1]])
    qkv_all = low(low_back(qkv_all + bias_all[:, None, :]))
    queries = qkv_all[0].reshape(num_rows, H, HD)
    keys_all = qkv_all[1].reshape(num_rows, H, HD)
    values_all = qkv_all[2].reshape(num_rows, H, HD)
    scores = jnp.einsum('qhd,khd->hqk', queries, keys_all, precision=HIGHEST) * HD ** (-0.5)
    same_image = segment[:, None] == segment[None, :]
    scores = low_back(jnp.where(same_image[None], scores, MASKED))
    top_score = lax.optimization_barrier(jnp.max(scores, axis=-1, keepdims=True))
    exp_scores = jnp.exp(scores - top_score)
    probabilities = low(exp_scores / lax.optimization_barrier(jnp.sum(exp_scores, axis=-1, keepdims=True)))
    attended = jnp.einsum('hqk,khd->qhd', probabilities, values_all, precision=HIGHEST).reshape(num_rows, D)
    attended = low(low_back(attended))
    branch = low_back(jnp.dot(attended, weight_proj, precision=HIGHEST) + bias_proj)
    middle = inputs + branch
    normed_two = low(layer_norm(middle, gain_two, offset_two))
    before_act = low_back(jnp.dot(normed_two, weight_up, precision=HIGHEST) + bias_up)
    activated = low(jax.nn.gelu(before_act, approximate=False))
    return middle + low_back(jnp.dot(activated, weight_down, precision=HIGHEST) + bias_down)

def reference(patches, out_grad, large_place, norm1_gain, norm1_bias, qkv_weight, qv_bias, proj_weight, proj_bias, norm2_gain, norm2_bias, up_weight, up_bias, down_weight, down_bias):
    raw_params = (norm1_gain, norm1_bias, qkv_weight, qv_bias, proj_weight, proj_bias, norm2_gain, norm2_bias, up_weight, up_bias, down_weight, down_bias)
    params = tuple((member.astype(jnp.float32) for member in raw_params))
    first_layer = tuple((member[0] for member in params))
    second_layer = tuple((member[1] for member in params))
    inputs_all = patches.astype(jnp.float32).reshape(MBS, TMB, D)
    cotangents = out_grad.astype(jnp.float32).reshape(MBS, TMB, D)
    zeros_all = tuple((jnp.zeros(member.shape, jnp.float32) for member in first_layer))

    def micro_step(state_now, member):
        totals_one, totals_two = state_now
        image_block, cotangent, large_slot = member
        segment = segment_ids(large_slot, TMB)

        def section_one(values, layer_params):
            return low(low_back(encoder_layer(values, segment, layer_params)))

        def section_two(values, layer_params):
            return encoder_layer(values, segment, layer_params)
        hidden, back_one = jax.vjp(section_one, image_block, first_layer)
        result, back_two = jax.vjp(section_two, hidden, second_layer)
        grad_hidden, grads_two = back_two(cotangent)
        grad_block, grads_one = back_one(grad_hidden)
        totals_one = tuple((previous + current for previous, current in zip(totals_one, grads_one)))
        totals_two = tuple((previous + current for previous, current in zip(totals_two, grads_two)))
        return ((totals_one, totals_two), (hidden.astype(jnp.bfloat16), result.astype(jnp.bfloat16), grad_block.astype(jnp.bfloat16), grad_hidden.astype(jnp.bfloat16)))
    (totals_one, totals_two), (hiddens, results, grad_blocks, grad_hiddens) = lax.scan(micro_step, (zeros_all, zeros_all), (inputs_all, cotangents, large_place))
    layer_outputs = jnp.stack([hiddens.reshape(TOKENS, D), results.reshape(TOKENS, D)])
    input_grads = jnp.stack([grad_blocks.reshape(TOKENS, D), grad_hiddens.reshape(TOKENS, D)])
    weight_grads = tuple((jnp.stack([one_grad, two_grad]) for one_grad, two_grad in zip(totals_one, totals_two)))
    return (layer_outputs, input_grads, weight_grads[0], weight_grads[1], weight_grads[2], weight_grads[3], weight_grads[4], weight_grads[5], weight_grads[6], weight_grads[7], weight_grads[8], weight_grads[9], weight_grads[10], weight_grads[11])
```

```python
import functools

import jax
import jax.numpy as jnp
from jax import lax
from jax.experimental import pallas as pl
from jax.experimental.pallas import tpu as pltpu
from jax.sharding import PartitionSpec as P

HD = 64
LEN_SMALL = 197
LEN_LARGE = 577
SMALL_MB = 3
EPSILON = 1e-06
MASKED = -1e30
SCALE = HD ** (-0.5)
BF = jnp.bfloat16
F32 = jnp.float32
VMEM_LIMIT = 56 * 1024 * 1024
CHUNKS = ((1, 592, LEN_LARGE), (SMALL_MB, 208, LEN_SMALL))


def params(**more):
    return pltpu.CompilerParams(vmem_limit_bytes=VMEM_LIMIT, **more)


def nn(a, b):
    return jnp.dot(a, b, preferred_element_type=F32)


def nt(a, b):
    return lax.dot_general(a, b, (((1,), (1,)), ((), ())), preferred_element_type=F32)


def tn(a, b):
    return lax.dot_general(a, b, (((0,), (0,)), ((), ())), preferred_element_type=F32)


def whole(shape):
    zeros = (0,) * len(shape)
    return pl.BlockSpec(shape, lambda *_: zeros)


def sds(shape, dtype):
    return jax.ShapeDtypeStruct(shape, dtype)


def norm_parts(values):
    mean = jnp.mean(values, axis=-1, keepdims=True)
    centred = values - mean
    rstd = lax.rsqrt(jnp.mean(centred * centred, axis=-1, keepdims=True) + EPSILON)
    return centred * rstd, rstd


def norm_back(xhat, rstd, grad, gain):
    scaled = grad * gain
    m1 = jnp.mean(scaled, axis=-1, keepdims=True)
    m2 = jnp.mean(scaled * xhat, axis=-1, keepdims=True)
    return rstd * (scaled - m1 - xhat * m2)


def rowsum(values):
    return jnp.sum(values.astype(F32), axis=0, keepdims=True)


def pre_fwd_kernel(x_ref, g_ref, b_ref, wo_ref, wp_ref, bias_ref, normed_ref, qkv_ref):
    @pl.when(pl.program_id(0) == 0)
    def _():
        xhat, _ = norm_parts(x_ref[...].astype(F32))
        normed_ref[...] = (xhat * g_ref[...] + b_ref[...]).astype(BF)

    weight = jnp.concatenate([wo_ref[0], wp_ref[0]], axis=1)
    qkv_ref[0] = (nn(normed_ref[...], weight) + bias_ref[0]).astype(BF)


def pre_fwd(x, w):
    n, d = x.shape
    half = w["wqkv_o"].shape[-1]
    return pl.pallas_call(
        pre_fwd_kernel,
        grid=(3,),
        in_specs=[
            whole((n, d)),
            whole((1, d)),
            whole((1, d)),
            pl.BlockSpec((1, d, half), lambda s: (s, 0, 0)),
            pl.BlockSpec((1, d, half), lambda s: (s, 0, 0)),
            pl.BlockSpec((1, 1, 2 * half), lambda s: (s, 0, 0)),
        ],
        out_specs=[whole((n, d)), pl.BlockSpec((1, n, 2 * half), lambda s: (s, 0, 0))],
        out_shape=[sds((n, d), BF), sds((3, n, 2 * half), BF)],
        compiler_params=params(),
        name="pre_fwd",
    )(x, w["g1"], w["b1"], w["wqkv_o"], w["wqkv_p"], w["bqkv"])


def mask_keys(scores, vlen):
    rows = scores.shape[0]
    keep = vlen // 8 * 8
    tail = scores[keep:]
    idx = lax.broadcasted_iota(jnp.int32, tail.shape, 0) + keep
    return jnp.concatenate([scores[:keep], jnp.where(idx < vlen, tail, MASKED)], axis=0)


def qblocks(plen):
    return [(q, min(256, plen - q)) for q in range(0, plen, 256)]


def attn_fwd_kernel(q_ref, k_ref, v_ref, o_ref, l_ref, *, nimg, plen, vlen):
    for im in range(nimg):
        r0 = im * plen
        k = k_ref[0, r0 : r0 + plen]
        vt = v_ref[0, r0 : r0 + plen].T
        for q0, qw in qblocks(plen):
            q = q_ref[0, r0 + q0 : r0 + q0 + qw]
            head = lax.broadcasted_iota(jnp.int32, q.shape, 1) // HD
            outs = []
            for h in range(2):
                qm = jnp.where(head == h, q, jnp.zeros_like(q))
                st = mask_keys(nt(k, qm), vlen)
                top = jnp.max(st, axis=0, keepdims=True)
                e = jnp.exp((st - top) * SCALE)
                total = jnp.sum(e, axis=0, keepdims=True)
                p = (e * (1.0 / total)).astype(BF)
                outs.append(nn(vt[h * HD : (h + 1) * HD], p))
                l_ref[0, h : h + 1, r0 + q0 : r0 + q0 + qw] = top * SCALE + jnp.log(total)
            o_ref[r0 + q0 : r0 + q0 + qw] = jnp.concatenate(outs, axis=0).T.astype(BF)


def attn_fwd(qkv, chunk):
    nimg, plen, vlen = chunk
    _, n, d = qkv.shape
    pairs = d // 128
    return pl.pallas_call(
        functools.partial(attn_fwd_kernel, nimg=nimg, plen=plen, vlen=vlen),
        grid=(pairs,),
        in_specs=[
            pl.BlockSpec((1, n, 128), lambda p, s=s: (s, 0, p)) for s in range(3)
        ],
        out_specs=[
            pl.BlockSpec((n, 128), lambda p: (0, p)),
            pl.BlockSpec((1, 2, n), lambda p: (p, 0, 0)),
        ],
        out_shape=[sds((n, d), BF), sds((pairs, 2, n), F32)],
        compiler_params=params(),
        name="attn_fwd",
    )(qkv, qkv, qkv)


def gelu_parts(x):
    cdf = 0.5 + 0.5 * lax.erf(x * (2.0**-0.5))
    pdf = jnp.exp(-0.5 * x * x) * 0.3989422804014327
    return x * cdf, cdf + x * pdf


def post_fwd_kernel(
    x_ref, att_ref, pwo_ref, pwp_ref, pb_ref, g_ref, b_ref, uo_ref, up_ref, ubo_ref, ubp_ref,
    do_ref, dp_ref, db_ref,
    mid_ref, n2_ref, ao_ref, ap_ref, go_ref, gp_ref, out_ref, acc_ref,
):
    j = pl.program_id(0)

    @pl.when(j == 0)
    def _():
        weight = jnp.concatenate([pwo_ref[...], pwp_ref[...]], axis=0)
        mid = x_ref[...].astype(F32) + (nn(att_ref[...], weight) + pb_ref[...])
        mid_ref[...] = mid
        xhat, _ = norm_parts(mid)
        n2_ref[...] = (xhat * g_ref[...] + b_ref[...]).astype(BF)
        acc_ref[...] = mid + db_ref[...]

    n2 = n2_ref[...]
    for u_ref, ub_ref, d_ref, a_ref, dg_ref in (
        (uo_ref, ubo_ref, do_ref, ao_ref, go_ref),
        (up_ref, ubp_ref, dp_ref, ap_ref, gp_ref),
    ):
        act, slope = gelu_parts(nn(n2, u_ref[...]) + ub_ref[...])
        act = act.astype(BF)
        a_ref[...] = act
        dg_ref[...] = slope.astype(BF)
        acc_ref[...] += nn(act, d_ref[...])

    @pl.when(j == pl.num_programs(0) - 1)
    def _():
        out_ref[...] = acc_ref[...].astype(BF)


def post_fwd(x, att, w):
    n, d = x.shape
    half = w["pw_o"].shape[0]
    fh = w["up_o"].shape[1]
    fb = fh // 2
    cols = lambda rows: pl.BlockSpec((rows, fb), lambda j: (0, j))
    rows_ = pl.BlockSpec((fb, d), lambda j: (j, 0))
    return pl.pallas_call(
        post_fwd_kernel,
        grid=(2,),
        in_specs=[
            whole((n, d)), whole((n, d)), whole((half, d)), whole((half, d)), whole((1, d)),
            whole((1, d)), whole((1, d)), cols(d), cols(d), cols(1), cols(1), rows_, rows_,
            whole((1, d)),
        ],
        out_specs=[
            whole((n, d)), whole((n, d)), cols(n), cols(n), cols(n), cols(n), whole((n, d)),
        ],
        out_shape=[
            sds((n, d), F32), sds((n, d), BF), sds((n, fh), BF), sds((n, fh), BF),
            sds((n, fh), BF), sds((n, fh), BF), sds((n, d), BF),
        ],
        scratch_shapes=[pltpu.VMEM((n, d), F32)],
        compiler_params=params(),
        name="post_fwd",
    )(
        x, att, w["pw_o"], w["pw_p"], w["pb"], w["g2"], w["b2"], w["up_o"], w["up_p"],
        w["ub_o"], w["ub_p"], w["dn_o"], w["dn_p"], w["db"],
    )


def forward(x, w, chunk):
    normed, qkv = pre_fwd(x, w)
    att, lse = attn_fwd(qkv, chunk)
    mid, n2, act_o, act_p, dg_o, dg_p, out = post_fwd(x, att, w)
    return (x, normed, qkv, att, lse, mid, n2, act_o, act_p, dg_o, dg_p, out)


def post_bwd_kernel(
    g_ref, mid_ref, gain_ref, go_ref, gp_ref, uo_ref, up_ref, do_ref, dp_ref, pwo_ref, pwp_ref,
    qo_ref, qp_ref, gm_ref, gb_ref, ga_ref, sums_ref, so_ref, sp_ref, acc_ref,
):
    j = pl.program_id(0)
    g = g_ref[...]

    @pl.when(j == 0)
    def _():
        acc_ref[...] = jnp.zeros_like(acc_ref)

    for dg_ref, u_ref, d_ref, q_ref, s_ref in (
        (go_ref, uo_ref, do_ref, qo_ref, so_ref),
        (gp_ref, up_ref, dp_ref, qp_ref, sp_ref),
    ):
        pre = (nt(g, d_ref[...]) * dg_ref[...].astype(F32)).astype(BF)
        q_ref[...] = pre
        s_ref[...] = rowsum(pre)
        acc_ref[...] += nt(pre, u_ref[...])

    @pl.when(j == pl.num_programs(0) - 1)
    def _():
        gn = acc_ref[...]
        xhat, rstd = norm_parts(mid_ref[...])
        gm = norm_back(xhat, rstd, gn, gain_ref[...]) + g.astype(F32)
        gm_ref[...] = gm
        gb = gm.astype(BF)
        gb_ref[...] = gb
        weight = jnp.concatenate([pwo_ref[...], pwp_ref[...]], axis=0)
        ga_ref[...] = nt(gb, weight).astype(BF)
        sums_ref[...] = jnp.concatenate(
            [rowsum(gn * xhat), rowsum(gn), rowsum(gb), rowsum(g)]
            + [jnp.zeros((4, gn.shape[1]), F32)], axis=0
        )


def post_bwd(g, kept, w):
    n, d = g.shape
    half = w["pw_o"].shape[0]
    fh = w["up_o"].shape[1]
    fb = fh // 2
    cols = lambda rows: pl.BlockSpec((rows, fb), lambda j: (0, j))
    rows_ = pl.BlockSpec((fb, d), lambda j: (j, 0))
    return pl.pallas_call(
        post_bwd_kernel,
        grid=(2,),
        in_specs=[
            whole((n, d)), whole((n, d)), whole((1, d)), cols(n), cols(n), cols(d), cols(d),
            rows_, rows_, whole((half, d)), whole((half, d)),
        ],
        out_specs=[
            cols(n), cols(n), whole((n, d)), whole((n, d)), whole((n, d)), whole((8, d)),
            cols(1), cols(1),
        ],
        out_shape=[
            sds((n, fh), BF), sds((n, fh), BF), sds((n, d), F32), sds((n, d), BF),
            sds((n, d), BF), sds((8, d), F32), sds((1, fh), F32), sds((1, fh), F32),
        ],
        scratch_shapes=[pltpu.VMEM((n, d), F32)],
        compiler_params=params(),
        name="post_bwd",
    )(
        g, kept["mid"], w["g2"], kept["dg_o"], kept["dg_p"], w["up_o"], w["up_p"], w["dn_o"],
        w["dn_p"], w["pw_o"], w["pw_p"],
    )


def attn_bwd_kernel(q_ref, k_ref, v_ref, ga_ref, l_ref, d_ref, s_ref, *, nimg, plen, vlen):
    sums = [jnp.zeros((1, 128), F32) for _ in range(3)]
    for im in range(nimg):
        r0 = im * plen
        k = k_ref[0, r0 : r0 + plen]
        v = v_ref[0, r0 : r0 + plen]
        kt = k.T
        dk = jnp.zeros((plen, 128), F32)
        dv = jnp.zeros((plen, 128), F32)
        for q0, qw in qblocks(plen):
            q = q_ref[0, r0 + q0 : r0 + q0 + qw]
            ga = ga_ref[r0 + q0 : r0 + q0 + qw]
            head = lax.broadcasted_iota(jnp.int32, q.shape, 1) // HD
            outs = []
            for h in range(2):
                qm = jnp.where(head == h, q, jnp.zeros_like(q))
                gam = jnp.where(head == h, ga, jnp.zeros_like(ga))
                lse = l_ref[0, h : h + 1, r0 + q0 : r0 + q0 + qw]
                st = mask_keys(nt(k, qm), vlen)
                p = jnp.exp(st * SCALE - lse)
                gp = nt(v, gam)
                dv += nn(p.astype(BF), gam)
                pg = p * gp
                ds = (pg - p * jnp.sum(pg, axis=0, keepdims=True)).astype(BF)
                dk += nn(ds, qm)
                outs.append(nn(kt[h * HD : (h + 1) * HD], ds))
            dq = (jnp.concatenate(outs, axis=0).T * SCALE).astype(BF)
            d_ref[0, r0 + q0 : r0 + q0 + qw] = dq
            sums[0] += rowsum(dq)
        dkb = (dk * SCALE).astype(BF)
        dvb = dv.astype(BF)
        d_ref[1, r0 : r0 + plen] = dkb
        d_ref[2, r0 : r0 + plen] = dvb
        sums[2] += rowsum(dvb)
    s_ref[...] = jnp.concatenate(sums + [jnp.zeros((5, 128), F32)], axis=0)


def attn_bwd(qkv, ga, lse, chunk):
    nimg, plen, vlen = chunk
    _, n, d = qkv.shape
    pairs = d // 128
    return pl.pallas_call(
        functools.partial(attn_bwd_kernel, nimg=nimg, plen=plen, vlen=vlen),
        grid=(pairs,),
        in_specs=[pl.BlockSpec((1, n, 128), lambda p, s=s: (s, 0, p)) for s in range(3)]
        + [pl.BlockSpec((n, 128), lambda p: (0, p)), pl.BlockSpec((1, 2, n), lambda p: (p, 0, 0))],
        out_specs=[
            pl.BlockSpec((3, n, 128), lambda p: (0, 0, p)),
            pl.BlockSpec((8, 128), lambda p: (0, p)),
        ],
        out_shape=[sds((3, n, d), BF), sds((8, d), F32)],
        compiler_params=params(),
        name="attn_bwd",
    )(qkv, qkv, qkv, ga, lse)


def pre_bwd_kernel(d_ref, wo_ref, wp_ref, x_ref, gain_ref, gm_ref, out_ref, sums_ref, acc_ref):
    j = pl.program_id(0)
    weight = jnp.concatenate([wo_ref[0], wp_ref[0]], axis=1)
    part = nt(d_ref[0], weight)

    @pl.when(j == 0)
    def _():
        acc_ref[...] = part

    @pl.when(j > 0)
    def _():
        acc_ref[...] += part

    @pl.when(j == pl.num_programs(0) - 1)
    def _():
        gn = acc_ref[...]
        xhat, rstd = norm_parts(x_ref[...].astype(F32))
        out_ref[...] = (norm_back(xhat, rstd, gn, gain_ref[...]) + gm_ref[...]).astype(BF)
        sums_ref[...] = jnp.concatenate(
            [rowsum(gn * xhat), rowsum(gn), jnp.zeros((6, gn.shape[1]), F32)], axis=0
        )


def pre_bwd(dqkv, x, gm, w):
    _, n, d = dqkv.shape
    half = w["wqkv_o"].shape[-1]
    return pl.pallas_call(
        pre_bwd_kernel,
        grid=(3,),
        in_specs=[
            pl.BlockSpec((1, n, d), lambda s: (s, 0, 0)),
            pl.BlockSpec((1, d, half), lambda s: (s, 0, 0)),
            pl.BlockSpec((1, d, half), lambda s: (s, 0, 0)),
            whole((n, d)), whole((1, d)), whole((n, d)),
        ],
        out_specs=[whole((n, d)), whole((8, d))],
        out_shape=[sds((n, d), BF), sds((8, d), F32)],
        scratch_shapes=[pltpu.VMEM((n, d), F32)],
        compiler_params=params(),
        name="pre_bwd",
    )(dqkv, w["wqkv_o"], w["wqkv_p"], x, w["g1"], gm)


def backward(g, kept, w, chunk):
    pre_o, pre_p, gm, gb, ga, sums2, so, sp = post_bwd(g, kept, w)
    dqkv, sums_qkv = attn_bwd(kept["qkv"], ga, kept["lse"], chunk)
    gx, sums1 = pre_bwd(dqkv, kept["x"], gm, w)
    return (g, pre_o, pre_p, gb, dqkv, sums2, so, sp, sums_qkv, sums1, gx)


def wgrad_qkv_kernel(*refs, count):
    a_refs, g_refs, (o_ref, p_ref) = refs[:count], refs[count : 2 * count], refs[2 * count :]
    total = sum(tn(a[...], g[0]) for a, g in zip(a_refs, g_refs))
    half = o_ref.shape[-1]
    o_ref[0] = total[:, :half].astype(BF)
    p_ref[0] = total[:, half:].astype(BF)


def wgrad_qkv(a_list, g_list):
    d = a_list[0].shape[1]
    half = d // 2
    return pl.pallas_call(
        functools.partial(wgrad_qkv_kernel, count=len(a_list)),
        grid=(3,),
        in_specs=[whole(a.shape) for a in a_list]
        + [pl.BlockSpec((1,) + g.shape[1:], lambda s: (s, 0, 0)) for g in g_list],
        out_specs=[pl.BlockSpec((1, d, half), lambda s: (s, 0, 0))] * 2,
        out_shape=[sds((3, d, half), BF)] * 2,
        compiler_params=params(),
        name="wgrad_qkv",
    )(*a_list, *g_list)


def wgrad_kernel(*refs, count):
    a_refs, g_refs, o_ref = refs[:count], refs[count : 2 * count], refs[2 * count]
    o_ref[...] = sum(tn(a[...], g[...]) for a, g in zip(a_refs, g_refs)).astype(BF)


def wgrad(a_list, g_list, split_a, block):
    m, k = a_list[0].shape[1], g_list[0].shape[1]
    whole_m = whole if split_a else None
    if split_a:
        grid = m // block
        a_specs = [pl.BlockSpec((a.shape[0], block), lambda j: (0, j)) for a in a_list]
        g_specs = [whole(g.shape) for g in g_list]
        out = pl.BlockSpec((block, k), lambda j: (j, 0))
    else:
        grid = k // block
        a_specs = [whole(a.shape) for a in a_list]
        g_specs = [pl.BlockSpec((g.shape[0], block), lambda j: (0, j)) for g in g_list]
        out = pl.BlockSpec((m, block), lambda j: (0, j))
    return pl.pallas_call(
        functools.partial(wgrad_kernel, count=len(a_list)),
        grid=(grid,),
        in_specs=a_specs + g_specs,
        out_specs=out,
        out_shape=sds((m, k), BF),
        compiler_params=params(),
        name="wgrad",
    )(*a_list, *g_list)


def blank_kernel(*refs):
    pass


def blank(like):
    shapes = [sds(a.shape, a.dtype) for a in like]
    return tuple(
        pl.pallas_call(
            blank_kernel,
            out_shape=shapes,
            out_specs=[pl.BlockSpec(memory_space=pl.ANY) for _ in shapes],
            name="blank",
        )()
    )


KEPT = ("x", "normed", "qkv", "att", "lse", "mid", "n2", "act_o", "act_p", "dg_o", "dg_p", "out")


def swap(array, axis, pairs):
    return lax.ppermute(array, axis, pairs)


def body(
    patches, out_grad, large_place, norm1_gain, norm1_bias, qkv_weight, qv_bias, proj_weight,
    proj_bias, norm2_gain, norm2_bias, up_weight, up_bias, down_weight, down_bias,
):
    d = patches.shape[1]
    rows = LEN_LARGE + SMALL_MB * LEN_SMALL
    half = qkv_weight.shape[-1]
    section = lax.axis_index("section")
    lane = lax.axis_index("tensor")
    both = [(0, 1), (1, 0)]
    other = lambda array: lax.ppermute(array, "tensor", both)

    wqkv, pw, up, dn = qkv_weight[0], proj_weight[0], up_weight[0], down_weight[0]
    small = jnp.concatenate([qv_bias[0].reshape(-1), up_bias[0]])
    small_p = other(small)
    zero_bias = jnp.zeros((half,), F32)

    def qkv_bias(own, partner):
        own, partner = own[: 2 * half].reshape(2, half), partner[: 2 * half].reshape(2, half)
        return jnp.stack(
            [
                jnp.concatenate([own[0], partner[0]]),
                jnp.concatenate([zero_bias, zero_bias]),
                jnp.concatenate([own[1], partner[1]]),
            ]
        )[:, None, :]

    w = {
        "g1": norm1_gain, "b1": norm1_bias, "g2": norm2_gain, "b2": norm2_bias,
        "pb": proj_bias, "db": down_bias,
        "wqkv_o": wqkv, "wqkv_p": other(wqkv), "pw_o": pw, "pw_p": other(pw),
        "up_o": up, "up_p": other(up), "dn_o": dn, "dn_p": other(dn),
        "bqkv": qkv_bias(small, small_p),
        "ub_o": small[None, 2 * half :], "ub_p": small_p[None, 2 * half :],
    }

    place = lax.dynamic_index_in_dim(large_place, lane, 0, keepdims=False)
    base = lane * rows
    starts = [place * LEN_SMALL]
    for j in range(SMALL_MB):
        slot = j + (j >= place).astype(jnp.int32)
        starts.append(slot * LEN_SMALL + (LEN_LARGE - LEN_SMALL) * (slot > place).astype(jnp.int32))
    lens = [LEN_LARGE] + [LEN_SMALL] * SMALL_MB

    def pieces(array):
        out, at = [], 0
        for nimg, plen, vlen in CHUNKS:
            parts = []
            for _ in range(nimg):
                part = lax.dynamic_slice(array, (base + starts[at], 0), (vlen, d))
                parts.append(jnp.pad(part, ((0, plen - vlen), (0, 0))))
                at += 1
            out.append(parts[0] if nimg == 1 else jnp.concatenate(parts, axis=0))
        return out

    def restore(parts):
        mine = jnp.zeros((rows, d), BF)
        at = 0
        for (nimg, plen, vlen), part in zip(CHUNKS, parts):
            for i in range(nimg):
                mine = lax.dynamic_update_slice(
                    mine, part[i * plen : i * plen + vlen], (starts[at], 0)
                )
                at += 1
        theirs = other(mine)
        first = lane == 0
        return jnp.concatenate([jnp.where(first, mine, theirs), jnp.where(first, theirs, mine)])

    xs = pieces(patches)
    gs = pieces(out_grad)

    fwd_like = [
        jax.eval_shape(functools.partial(forward, chunk=chunk), x, w)
        for x, chunk in zip(xs, CHUNKS)
    ]
    kept = []
    for x, chunk, like in zip(xs, CHUNKS, fwd_like):
        kept.append(
            lax.cond(
                section == 0,
                lambda x=x, chunk=chunk: tuple(forward(x, w, chunk)),
                lambda like=like: blank(like),
            )
        )
    received = [lax.ppermute(k[-1], "section", [(0, 1)]) for k in kept]
    kept = [
        lax.cond(
            section == 1,
            lambda r=r, chunk=chunk: tuple(forward(r, w, chunk)),
            lambda k=k: tuple(k),
        )
        for r, k, chunk in zip(received, kept, CHUNKS)
    ]
    outputs = restore([k[-1] for k in kept])
    kept = [dict(zip(KEPT, k)) for k in kept]

    order = list(reversed(range(len(CHUNKS))))
    back = [None] * len(CHUNKS)
    for c in order:
        like = jax.eval_shape(
            functools.partial(backward, chunk=CHUNKS[c]), gs[c], kept[c], w
        )
        back[c] = lax.cond(
            section == 1,
            lambda c=c: tuple(backward(gs[c], kept[c], w, CHUNKS[c])),
            lambda like=like: blank(like),
        )
    received = [lax.ppermute(b[-1], "section", [(1, 0)]) for b in back]
    for c in order:
        back[c] = lax.cond(
            section == 0,
            lambda c=c: tuple(backward(received[c], kept[c], w, CHUNKS[c])),
            lambda c=c: tuple(back[c]),
        )
    input_grads = restore([b[-1] for b in back])

    g_all = [b[0] for b in back]
    pre_o = [b[1] for b in back]
    pre_p = [b[2] for b in back]
    gb = [b[3] for b in back]
    dqkv = [b[4] for b in back]
    field = lambda name: [k[name] for k in kept]

    def reduce(own, partner):
        return lax.psum(own + other(partner), "dp").astype(F32)

    g_dn = reduce(
        wgrad(field("act_o"), g_all, True, 768), wgrad(field("act_p"), g_all, True, 768)
    )
    g_up = reduce(
        wgrad(field("n2"), pre_o, False, 768), wgrad(field("n2"), pre_p, False, 768)
    )
    pw_all = wgrad(field("att"), gb, True, d)
    g_pw = reduce(pw_all[:half], pw_all[half:])
    g_qkv = reduce(*wgrad_qkv(field("normed"), dqkv))

    total = lambda i: sum(b[i] for b in back)
    sums2, so, sp, sums_qkv, sums1 = (total(i) for i in range(5, 10))
    full = jnp.concatenate([sums1[:2].reshape(-1), sums2[:4].reshape(-1)])
    qv = jnp.stack([sums_qkv[0], sums_qkv[2]])
    mine = jnp.concatenate([full, qv[:, :half].reshape(-1), so[0]])
    theirs = jnp.concatenate([full, qv[:, half:].reshape(-1), sp[0]])
    vec = lax.psum((mine + other(theirs)).reshape(-1, 128), "dp").reshape(-1)
    one = lambda i: vec[None, i * d : (i + 1) * d]
    return (
        outputs[None],
        input_grads[None],
        one(0),
        one(1),
        g_qkv[None],
        vec[6 * d : 6 * d + 2 * half].reshape(1, 2, half),
        g_pw[None],
        one(4),
        one(2),
        one(3),
        g_up[None],
        vec[None, 6 * d + 2 * half :],
        g_dn[None],
        one(5),
    )


def solution(mesh):
    placed = (
        P("dp", None), P("dp", None), P("dp"), P("section", None), P("section", None),
        P("section", None, None, "tensor"), P("section", None, "tensor"),
        P("section", "tensor", None), P("section", None), P("section", None),
        P("section", None), P("section", None, "tensor"), P("section", "tensor"),
        P("section", "tensor", None), P("section", None),
    )
    return jax.shard_map(
        body,
        mesh=mesh,
        in_specs=placed,
        out_specs=(
            P("section", "dp", None), P("section", "dp", None), P("section", None),
            P("section", None), P("section", None, None, "tensor"), P("section", None, "tensor"),
            P("section", "tensor", None), P("section", None), P("section", None),
            P("section", None), P("section", None, "tensor"), P("section", "tensor"),
            P("section", "tensor", None), P("section", None),
        ),
        check_vma=False,
    )
```

```python
import functools

import jax
import jax.numpy as jnp
from jax import lax
from jax.experimental import pallas as pl
from jax.experimental.pallas import tpu as pltpu
from jax.sharding import PartitionSpec as P

HD = 64
LEN_SMALL = 197
LEN_LARGE = 577
SMALL_MB = 3
EPSILON = 1e-06
MASKED = -1e30
SCALE = HD ** (-0.5)
BF = jnp.bfloat16
F32 = jnp.float32
VMEM_LIMIT = 56 * 1024 * 1024
CHUNKS = ((1, 592, LEN_LARGE), (SMALL_MB, 208, LEN_SMALL))


def params(**more):
    return pltpu.CompilerParams(vmem_limit_bytes=VMEM_LIMIT, **more)


def nn(a, b):
    return jnp.dot(a, b, preferred_element_type=F32)


def nt(a, b):
    return lax.dot_general(a, b, (((1,), (1,)), ((), ())), preferred_element_type=F32)


def tn(a, b):
    return lax.dot_general(a, b, (((0,), (0,)), ((), ())), preferred_element_type=F32)


def whole(shape):
    zeros = (0,) * len(shape)
    return pl.BlockSpec(shape, lambda *_: zeros)


def sds(shape, dtype):
    return jax.ShapeDtypeStruct(shape, dtype)


def norm_parts(values):
    mean = jnp.mean(values, axis=-1, keepdims=True)
    centred = values - mean
    rstd = lax.rsqrt(jnp.mean(centred * centred, axis=-1, keepdims=True) + EPSILON)
    return centred * rstd, rstd


def norm_back(xhat, rstd, grad, gain):
    scaled = grad * gain
    m1 = jnp.mean(scaled, axis=-1, keepdims=True)
    m2 = jnp.mean(scaled * xhat, axis=-1, keepdims=True)
    return rstd * (scaled - m1 - xhat * m2)


def rowsum(values):
    return jnp.sum(values.astype(F32), axis=0, keepdims=True)


def pre_fwd_kernel(x_ref, g_ref, b_ref, wo_ref, wp_ref, bias_ref, normed_ref, qkv_ref):
    @pl.when(pl.program_id(0) == 0)
    def _():
        xhat, _ = norm_parts(x_ref[...].astype(F32))
        normed_ref[...] = (xhat * g_ref[...] + b_ref[...]).astype(BF)

    weight = jnp.concatenate([wo_ref[0], wp_ref[0]], axis=1)
    qkv_ref[0] = (nn(normed_ref[...], weight) + bias_ref[0]).astype(BF)


def pre_fwd(x, w):
    n, d = x.shape
    half = w["wqkv_o"].shape[-1]
    return pl.pallas_call(
        pre_fwd_kernel,
        grid=(3,),
        in_specs=[
            whole((n, d)),
            whole((1, d)),
            whole((1, d)),
            pl.BlockSpec((1, d, half), lambda s: (s, 0, 0)),
            pl.BlockSpec((1, d, half), lambda s: (s, 0, 0)),
            pl.BlockSpec((1, 1, 2 * half), lambda s: (s, 0, 0)),
        ],
        out_specs=[whole((n, d)), pl.BlockSpec((1, n, 2 * half), lambda s: (s, 0, 0))],
        out_shape=[sds((n, d), BF), sds((3, n, 2 * half), BF)],
        compiler_params=params(),
        name="pre_fwd",
    )(x, w["g1"], w["b1"], w["wqkv_o"], w["wqkv_p"], w["bqkv"])


def mask_keys(scores, vlen):
    rows = scores.shape[0]
    keep = vlen // 8 * 8
    tail = scores[keep:]
    idx = lax.broadcasted_iota(jnp.int32, tail.shape, 0) + keep
    return jnp.concatenate([scores[:keep], jnp.where(idx < vlen, tail, MASKED)], axis=0)


def qblocks(plen):
    return [(q, min(256, plen - q)) for q in range(0, plen, 256)]


def attn_fwd_kernel(q_ref, k_ref, v_ref, o_ref, l_ref, *, nimg, plen, vlen):
    for im in range(nimg):
        r0 = im * plen
        k = k_ref[0, r0 : r0 + plen]
        vt = v_ref[0, r0 : r0 + plen].T
        for q0, qw in qblocks(plen):
            q = q_ref[0, r0 + q0 : r0 + q0 + qw]
            head = lax.broadcasted_iota(jnp.int32, q.shape, 1) // HD
            outs = []
            for h in range(2):
                qm = jnp.where(head == h, q, jnp.zeros_like(q))
                st = mask_keys(nt(k, qm), vlen)
                top = jnp.max(st, axis=0, keepdims=True)
                e = jnp.exp((st - top) * SCALE)
                total = jnp.sum(e, axis=0, keepdims=True)
                p = (e * (1.0 / total)).astype(BF)
                outs.append(nn(vt[h * HD : (h + 1) * HD], p))
                l_ref[0, h : h + 1, r0 + q0 : r0 + q0 + qw] = top * SCALE + jnp.log(total)
            o_ref[r0 + q0 : r0 + q0 + qw] = jnp.concatenate(outs, axis=0).T.astype(BF)


def attn_fwd(qkv, chunk):
    nimg, plen, vlen = chunk
    _, n, d = qkv.shape
    pairs = d // 128
    return pl.pallas_call(
        functools.partial(attn_fwd_kernel, nimg=nimg, plen=plen, vlen=vlen),
        grid=(pairs,),
        in_specs=[
            pl.BlockSpec((1, n, 128), lambda p, s=s: (s, 0, p)) for s in range(3)
        ],
        out_specs=[
            pl.BlockSpec((n, 128), lambda p: (0, p)),
            pl.BlockSpec((1, 2, n), lambda p: (p, 0, 0)),
        ],
        out_shape=[sds((n, d), BF), sds((pairs, 2, n), F32)],
        compiler_params=params(),
        name="attn_fwd",
    )(qkv, qkv, qkv)


def gelu_parts(x):
    cdf = 0.5 + 0.5 * lax.erf(x * (2.0**-0.5))
    pdf = jnp.exp(-0.5 * x * x) * 0.3989422804014327
    return x * cdf, cdf + x * pdf


def post_fwd_kernel(
    x_ref, att_ref, pwo_ref, pwp_ref, pb_ref, g_ref, b_ref, uo_ref, up_ref, ubo_ref, ubp_ref,
    do_ref, dp_ref, db_ref,
    mid_ref, n2_ref, ao_ref, ap_ref, go_ref, gp_ref, out_ref, acc_ref,
):
    j = pl.program_id(0)

    @pl.when(j == 0)
    def _():
        weight = jnp.concatenate([pwo_ref[...], pwp_ref[...]], axis=0)
        mid = x_ref[...].astype(F32) + (nn(att_ref[...], weight) + pb_ref[...])
        mid_ref[...] = mid
        xhat, _ = norm_parts(mid)
        n2_ref[...] = (xhat * g_ref[...] + b_ref[...]).astype(BF)
        acc_ref[...] = mid + db_ref[...]

    n2 = n2_ref[...]
    for u_ref, ub_ref, d_ref, a_ref, dg_ref in (
        (uo_ref, ubo_ref, do_ref, ao_ref, go_ref),
        (up_ref, ubp_ref, dp_ref, ap_ref, gp_ref),
    ):
        act, slope = gelu_parts(nn(n2, u_ref[...]) + ub_ref[...])
        act = act.astype(BF)
        a_ref[...] = act
        dg_ref[...] = slope.astype(BF)
        acc_ref[...] += nn(act, d_ref[...])

    @pl.when(j == pl.num_programs(0) - 1)
    def _():
        out_ref[...] = acc_ref[...].astype(BF)


def post_fwd(x, att, w):
    n, d = x.shape
    half = w["pw_o"].shape[0]
    fh = w["up_o"].shape[1]
    fb = fh // 2
    cols = lambda rows: pl.BlockSpec((rows, fb), lambda j: (0, j))
    rows_ = pl.BlockSpec((fb, d), lambda j: (j, 0))
    return pl.pallas_call(
        post_fwd_kernel,
        grid=(2,),
        in_specs=[
            whole((n, d)), whole((n, d)), whole((half, d)), whole((half, d)), whole((1, d)),
            whole((1, d)), whole((1, d)), cols(d), cols(d), cols(1), cols(1), rows_, rows_,
            whole((1, d)),
        ],
        out_specs=[
            whole((n, d)), whole((n, d)), cols(n), cols(n), cols(n), cols(n), whole((n, d)),
        ],
        out_shape=[
            sds((n, d), F32), sds((n, d), BF), sds((n, fh), BF), sds((n, fh), BF),
            sds((n, fh), BF), sds((n, fh), BF), sds((n, d), BF),
        ],
        scratch_shapes=[pltpu.VMEM((n, d), F32)],
        compiler_params=params(),
        name="post_fwd",
    )(
        x, att, w["pw_o"], w["pw_p"], w["pb"], w["g2"], w["b2"], w["up_o"], w["up_p"],
        w["ub_o"], w["ub_p"], w["dn_o"], w["dn_p"], w["db"],
    )


def forward(x, w, chunk):
    normed, qkv = pre_fwd(x, w)
    att, lse = attn_fwd(qkv, chunk)
    mid, n2, act_o, act_p, dg_o, dg_p, out = post_fwd(x, att, w)
    return (x, normed, qkv, att, lse, mid, n2, act_o, act_p, dg_o, dg_p, out)


def post_bwd_kernel(
    g_ref, mid_ref, gain_ref, go_ref, gp_ref, uo_ref, up_ref, do_ref, dp_ref, pwo_ref, pwp_ref,
    qo_ref, qp_ref, gm_ref, gb_ref, ga_ref, sums_ref, so_ref, sp_ref, acc_ref,
):
    j = pl.program_id(0)
    g = g_ref[...]

    @pl.when(j == 0)
    def _():
        acc_ref[...] = jnp.zeros_like(acc_ref)

    for dg_ref, u_ref, d_ref, q_ref, s_ref in (
        (go_ref, uo_ref, do_ref, qo_ref, so_ref),
        (gp_ref, up_ref, dp_ref, qp_ref, sp_ref),
    ):
        pre = (nt(g, d_ref[...]) * dg_ref[...].astype(F32)).astype(BF)
        q_ref[...] = pre
        s_ref[...] = rowsum(pre)
        acc_ref[...] += nt(pre, u_ref[...])

    @pl.when(j == pl.num_programs(0) - 1)
    def _():
        gn = acc_ref[...]
        xhat, rstd = norm_parts(mid_ref[...])
        gm = norm_back(xhat, rstd, gn, gain_ref[...]) + g.astype(F32)
        gm_ref[...] = gm
        gb = gm.astype(BF)
        gb_ref[...] = gb
        weight = jnp.concatenate([pwo_ref[...], pwp_ref[...]], axis=0)
        ga_ref[...] = nt(gb, weight).astype(BF)
        sums_ref[...] = jnp.concatenate(
            [rowsum(gn * xhat), rowsum(gn), rowsum(gb), rowsum(g)]
            + [jnp.zeros((4, gn.shape[1]), F32)], axis=0
        )


def post_bwd(g, kept, w):
    n, d = g.shape
    half = w["pw_o"].shape[0]
    fh = w["up_o"].shape[1]
    fb = fh // 2
    cols = lambda rows: pl.BlockSpec((rows, fb), lambda j: (0, j))
    rows_ = pl.BlockSpec((fb, d), lambda j: (j, 0))
    return pl.pallas_call(
        post_bwd_kernel,
        grid=(2,),
        in_specs=[
            whole((n, d)), whole((n, d)), whole((1, d)), cols(n), cols(n), cols(d), cols(d),
            rows_, rows_, whole((half, d)), whole((half, d)),
        ],
        out_specs=[
            cols(n), cols(n), whole((n, d)), whole((n, d)), whole((n, d)), whole((8, d)),
            cols(1), cols(1),
        ],
        out_shape=[
            sds((n, fh), BF), sds((n, fh), BF), sds((n, d), F32), sds((n, d), BF),
            sds((n, d), BF), sds((8, d), F32), sds((1, fh), F32), sds((1, fh), F32),
        ],
        scratch_shapes=[pltpu.VMEM((n, d), F32)],
        compiler_params=params(),
        name="post_bwd",
    )(
        g, kept["mid"], w["g2"], kept["dg_o"], kept["dg_p"], w["up_o"], w["up_p"], w["dn_o"],
        w["dn_p"], w["pw_o"], w["pw_p"],
    )


def attn_bwd_kernel(q_ref, k_ref, v_ref, ga_ref, l_ref, d_ref, s_ref, *, nimg, plen, vlen):
    sums = [jnp.zeros((1, 128), F32) for _ in range(3)]
    for im in range(nimg):
        r0 = im * plen
        k = k_ref[0, r0 : r0 + plen]
        v = v_ref[0, r0 : r0 + plen]
        kt = k.T
        dk = jnp.zeros((plen, 128), F32)
        dv = jnp.zeros((plen, 128), F32)
        for q0, qw in qblocks(plen):
            q = q_ref[0, r0 + q0 : r0 + q0 + qw]
            ga = ga_ref[r0 + q0 : r0 + q0 + qw]
            head = lax.broadcasted_iota(jnp.int32, q.shape, 1) // HD
            outs = []
            for h in range(2):
                qm = jnp.where(head == h, q, jnp.zeros_like(q))
                gam = jnp.where(head == h, ga, jnp.zeros_like(ga))
                lse = l_ref[0, h : h + 1, r0 + q0 : r0 + q0 + qw]
                st = mask_keys(nt(k, qm), vlen)
                p = jnp.exp(st * SCALE - lse)
                gp = nt(v, gam)
                dv += nn(p.astype(BF), gam)
                pg = p * gp
                ds = (pg - p * jnp.sum(pg, axis=0, keepdims=True)).astype(BF)
                dk += nn(ds, qm)
                outs.append(nn(kt[h * HD : (h + 1) * HD], ds))
            dq = (jnp.concatenate(outs, axis=0).T * SCALE).astype(BF)
            d_ref[0, r0 + q0 : r0 + q0 + qw] = dq
            sums[0] += rowsum(dq)
        dkb = (dk * SCALE).astype(BF)
        dvb = dv.astype(BF)
        d_ref[1, r0 : r0 + plen] = dkb
        d_ref[2, r0 : r0 + plen] = dvb
        sums[2] += rowsum(dvb)
    s_ref[...] = jnp.concatenate(sums + [jnp.zeros((5, 128), F32)], axis=0)


def attn_bwd(qkv, ga, lse, chunk):
    nimg, plen, vlen = chunk
    _, n, d = qkv.shape
    pairs = d // 128
    return pl.pallas_call(
        functools.partial(attn_bwd_kernel, nimg=nimg, plen=plen, vlen=vlen),
        grid=(pairs,),
        in_specs=[pl.BlockSpec((1, n, 128), lambda p, s=s: (s, 0, p)) for s in range(3)]
        + [pl.BlockSpec((n, 128), lambda p: (0, p)), pl.BlockSpec((1, 2, n), lambda p: (p, 0, 0))],
        out_specs=[
            pl.BlockSpec((3, n, 128), lambda p: (0, 0, p)),
            pl.BlockSpec((8, 128), lambda p: (0, p)),
        ],
        out_shape=[sds((3, n, d), BF), sds((8, d), F32)],
        compiler_params=params(),
        name="attn_bwd",
    )(qkv, qkv, qkv, ga, lse)


def pre_bwd_kernel(d_ref, wo_ref, wp_ref, x_ref, gain_ref, gm_ref, out_ref, sums_ref, acc_ref):
    j = pl.program_id(0)
    weight = jnp.concatenate([wo_ref[0], wp_ref[0]], axis=1)
    part = nt(d_ref[0], weight)

    @pl.when(j == 0)
    def _():
        acc_ref[...] = part

    @pl.when(j > 0)
    def _():
        acc_ref[...] += part

    @pl.when(j == pl.num_programs(0) - 1)
    def _():
        gn = acc_ref[...]
        xhat, rstd = norm_parts(x_ref[...].astype(F32))
        out_ref[...] = (norm_back(xhat, rstd, gn, gain_ref[...]) + gm_ref[...]).astype(BF)
        sums_ref[...] = jnp.concatenate(
            [rowsum(gn * xhat), rowsum(gn), jnp.zeros((6, gn.shape[1]), F32)], axis=0
        )


def pre_bwd(dqkv, x, gm, w):
    _, n, d = dqkv.shape
    half = w["wqkv_o"].shape[-1]
    return pl.pallas_call(
        pre_bwd_kernel,
        grid=(3,),
        in_specs=[
            pl.BlockSpec((1, n, d), lambda s: (s, 0, 0)),
            pl.BlockSpec((1, d, half), lambda s: (s, 0, 0)),
            pl.BlockSpec((1, d, half), lambda s: (s, 0, 0)),
            whole((n, d)), whole((1, d)), whole((n, d)),
        ],
        out_specs=[whole((n, d)), whole((8, d))],
        out_shape=[sds((n, d), BF), sds((8, d), F32)],
        scratch_shapes=[pltpu.VMEM((n, d), F32)],
        compiler_params=params(),
        name="pre_bwd",
    )(dqkv, w["wqkv_o"], w["wqkv_p"], x, w["g1"], gm)


def backward(g, kept, w, chunk):
    pre_o, pre_p, gm, gb, ga, sums2, so, sp = post_bwd(g, kept, w)
    dqkv, sums_qkv = attn_bwd(kept["qkv"], ga, kept["lse"], chunk)
    gx, sums1 = pre_bwd(dqkv, kept["x"], gm, w)
    return (g, pre_o, pre_p, gb, dqkv, sums2, so, sp, sums_qkv, sums1, gx)


def wgrad_mlp_kernel(*refs, more):
    ao, ap, n2, po, pp, g = refs[:6]
    init = refs[6 : 6 + more]
    outs = refs[6 + more :]
    g, n2 = g[...], n2[...]
    results = (
        tn(ao[...], g), tn(ap[...], g), tn(n2, po[...]), tn(n2, pp[...]),
    )
    for i, (out, value) in enumerate(zip(outs, results)):
        if more:
            value += init[i][...].astype(F32)
        out[...] = value.astype(BF)


def wgrad_mlp(kept, back, init=()):
    n, d = back["g"].shape
    fh = kept["act_o"].shape[1]
    fb = fh // 4
    cols = lambda rows: pl.BlockSpec((rows, fb), lambda j: (0, j))
    rows_ = pl.BlockSpec((fb, d), lambda j: (j, 0))
    outs = [rows_, rows_, cols(d), cols(d)]
    return pl.pallas_call(
        functools.partial(wgrad_mlp_kernel, more=len(init)),
        grid=(4,),
        in_specs=[cols(n), cols(n), whole((n, d)), cols(n), cols(n), whole((n, d))]
        + outs[: len(init)],
        out_specs=outs,
        out_shape=[sds((fh, d), BF)] * 2 + [sds((d, fh), BF)] * 2,
        compiler_params=params(),
        name="wgrad_mlp",
    )(kept["act_o"], kept["act_p"], kept["n2"], back["pre_o"], back["pre_p"], back["g"], *init)


def wgrad_attn_kernel(*refs, more):
    normed, dqkv, att, gb = refs[:4]
    init = refs[4 : 4 + more]
    o_ref, p_ref, w_ref = refs[4 + more :]
    total = tn(normed[...], dqkv[0])
    branch = tn(att[...], gb[...])
    half = o_ref.shape[-1]
    own, partner = total[:, :half], total[:, half:]
    if more:
        own += init[0][0].astype(F32)
        partner += init[1][0].astype(F32)
        branch += init[2][...].astype(F32)
    o_ref[0] = own.astype(BF)
    p_ref[0] = partner.astype(BF)
    w_ref[...] = branch.astype(BF)


def wgrad_attn(kept, back, init=()):
    n, d = kept["normed"].shape
    half, block = d // 2, d // 3
    part = pl.BlockSpec((1, d, half), lambda s: (s, 0, 0))
    outs = [part, part, pl.BlockSpec((block, d), lambda s: (s, 0))]
    return pl.pallas_call(
        functools.partial(wgrad_attn_kernel, more=len(init)),
        grid=(3,),
        in_specs=[
            whole((n, d)), pl.BlockSpec((1, n, d), lambda s: (s, 0, 0)),
            pl.BlockSpec((n, block), lambda s: (0, s)), whole((n, d)),
        ]
        + outs[: len(init)],
        out_specs=outs,
        out_shape=[sds((3, d, half), BF)] * 2 + [sds((d, d), BF)],
        compiler_params=params(),
        name="wgrad_attn",
    )(kept["normed"], back["dqkv"], kept["att"], back["gb"], *init)


RING = 8
WAYS = (1, 1, -1, -1, -1)


def ring_kernel(*refs, n):
    owns, others, vec_ref = refs[:n], refs[n : 2 * n], refs[2 * n]
    outs, vsum_ref = refs[2 * n + 1 : 3 * n + 1], refs[3 * n + 1]
    slots, vslot = refs[3 * n + 2 : 4 * n + 2], refs[4 * n + 2]
    send, recv, vsend, vrecv = refs[4 * n + 3 :]
    me = lax.axis_index("dp")
    z, x = me // 2, me % 2
    pos = z + x * (RING - 1 - 2 * z)

    def member(p):
        p = p % RING
        return {"dp": 2 * p + (p // (RING // 2)) * (2 * RING - 1 - 4 * p)}

    barrier = pltpu.get_barrier_semaphore()
    for k in range(1, RING):
        pl.semaphore_signal(
            barrier, inc=1, device_id=member(pos + k), device_id_type=pl.DeviceIdType.MESH
        )
    pl.semaphore_wait(barrier, RING - 1)

    def part(ref, chunk):
        rows = ref.shape[0] // RING
        return ref.at[pl.ds(pl.multiple_of((chunk % RING) * rows, rows), rows)]

    def mine(a, chunk):
        return part(owns[a], chunk)[...].astype(F32) + part(others[a], chunk)[...].astype(F32)

    def remote(src, dst, a, step):
        return pltpu.make_async_remote_copy(
            src_ref=src,
            dst_ref=dst,
            send_sem=send.at[a, step],
            recv_sem=recv.at[a, step],
            device_id=member(pos + WAYS[a] + RING),
            device_id_type=pl.DeviceIdType.MESH,
        )

    def vcopy(k):
        return pltpu.make_async_remote_copy(
            src_ref=vec_ref,
            dst_ref=vslot.at[k - 1],
            send_sem=vsend.at[k - 1],
            recv_sem=vrecv.at[k - 1],
            device_id=member(pos + k),
            device_id_type=pl.DeviceIdType.MESH,
        )

    for a in range(n):
        slots[a][0] = mine(a, pos).astype(BF)
        remote(slots[a].at[0], slots[a].at[1], a, 0).start()
    for k in range(1, RING):
        vcopy(k).start()

    def scatter(s, carry):
        for a in range(n):
            here = slots[a].at[s]
            remote(here, here, a, s - 1).wait_recv()
            here[...] = (here[...].astype(F32) + mine(a, pos + 2 * RING - WAYS[a] * s)).astype(BF)
            remote(here, slots[a].at[s + 1], a, s).start()
        return carry

    lax.fori_loop(1, RING - 1, scatter, 0)
    for a in range(n):
        last = slots[a].at[RING - 1]
        remote(last, last, a, RING - 2).wait_recv()
        own = part(outs[a], pos + RING + WAYS[a])
        own[...] = (last[...].astype(F32) + mine(a, pos + RING + WAYS[a])).astype(BF)
        remote(own, own, a, RING - 1).start()

    def gather(t, carry):
        for a in range(n):
            here = part(outs[a], pos + 2 * RING + WAYS[a] * (1 - t))
            remote(here, here, a, RING - 2 + t).wait_recv()
            remote(here, here, a, RING - 1 + t).start()
        return carry

    lax.fori_loop(1, RING - 1, gather, 0)
    total = vec_ref[...]
    for k in range(1, RING):
        vcopy(k).wait()
        total += vslot[k - 1]
    vsum_ref[...] = total
    for a in range(n):
        here = part(outs[a], pos + 2 * RING + WAYS[a] * (2 - RING))
        remote(here, here, a, 2 * RING - 3).wait_recv()
    for a in range(n):
        for s in range(RING - 1):
            remote(slots[a].at[0], slots[a].at[0], a, s).wait_send()
            remote(part(outs[a], pos), part(outs[a], pos), a, RING - 1 + s).wait_send()


def ring(owns, others, vec):
    n = len(owns)
    vmem = pl.BlockSpec(memory_space=pltpu.VMEM)
    out = pl.pallas_call(
        functools.partial(ring_kernel, n=n),
        in_specs=[vmem] * (2 * n + 1),
        out_specs=[vmem] * (n + 1),
        out_shape=[sds(a.shape, BF) for a in owns] + [sds(vec.shape, F32)],
        scratch_shapes=[pltpu.VMEM((RING, a.shape[0] // RING, a.shape[1]), BF) for a in owns]
        + [
            pltpu.VMEM((RING - 1,) + vec.shape, F32),
            pltpu.SemaphoreType.DMA((n, 2 * RING - 2)),
            pltpu.SemaphoreType.DMA((n, 2 * RING - 2)),
            pltpu.SemaphoreType.DMA((RING - 1,)),
            pltpu.SemaphoreType.DMA((RING - 1,)),
        ],
        compiler_params=params(collective_id=1, has_side_effects=True),
        name="ring",
    )(*owns, *others, vec)
    return out[:n], out[n]


def dp_sum(owns, others, vec):
    if lax.axis_size("dp") == RING:
        return ring(owns, others, vec)
    return [lax.psum(a + b, "dp") for a, b in zip(owns, others)], lax.psum(vec, "dp")


def starts_of(place):
    slots = [j + (j >= place) for j in range(SMALL_MB)]
    return [place * LEN_SMALL] + [
        slot * LEN_SMALL + (LEN_LARGE - LEN_SMALL) * (slot > place) for slot in slots
    ]


def layout(place):
    at = 0
    starts = starts_of(place)
    for c, (nimg, plen, vlen) in enumerate(CHUNKS):
        for i in range(nimg):
            yield starts[at], c, i * plen, plen, vlen
            at += 1


def cut_kernel(meta_ref, x_ref, *refs):
    outs, flat = refs[:-1], refs[-1]
    rows = x_ref.shape[0]
    flat[:rows] = x_ref[...].astype(F32)
    flat[rows:] = jnp.zeros((flat.shape[0] - rows, flat.shape[1]), F32)
    for place in range(SMALL_MB + 1):

        @pl.when(meta_ref[1] == place)
        def _():
            for start, c, r0, plen, vlen in layout(place):
                value = flat[start : start + plen]
                row = lax.broadcasted_iota(jnp.int32, value.shape, 0)
                outs[c][r0 : r0 + plen] = jnp.where(row < vlen, value, 0.0).astype(BF)


def cut(array, meta):
    rows = LEN_LARGE + SMALL_MB * LEN_SMALL
    d = array.shape[1]
    block = d // 3
    return pl.pallas_call(
        cut_kernel,
        grid_spec=pltpu.PrefetchScalarGridSpec(
            num_scalar_prefetch=1,
            grid=(3,),
            in_specs=[pl.BlockSpec((rows, block), lambda j, m: (m[0], j))],
            out_specs=[pl.BlockSpec((k * p, block), lambda j, m: (0, j)) for k, p, _ in CHUNKS],
            scratch_shapes=[pltpu.VMEM((rows + 16, block), F32)],
        ),
        out_shape=[sds((k * p, d), BF) for k, p, _ in CHUNKS],
        compiler_params=params(),
        name="cut",
    )(meta, array)


def join_kernel(meta_ref, *refs):
    count = len(CHUNKS)
    mine, theirs, out_ref, flat = refs[:count], refs[count : 2 * count], refs[-2], refs[-1]
    rows = flat.shape[0]
    for lane in range(2):
        here = meta_ref[0] == lane
        for place in range(SMALL_MB + 1):

            @pl.when(meta_ref[2 + lane] == place)
            def _():
                for start, c, r0, plen, vlen in layout(place):
                    own = mine[c][r0 : r0 + plen].astype(F32)
                    value = jnp.where(here, own, theirs[c][r0 : r0 + plen].astype(F32))
                    flat[start : start + vlen] = value[:vlen]

        out_ref[lane * rows : (lane + 1) * rows] = flat[...].astype(BF)


def join(mine, theirs, meta):
    rows = LEN_LARGE + SMALL_MB * LEN_SMALL
    d = mine[0].shape[1]
    block = d // 3
    return pl.pallas_call(
        join_kernel,
        grid_spec=pltpu.PrefetchScalarGridSpec(
            num_scalar_prefetch=1,
            grid=(3,),
            in_specs=[pl.BlockSpec((k * p, block), lambda j, m: (0, j)) for k, p, _ in CHUNKS] * 2,
            out_specs=pl.BlockSpec((2 * rows, block), lambda j, m: (0, j)),
            scratch_shapes=[pltpu.VMEM((rows, block), F32)],
        ),
        out_shape=sds((2 * rows, d), BF),
        compiler_params=params(),
        name="join",
    )(meta, *mine, *theirs)


def blank_kernel(*refs):
    pass


def blank(like):
    shapes = [sds(a.shape, a.dtype) for a in like]
    return tuple(
        pl.pallas_call(
            blank_kernel,
            out_shape=shapes,
            out_specs=[pl.BlockSpec(memory_space=pl.ANY) for _ in shapes],
            name="blank",
        )()
    )


KEPT = ("x", "normed", "qkv", "att", "lse", "mid", "n2", "act_o", "act_p", "dg_o", "dg_p", "out")
BACK = ("g", "pre_o", "pre_p", "gb", "dqkv", "sums2", "so", "sp", "sums_qkv", "sums1", "gx")


def after(value, *earlier):
    return lax.optimization_barrier((value, earlier))[0]


def body(
    patches, out_grad, large_place, norm1_gain, norm1_bias, qkv_weight, qv_bias, proj_weight,
    proj_bias, norm2_gain, norm2_bias, up_weight, up_bias, down_weight, down_bias,
):
    d = patches.shape[1]
    half = qkv_weight.shape[-1]
    section = lax.axis_index("section")
    lane = lax.axis_index("tensor")
    both = [(0, 1), (1, 0)]
    other = lambda array: lax.ppermute(array, "tensor", both)

    wqkv, pw, up, dn = qkv_weight[0], proj_weight[0], up_weight[0], down_weight[0]
    small = jnp.concatenate([qv_bias[0].reshape(-1), up_bias[0]])
    small_p = other(small)
    zero_bias = jnp.zeros((half,), F32)

    def qkv_bias(own, partner):
        own, partner = own[: 2 * half].reshape(2, half), partner[: 2 * half].reshape(2, half)
        return jnp.stack(
            [
                jnp.concatenate([own[0], partner[0]]),
                jnp.concatenate([zero_bias, zero_bias]),
                jnp.concatenate([own[1], partner[1]]),
            ]
        )[:, None, :]

    w = {
        "g1": norm1_gain, "b1": norm1_bias, "g2": norm2_gain, "b2": norm2_bias,
        "pb": proj_bias, "db": down_bias,
        "wqkv_o": wqkv, "wqkv_p": other(wqkv), "pw_o": pw, "pw_p": other(pw),
        "up_o": up, "up_p": other(up), "dn_o": dn, "dn_p": other(dn),
        "bqkv": qkv_bias(small, small_p),
        "ub_o": small[None, 2 * half :], "ub_p": small_p[None, 2 * half :],
    }


    place = jnp.where(lane == 0, large_place[0], large_place[1])
    meta = jnp.stack([lane, place, large_place[0], large_place[1]]).astype(jnp.int32)
    large, smalls = 0, 1
    xs = cut(patches, meta)
    gs = cut(out_grad, meta)

    def fwd(c, on, x, otherwise=None):
        like = jax.eval_shape(functools.partial(forward, chunk=CHUNKS[c]), x, w)
        return lax.cond(
            section == on,
            lambda: tuple(forward(x, w, CHUNKS[c])),
            lambda: blank(like) if otherwise is None else tuple(otherwise),
        )

    def bwd(c, on, g, kept, otherwise=None):
        kept = dict(zip(KEPT, kept))
        like = jax.eval_shape(functools.partial(backward, chunk=CHUNKS[c]), g, kept, w)
        return lax.cond(
            section == on,
            lambda: tuple(backward(g, kept, w, CHUNKS[c])),
            lambda: blank(like) if otherwise is None else tuple(otherwise),
        )

    down = lambda array: lax.ppermute(array, "section", [(0, 1)])
    up_ = lambda array: lax.ppermute(array, "section", [(1, 0)])

    kept_s = fwd(smalls, 0, xs[smalls])
    sent_s = down(kept_s[-1])
    kept_l = fwd(large, 0, after(xs[large], kept_s[-1]))
    sent_l = down(kept_l[-1])
    kept_s = fwd(smalls, 1, after(sent_s, kept_l[-1]), kept_s)
    back_s = bwd(smalls, 1, gs[smalls], kept_s)
    sent_s = up_(back_s[-1])
    kept_l = fwd(large, 1, after(sent_l, back_s[-1]), kept_l)
    back_l = bwd(large, 1, gs[large], kept_l)
    sent_l = up_(back_l[-1])
    back_s = bwd(smalls, 0, after(sent_s, back_l[-1]), kept_s, back_s)
    named = lambda names, values: dict(zip(names, values))
    part_mlp = wgrad_mlp(named(KEPT, kept_s), named(BACK, back_s))
    part_attn = wgrad_attn(named(KEPT, kept_s), named(BACK, back_s))
    outs = [kept_l[-1], kept_s[-1]]
    outputs = join(outs, [other(a) for a in outs], meta)
    sent_l = after(sent_l, part_mlp, part_attn, outputs)
    back_l = bwd(large, 0, sent_l, kept_l, back_l)
    dn_o, dn_p, up_o, up_p = wgrad_mlp(named(KEPT, kept_l), named(BACK, back_l), part_mlp)
    qkv_o, qkv_p, pw_all = wgrad_attn(named(KEPT, kept_l), named(BACK, back_l), part_attn)
    grads = [back_l[-1], back_s[-1]]
    input_grads = join(grads, [other(a) for a in grads], meta)

    total = lambda i: back_s[i] + back_l[i]
    sums2, so, sp, sums_qkv, sums1 = (total(i) for i in range(5, 10))
    full = jnp.concatenate([sums1[:2].reshape(-1), sums2[:4].reshape(-1)])
    qv = jnp.stack([sums_qkv[0], sums_qkv[2]])
    mine = jnp.concatenate([full, qv[:, :half].reshape(-1), so[0]])
    theirs = jnp.concatenate([full, qv[:, half:].reshape(-1), sp[0]])
    vec = (mine + other(theirs)).reshape(-1, 128)

    def flat(qkv):
        return qkv[:2].reshape(2 * d, half), qkv[2]

    qk_o, v_o = flat(qkv_o)
    qk_p, v_p = flat(other(qkv_p))
    summed, vec = dp_sum(
        [dn_o, qk_o, up_o, v_o, pw_all[:half]],
        [other(dn_p), qk_p, other(up_p), v_p, other(pw_all[half:])],
        vec,
    )
    g_dn, g_qk, g_up, g_v, g_pw = (a.astype(F32) for a in summed)
    g_qkv = jnp.concatenate([g_qk.reshape(2, d, half), g_v[None]])
    vec = vec.reshape(-1)
    one = lambda i: vec[None, i * d : (i + 1) * d]
    return (
        outputs[None],
        input_grads[None],
        one(0),
        one(1),
        g_qkv[None],
        vec[6 * d : 6 * d + 2 * half].reshape(1, 2, half),
        g_pw[None],
        one(4),
        one(2),
        one(3),
        g_up[None],
        vec[None, 6 * d + 2 * half :],
        g_dn[None],
        one(5),
    )


def solution(mesh):
    placed = (
        P("dp", None), P("dp", None), P("dp"), P("section", None), P("section", None),
        P("section", None, None, "tensor"), P("section", None, "tensor"),
        P("section", "tensor", None), P("section", None), P("section", None),
        P("section", None), P("section", None, "tensor"), P("section", "tensor"),
        P("section", "tensor", None), P("section", None),
    )
    return jax.shard_map(
        body,
        mesh=mesh,
        in_specs=placed,
        out_specs=(
            P("section", "dp", None), P("section", "dp", None), P("section", None),
            P("section", None), P("section", None, None, "tensor"), P("section", None, "tensor"),
            P("section", "tensor", None), P("section", None), P("section", None),
            P("section", None), P("section", None, "tensor"), P("section", "tensor"),
            P("section", "tensor", None), P("section", None),
        ),
        check_vma=False,
    )
```

```python
import functools

import jax
import jax.numpy as jnp
from jax import lax
from jax.experimental import pallas as pl
from jax.experimental.pallas import tpu as pltpu
from jax.sharding import PartitionSpec as P

HD = 64
LEN_SMALL = 197
LEN_LARGE = 577
SMALL_MB = 3
EPSILON = 1e-06
MASKED = -1e30
SCALE = HD ** (-0.5)
SCALE2 = SCALE * 1.4426950408889634
BF = jnp.bfloat16
F32 = jnp.float32
VMEM_LIMIT = 56 * 1024 * 1024
CHUNKS = ((1, 592, LEN_LARGE), (SMALL_MB, 208, LEN_SMALL))


def params(**more):
    return pltpu.CompilerParams(vmem_limit_bytes=VMEM_LIMIT, **more)


def nn(a, b):
    return jnp.dot(a, b, preferred_element_type=F32)


def nt(a, b):
    return lax.dot_general(a, b, (((1,), (1,)), ((), ())), preferred_element_type=F32)


def tn(a, b):
    return lax.dot_general(a, b, (((0,), (0,)), ((), ())), preferred_element_type=F32)


def whole(shape):
    zeros = (0,) * len(shape)
    return pl.BlockSpec(shape, lambda *_: zeros)


def sds(shape, dtype):
    return jax.ShapeDtypeStruct(shape, dtype)


def norm_parts(values):
    mean = jnp.mean(values, axis=-1, keepdims=True)
    centred = values - mean
    rstd = lax.rsqrt(jnp.mean(centred * centred, axis=-1, keepdims=True) + EPSILON)
    return centred * rstd, rstd


def norm_back(xhat, rstd, grad, gain):
    scaled = grad * gain
    m1 = jnp.mean(scaled, axis=-1, keepdims=True)
    m2 = jnp.mean(scaled * xhat, axis=-1, keepdims=True)
    return rstd * (scaled - m1 - xhat * m2)


def rowsum(values):
    return jnp.sum(values.astype(F32), axis=0, keepdims=True)


def pre_fwd_kernel(x_ref, g_ref, b_ref, wo_ref, wp_ref, bo_ref, bp_ref, normed_ref, qkv_ref):
    s = pl.program_id(0)

    @pl.when(s == 0)
    def _():
        xhat, _ = norm_parts(x_ref[...].astype(F32))
        normed_ref[...] = (xhat * g_ref[...] + b_ref[...]).astype(BF)

    weight = jnp.concatenate([wo_ref[0], wp_ref[0]], axis=1)
    biases = jnp.concatenate([bo_ref[...], bp_ref[...]], axis=1)
    bias = jnp.where(s == 0, biases[:1], jnp.where(s == 1, 0.0, biases[1:]))
    qkv_ref[0] = (nn(normed_ref[...], weight) + bias).astype(BF)


def pre_fwd(x, w):
    n, d = x.shape
    half = w["wqkv_o"].shape[-1]
    return pl.pallas_call(
        pre_fwd_kernel,
        grid=(3,),
        in_specs=[
            whole((n, d)),
            whole((1, d)),
            whole((1, d)),
            pl.BlockSpec((1, d, half), lambda s: (s, 0, 0)),
            pl.BlockSpec((1, d, half), lambda s: (s, 0, 0)),
            whole((2, half)),
            whole((2, half)),
        ],
        out_specs=[whole((n, d)), pl.BlockSpec((1, n, 2 * half), lambda s: (s, 0, 0))],
        out_shape=[sds((n, d), BF), sds((3, n, 2 * half), BF)],
        compiler_params=params(),
        name="pre_fwd",
    )(x, w["g1"], w["b1"], w["wqkv_o"], w["wqkv_p"], w["bq_o"], w["bq_p"])


def mask_keys(scores, vlen):
    rows = scores.shape[0]
    keep = vlen // 8 * 8
    tail = scores[keep:]
    idx = lax.broadcasted_iota(jnp.int32, tail.shape, 0) + keep
    return jnp.concatenate([scores[:keep], jnp.where(idx < vlen, tail, MASKED)], axis=0)


def qblocks(plen):
    step = min(256, plen)
    return [(q, min(step, 2 * plen - q)) for q in range(0, 2 * plen, step)]


def lse_width(chunk):
    nimg, plen, _ = chunk
    return nimg * len(qblocks(plen)) * 256


def both_heads(rows):
    head = lax.broadcasted_iota(jnp.int32, rows.shape, 1) // HD
    none = jnp.zeros_like(rows)
    return jnp.concatenate([jnp.where(head == h, rows, none) for h in range(2)], axis=0)


def one_each(stacked, plen):
    head = lax.broadcasted_iota(jnp.int32, (plen, stacked.shape[1]), 1) // HD
    return jnp.where(head == 0, stacked[:plen], stacked[plen:])


def attn_fwd_kernel(q_ref, k_ref, v_ref, o_ref, l_ref, o_tmp, *, nimg, plen, vlen):
    at = 0
    for im in range(nimg):
        rows = slice(im * plen, (im + 1) * plen)
        k = k_ref[0, rows]
        vt = v_ref[0, rows].T
        queries = both_heads(q_ref[0, rows])
        for q0, qw in qblocks(plen):
            st = mask_keys(nt(k, queries[q0 : q0 + qw]), vlen)
            top = jnp.max(st, axis=0, keepdims=True)
            e = jnp.exp2((st - top) * SCALE2)
            total = jnp.sum(e, axis=0, keepdims=True)
            o_tmp[q0 : q0 + qw] = (nn(vt, e.astype(BF)) * (1.0 / total)).T
            l_ref[0, :, at : at + qw] = top * SCALE2 + jnp.log2(total)
            at += 256
        o_ref[rows] = one_each(o_tmp, plen).astype(BF)


def attn_fwd(qkv, chunk):
    nimg, plen, vlen = chunk
    _, n, d = qkv.shape
    pairs = d // 128
    width = lse_width(chunk)
    return pl.pallas_call(
        functools.partial(attn_fwd_kernel, nimg=nimg, plen=plen, vlen=vlen),
        grid=(pairs,),
        in_specs=[
            pl.BlockSpec((1, n, 128), lambda p, s=s: (s, 0, p)) for s in range(3)
        ],
        out_specs=[
            pl.BlockSpec((n, 128), lambda p: (0, p)),
            pl.BlockSpec((1, 1, width), lambda p: (p, 0, 0)),
        ],
        out_shape=[sds((n, d), BF), sds((pairs, 1, width), F32)],
        scratch_shapes=[pltpu.VMEM((2 * plen, 128), F32)],
        compiler_params=params(),
        name="attn_fwd",
    )(qkv, qkv, qkv)


def gelu_parts(x):
    cdf = 0.5 + 0.5 * lax.erf(x * (2.0**-0.5))
    pdf = jnp.exp(-0.5 * x * x) * 0.3989422804014327
    return x * cdf, cdf + x * pdf


def post_fwd_kernel(
    x_ref, att_ref, pwo_ref, pwp_ref, pb_ref, g_ref, b_ref, uo_ref, up_ref, ubo_ref, ubp_ref,
    do_ref, dp_ref, db_ref,
    mid_ref, n2_ref, ao_ref, ap_ref, go_ref, gp_ref, out_ref, acc_ref,
):
    j = pl.program_id(0)

    @pl.when(j == 0)
    def _():
        weight = jnp.concatenate([pwo_ref[...], pwp_ref[...]], axis=0)
        mid = x_ref[...].astype(F32) + (nn(att_ref[...], weight) + pb_ref[...])
        mid_ref[...] = mid
        xhat, _ = norm_parts(mid)
        n2_ref[...] = (xhat * g_ref[...] + b_ref[...]).astype(BF)
        acc_ref[...] = mid + db_ref[...]

    n2 = n2_ref[...]
    for u_ref, ub_ref, d_ref, a_ref, dg_ref in (
        (uo_ref, ubo_ref, do_ref, ao_ref, go_ref),
        (up_ref, ubp_ref, dp_ref, ap_ref, gp_ref),
    ):
        act, slope = gelu_parts(nn(n2, u_ref[...]) + ub_ref[...])
        act = act.astype(BF)
        a_ref[...] = act
        dg_ref[...] = slope.astype(BF)
        acc_ref[...] += nn(act, d_ref[...])

    @pl.when(j == pl.num_programs(0) - 1)
    def _():
        out_ref[...] = acc_ref[...].astype(BF)


def post_fwd(x, att, w):
    n, d = x.shape
    half = w["pw_o"].shape[0]
    fh = w["up_o"].shape[1]
    fb = fh // 2
    cols = lambda rows: pl.BlockSpec((rows, fb), lambda j: (0, j))
    rows_ = pl.BlockSpec((fb, d), lambda j: (j, 0))
    return pl.pallas_call(
        post_fwd_kernel,
        grid=(2,),
        in_specs=[
            whole((n, d)), whole((n, d)), whole((half, d)), whole((half, d)), whole((1, d)),
            whole((1, d)), whole((1, d)), cols(d), cols(d), cols(1), cols(1), rows_, rows_,
            whole((1, d)),
        ],
        out_specs=[
            whole((n, d)), whole((n, d)), cols(n), cols(n), cols(n), cols(n), whole((n, d)),
        ],
        out_shape=[
            sds((n, d), F32), sds((n, d), BF), sds((n, fh), BF), sds((n, fh), BF),
            sds((n, fh), BF), sds((n, fh), BF), sds((n, d), BF),
        ],
        scratch_shapes=[pltpu.VMEM((n, d), F32)],
        compiler_params=params(),
        name="post_fwd",
    )(
        x, att, w["pw_o"], w["pw_p"], w["pb"], w["g2"], w["b2"], w["up_o"], w["up_p"],
        w["ub_o"], w["ub_p"], w["dn_o"], w["dn_p"], w["db"],
    )


def forward(x, w, chunk):
    normed, qkv = pre_fwd(x, w)
    att, lse = attn_fwd(qkv, chunk)
    mid, n2, act_o, act_p, dg_o, dg_p, out = post_fwd(x, att, w)
    return (normed, qkv, att, lse, mid, n2, act_o, act_p, dg_o, dg_p, out)


def post_bwd_kernel(
    g_ref, mid_ref, gain_ref, go_ref, gp_ref, uo_ref, up_ref, do_ref, dp_ref, pwo_ref, pwp_ref,
    qo_ref, qp_ref, gm_ref, gb_ref, ga_ref, sums_ref, so_ref, sp_ref, copy_ref, acc_ref,
):
    j = pl.program_id(0)
    g = g_ref[...]

    @pl.when(j == 0)
    def _():
        acc_ref[...] = jnp.zeros_like(acc_ref)
        copy_ref[...] = g

    for dg_ref, u_ref, d_ref, q_ref, s_ref in (
        (go_ref, uo_ref, do_ref, qo_ref, so_ref),
        (gp_ref, up_ref, dp_ref, qp_ref, sp_ref),
    ):
        pre = (nt(g, d_ref[...]) * dg_ref[...].astype(F32)).astype(BF)
        q_ref[...] = pre
        s_ref[...] = rowsum(pre)
        acc_ref[...] += nt(pre, u_ref[...])

    @pl.when(j == pl.num_programs(0) - 1)
    def _():
        gn = acc_ref[...]
        xhat, rstd = norm_parts(mid_ref[...])
        gm = norm_back(xhat, rstd, gn, gain_ref[...]) + g.astype(F32)
        gm_ref[...] = gm
        gb = gm.astype(BF)
        gb_ref[...] = gb
        weight = jnp.concatenate([pwo_ref[...], pwp_ref[...]], axis=0)
        ga_ref[...] = nt(gb, weight).astype(BF)
        sums_ref[...] = jnp.concatenate(
            [rowsum(gn * xhat), rowsum(gn), rowsum(gb), rowsum(g)]
            + [jnp.zeros((4, gn.shape[1]), F32)], axis=0
        )


def post_bwd(g, kept, w):
    n, d = g.shape
    half = w["pw_o"].shape[0]
    fh = w["up_o"].shape[1]
    fb = fh // 2
    cols = lambda rows: pl.BlockSpec((rows, fb), lambda j: (0, j))
    rows_ = pl.BlockSpec((fb, d), lambda j: (j, 0))
    return pl.pallas_call(
        post_bwd_kernel,
        grid=(2,),
        in_specs=[
            whole((n, d)), whole((n, d)), whole((1, d)), cols(n), cols(n), cols(d), cols(d),
            rows_, rows_, whole((half, d)), whole((half, d)),
        ],
        out_specs=[
            cols(n), cols(n), whole((n, d)), whole((n, d)), whole((n, d)), whole((8, d)),
            cols(1), cols(1), whole((n, d)),
        ],
        out_shape=[
            sds((n, fh), BF), sds((n, fh), BF), sds((n, d), F32), sds((n, d), BF),
            sds((n, d), BF), sds((8, d), F32), sds((1, fh), F32), sds((1, fh), F32),
            sds((n, d), BF),
        ],
        scratch_shapes=[pltpu.VMEM((n, d), F32)],
        compiler_params=params(),
        name="post_bwd",
    )(
        g, kept["mid"], w["g2"], kept["dg_o"], kept["dg_p"], w["up_o"], w["up_p"], w["dn_o"],
        w["dn_p"], w["pw_o"], w["pw_p"],
    )


def attn_bwd_kernel(q_ref, k_ref, v_ref, ga_ref, l_ref, d_ref, s_ref, dq_tmp, *, nimg, plen, vlen):
    sums = [jnp.zeros((1, 128), F32) for _ in range(3)]
    at = 0
    for im in range(nimg):
        rows = slice(im * plen, (im + 1) * plen)
        k = k_ref[0, rows]
        v = v_ref[0, rows]
        kt = k.T
        queries = both_heads(q_ref[0, rows])
        grads = both_heads(ga_ref[rows])
        dk = jnp.zeros((plen, 128), F32)
        dv = jnp.zeros((plen, 128), F32)
        for q0, qw in qblocks(plen):
            q = queries[q0 : q0 + qw]
            ga = grads[q0 : q0 + qw]
            st = mask_keys(nt(k, q), vlen)
            p = jnp.exp2(st * SCALE2 - l_ref[0, :, at : at + qw])
            gp = nt(v, ga)
            dv += nn(p.astype(BF), ga)
            pg = p * gp
            ds = (pg - p * jnp.sum(pg, axis=0, keepdims=True)).astype(BF)
            dk += nn(ds, q)
            dq_tmp[q0 : q0 + qw] = nn(kt, ds).T
            at += 256
        dq = (one_each(dq_tmp, plen) * SCALE).astype(BF)
        dkb = (dk * SCALE).astype(BF)
        dvb = dv.astype(BF)
        d_ref[0, rows] = dq
        d_ref[1, rows] = dkb
        d_ref[2, rows] = dvb
        sums[0] += rowsum(dq)
        sums[2] += rowsum(dvb)
    s_ref[...] = jnp.concatenate(sums + [jnp.zeros((5, 128), F32)], axis=0)


def attn_bwd(qkv, ga, lse, chunk):
    nimg, plen, vlen = chunk
    _, n, d = qkv.shape
    pairs = d // 128
    return pl.pallas_call(
        functools.partial(attn_bwd_kernel, nimg=nimg, plen=plen, vlen=vlen),
        grid=(pairs,),
        in_specs=[pl.BlockSpec((1, n, 128), lambda p, s=s: (s, 0, p)) for s in range(3)]
        + [
            pl.BlockSpec((n, 128), lambda p: (0, p)),
            pl.BlockSpec((1, 1, lse_width(chunk)), lambda p: (p, 0, 0)),
        ],
        out_specs=[
            pl.BlockSpec((3, n, 128), lambda p: (0, 0, p)),
            pl.BlockSpec((8, 128), lambda p: (0, p)),
        ],
        out_shape=[sds((3, n, d), BF), sds((8, d), F32)],
        scratch_shapes=[pltpu.VMEM((2 * plen, 128), F32)],
        compiler_params=params(),
        name="attn_bwd",
    )(qkv, qkv, qkv, ga, lse)


def pre_bwd_kernel(d_ref, wo_ref, wp_ref, x_ref, gain_ref, gm_ref, out_ref, sums_ref, acc_ref):
    j = pl.program_id(0)
    weight = jnp.concatenate([wo_ref[0], wp_ref[0]], axis=1)
    part = nt(d_ref[0], weight)

    @pl.when(j == 0)
    def _():
        acc_ref[...] = part

    @pl.when(j > 0)
    def _():
        acc_ref[...] += part

    @pl.when(j == pl.num_programs(0) - 1)
    def _():
        gn = acc_ref[...]
        xhat, rstd = norm_parts(x_ref[...].astype(F32))
        out_ref[...] = (norm_back(xhat, rstd, gn, gain_ref[...]) + gm_ref[...]).astype(BF)
        sums_ref[...] = jnp.concatenate(
            [rowsum(gn * xhat), rowsum(gn), jnp.zeros((6, gn.shape[1]), F32)], axis=0
        )


def pre_bwd(dqkv, x, gm, w):
    _, n, d = dqkv.shape
    half = w["wqkv_o"].shape[-1]
    return pl.pallas_call(
        pre_bwd_kernel,
        grid=(3,),
        in_specs=[
            pl.BlockSpec((1, n, d), lambda s: (s, 0, 0)),
            pl.BlockSpec((1, d, half), lambda s: (s, 0, 0)),
            pl.BlockSpec((1, d, half), lambda s: (s, 0, 0)),
            whole((n, d)), whole((1, d)), whole((n, d)),
        ],
        out_specs=[whole((n, d)), whole((8, d))],
        out_shape=[sds((n, d), BF), sds((8, d), F32)],
        scratch_shapes=[pltpu.VMEM((n, d), F32)],
        compiler_params=params(),
        name="pre_bwd",
    )(dqkv, w["wqkv_o"], w["wqkv_p"], x, w["g1"], gm)


def backward(g, x, kept, w, chunk):
    pre_o, pre_p, gm, gb, ga, sums2, so, sp, copy = post_bwd(g, kept, w)
    dqkv, sums_qkv = attn_bwd(kept["qkv"], ga, kept["lse"], chunk)
    gx, sums1 = pre_bwd(dqkv, x, gm, w)
    return (copy, pre_o, pre_p, gb, dqkv, sums2, so, sp, sums_qkv, sums1, gx)


def wgrad_mlp_kernel(*refs, more):
    ao, ap, n2, po, pp, g = refs[:6]
    init = refs[6 : 6 + more]
    outs = refs[6 + more :]
    g, n2 = g[...], n2[...]
    results = (
        tn(ao[...], g), tn(ap[...], g), tn(n2, po[...]), tn(n2, pp[...]),
    )
    for i, (out, value) in enumerate(zip(outs, results)):
        if more:
            value += init[i][...].astype(F32)
        out[...] = value.astype(BF)


def wgrad_mlp(kept, back, init=()):
    n, d = back["g"].shape
    fh = kept["act_o"].shape[1]
    fb = fh // 4
    cols = lambda rows: pl.BlockSpec((rows, fb), lambda j: (0, j))
    rows_ = pl.BlockSpec((fb, d), lambda j: (j, 0))
    outs = [rows_, rows_, cols(d), cols(d)]
    return pl.pallas_call(
        functools.partial(wgrad_mlp_kernel, more=len(init)),
        grid=(4,),
        in_specs=[cols(n), cols(n), whole((n, d)), cols(n), cols(n), whole((n, d))]
        + outs[: len(init)],
        out_specs=outs,
        out_shape=[sds((fh, d), BF)] * 2 + [sds((d, fh), BF)] * 2,
        compiler_params=params(),
        name="wgrad_mlp",
    )(kept["act_o"], kept["act_p"], kept["n2"], back["pre_o"], back["pre_p"], back["g"], *init)


def wgrad_attn_kernel(*refs, more):
    normed, dqkv, att, gb = refs[:4]
    init = refs[4 : 4 + more]
    outs = refs[4 + more :]
    s = pl.program_id(0)
    total = tn(normed[...], dqkv[0])
    half = outs[0].shape[-1]
    for i, value in enumerate((total[:, :half], total[:, half:])):
        if more:
            value += init[i][0].astype(F32)
        outs[i][0] = value.astype(BF)
    for i in range(2):

        @pl.when(s == i)
        def _():
            value = tn(att[...], gb[...])
            if more:
                value += init[2 + i][...].astype(F32)
            outs[2 + i][...] = value.astype(BF)


def wgrad_attn(kept, back, init=()):
    n, d = kept["normed"].shape
    half = d // 2
    part = pl.BlockSpec((1, d, half), lambda s: (s, 0, 0))
    outs = [part, part, whole((half, d)), whole((half, d))]
    return pl.pallas_call(
        functools.partial(wgrad_attn_kernel, more=len(init)),
        grid=(3,),
        in_specs=[
            whole((n, d)), pl.BlockSpec((1, n, d), lambda s: (s, 0, 0)),
            pl.BlockSpec((n, half), lambda s: (0, jnp.minimum(s, 1))), whole((n, d)),
        ]
        + outs[: len(init)],
        out_specs=outs,
        out_shape=[sds((3, d, half), BF)] * 2 + [sds((half, d), BF)] * 2,
        compiler_params=params(),
        name="wgrad_attn",
    )(kept["normed"], back["dqkv"], kept["att"], back["gb"], *init)


RING = 8
VEC_ROWS = 16


def items_of(d):
    return ((0, 0, 2 * d, 1), (2, 0, 2 * d, 1), (1, 0, d, -1), (2, 2 * d, d, -1), (3, 0, d // 2, -1))


def vector_block(sums):
    s1, s2, sq, so, sp = sums
    d = s1.shape[1]
    wide = lambda v: [v[:, i : i + d] for i in range(0, v.shape[1], d)]
    rows = [s1[:2], s2[:4], sq[0:1], sq[2:3]] + wide(so) + wide(sp)
    used = 8 + 2 * (so.shape[1] // d)
    return jnp.concatenate(rows + [jnp.zeros((VEC_ROWS - used, d), F32)], axis=0)


def as_own(block, fold):
    half = block.shape[1] // 2
    qv = block[6:8]
    return jnp.concatenate(
        [
            block[:6], jnp.concatenate([qv[:, half:], qv[:, :half]], axis=1),
            block[8 + fold : 8 + 2 * fold], block[8 : 8 + fold], block[8 + 2 * fold :],
        ],
        axis=0,
    )


def ring_kernel(*refs, n, items, fold):
    owns, gifts = refs[:n], refs[n : 2 * n]
    sums = refs[2 * n : 2 * n + 10]
    at = 2 * n + 10
    outs, vsum_ref = refs[at : at + n], refs[at + n]
    at += n + 1
    theirs = refs[at : at + n]
    at += n
    m = len(items)
    slots = refs[at : at + m]
    vbuf, vother, vmine, vslot, send, recv, xsend, xrecv, vsend, vrecv, vxs, vxr = refs[at + m :]
    mesh_id = pl.DeviceIdType.MESH
    me = lax.axis_index("dp")
    partner = {"tensor": 1 - lax.axis_index("tensor")}
    z, x = me // 2, me % 2
    pos = z + x * (RING - 1 - 2 * z)

    def member(p):
        p = p % RING
        return {"dp": 2 * p + (p // (RING // 2)) * (2 * RING - 1 - 4 * p)}

    barrier = pltpu.get_barrier_semaphore()
    for k in range(1, RING):
        pl.semaphore_signal(barrier, inc=1, device_id=member(pos + k), device_id_type=mesh_id)
    pl.semaphore_signal(barrier, inc=1, device_id=partner, device_id_type=mesh_id)
    pl.semaphore_wait(barrier, RING)

    def part(arrays, a, chunk):
        i, first, rows, _ = items[a]
        rows = rows // RING
        return arrays[i].at[pl.ds(pl.multiple_of(first + (chunk % RING) * rows, rows), rows)]

    def chunk_at(a, step):
        return pos + 2 * RING - items[a][3] * step

    def exchange(a, step):
        return pltpu.make_async_remote_copy(
            src_ref=part(gifts, a, chunk_at(a, step)),
            dst_ref=part(theirs, a, chunk_at(a, step)),
            send_sem=xsend.at[a, step],
            recv_sem=xrecv.at[a, step],
            device_id=partner,
            device_id_type=mesh_id,
        )

    def mine(a, step):
        exchange(a, step).wait_recv()
        chunk = chunk_at(a, step)
        return part(owns, a, chunk)[...].astype(F32) + part(theirs, a, chunk)[...].astype(F32)

    def remote(src, dst, a, step):
        return pltpu.make_async_remote_copy(
            src_ref=src,
            dst_ref=dst,
            send_sem=send.at[a, step],
            recv_sem=recv.at[a, step],
            device_id=member(pos + items[a][3] + RING),
            device_id_type=mesh_id,
        )

    def vcopy(k):
        return pltpu.make_async_remote_copy(
            src_ref=vmine,
            dst_ref=vslot.at[k - 1],
            send_sem=vsend.at[k - 1],
            recv_sem=vrecv.at[k - 1],
            device_id=member(pos + k),
            device_id_type=mesh_id,
        )

    vexchange = pltpu.make_async_remote_copy(
        src_ref=vbuf, dst_ref=vother, send_sem=vxs, recv_sem=vxr,
        device_id=partner, device_id_type=mesh_id,
    )

    for step in range(2):
        for a in range(m):
            exchange(a, step).start()
    vbuf[...] = vector_block([sums[i][...] + sums[5 + i][...] for i in range(5)])
    vexchange.start()
    for a in range(m):
        slots[a][0] = mine(a, 0).astype(BF)
        remote(slots[a].at[0], slots[a].at[1], a, 0).start()

    def scatter(s, carry):
        for a in range(m):
            exchange(a, s + 1).start()
        for a in range(m):
            here = slots[a].at[s]
            own = mine(a, s)
            remote(here, here, a, s - 1).wait_recv()
            here[...] = (here[...].astype(F32) + own).astype(BF)
            remote(here, slots[a].at[s + 1], a, s).start()
        return carry

    lax.fori_loop(1, RING - 1, scatter, 0)
    vexchange.wait()
    vmine[...] = vbuf[...] + as_own(vother[...], fold)
    for k in range(1, RING):
        vcopy(k).start()
    for a in range(m):
        last = slots[a].at[RING - 1]
        own = mine(a, RING - 1)
        remote(last, last, a, RING - 2).wait_recv()
        done = part(outs, a, chunk_at(a, RING - 1))
        done[...] = (last[...].astype(F32) + own).astype(BF)
        remote(done, done, a, RING - 1).start()

    def gather(t, carry):
        for a in range(m):
            here = part(outs, a, chunk_at(a, t - 1))
            remote(here, here, a, RING - 2 + t).wait_recv()
            remote(here, here, a, RING - 1 + t).start()
        return carry

    lax.fori_loop(1, RING - 1, gather, 0)
    total = vmine[...]
    for k in range(1, RING):
        vcopy(k).wait()
        total += vslot[k - 1]
    vsum_ref[...] = total
    for a in range(m):
        here = part(outs, a, chunk_at(a, RING - 2))
        remote(here, here, a, 2 * RING - 3).wait_recv()
    for a in range(m):
        for s in range(RING - 1):
            remote(slots[a].at[0], slots[a].at[0], a, s).wait_send()
            here = part(outs, a, pos)
            remote(here, here, a, RING - 1 + s).wait_send()
        for s in range(RING):
            exchange(a, s).wait_send()


def ring(owns, gifts, sums_s, sums_l):
    n = len(owns)
    d = owns[0].shape[1]
    items = items_of(d)
    m = len(items)
    vmem = pl.BlockSpec(memory_space=pltpu.VMEM)
    dma = pltpu.SemaphoreType.DMA
    vec = pltpu.VMEM((VEC_ROWS, d), F32)
    out = pl.pallas_call(
        functools.partial(ring_kernel, n=n, items=items, fold=sums_s[3].shape[1] // d),
        in_specs=[vmem] * (2 * n + 10),
        out_specs=[vmem] * (n + 1),
        out_shape=[sds(a.shape, BF) for a in owns] + [sds((VEC_ROWS, d), F32)],
        scratch_shapes=[pltpu.VMEM(a.shape, BF) for a in owns]
        + [pltpu.VMEM((RING, rows // RING, owns[i].shape[1]), BF) for i, _, rows, _ in items]
        + [
            vec, vec, vec, pltpu.VMEM((RING - 1, VEC_ROWS, d), F32),
            dma((m, 2 * RING - 2)), dma((m, 2 * RING - 2)), dma((m, RING)), dma((m, RING)),
            dma((RING - 1,)), dma((RING - 1,)), dma, dma,
        ],
        compiler_params=params(collective_id=1, has_side_effects=True),
        name="ring",
    )(*owns, *gifts, *sums_s, *sums_l)
    return out[:n], out[n]


def dp_sum(owns, gifts, sums_s, sums_l):
    if lax.axis_size("dp") == RING:
        return ring(owns, gifts, sums_s, sums_l)
    other = lambda array: lax.ppermute(array, "tensor", [(0, 1), (1, 0)])
    fold = sums_s[3].shape[1] // owns[0].shape[1]
    block = vector_block([a + b for a, b in zip(sums_s, sums_l)])
    summed = [lax.psum(a + other(b), "dp") for a, b in zip(owns, gifts)]
    return summed, lax.psum(block + as_own(other(block), fold), "dp")


def finish_kernel(*refs, fold):
    grads, vec, outs = refs[:4], refs[4], refs[5:]
    for g, out in zip(grads, outs):
        out[0] = g[...].astype(F32)

    @pl.when(pl.program_id(0) == 0)
    def _():
        half = vec.shape[1] // 2
        for i in range(6):
            outs[4 + i][...] = vec[i : i + 1]
        outs[10][0] = vec[6:8, :half]
        outs[11][...] = jnp.concatenate([vec[8 + i : 9 + i] for i in range(fold)], axis=1)


def finish(grads, vec):
    d = vec.shape[1]
    fold = grads[1].shape[1] // d
    steps = 8
    rows_in = lambda a: pl.BlockSpec((a.shape[0] // steps, a.shape[1]), lambda j: (j, 0))
    rows_out = lambda a: pl.BlockSpec((1, a.shape[0] // steps, a.shape[1]), lambda j: (0, j, 0))
    small = [(1, d)] * 6 + [(1, 2, d // 2), (1, fold * d)]
    return pl.pallas_call(
        functools.partial(finish_kernel, fold=fold),
        grid=(steps,),
        in_specs=[rows_in(a) for a in grads] + [whole(vec.shape)],
        out_specs=[rows_out(a) for a in grads] + [whole(a) for a in small],
        out_shape=[sds((1,) + a.shape, F32) for a in grads] + [sds(a, F32) for a in small],
        compiler_params=params(),
        name="finish",
    )(*grads, vec)


def starts_of(place):
    slots = [j + (j >= place) for j in range(SMALL_MB)]
    return [place * LEN_SMALL] + [
        slot * LEN_SMALL + (LEN_LARGE - LEN_SMALL) * (slot > place) for slot in slots
    ]


def layout(place):
    at = 0
    starts = starts_of(place)
    for c, (nimg, plen, vlen) in enumerate(CHUNKS):
        for i in range(nimg):
            yield starts[at], c, i * plen, plen, vlen
            at += 1


def cut_kernel(meta_ref, x_ref, *refs):
    outs, flat = refs[:-1], refs[-1]
    rows = x_ref.shape[0]
    flat[:rows] = x_ref[...].astype(F32)
    flat[rows:] = jnp.zeros((flat.shape[0] - rows, flat.shape[1]), F32)
    for place in range(SMALL_MB + 1):

        @pl.when(meta_ref[1 + meta_ref[0]] == place)
        def _():
            for start, c, r0, plen, vlen in layout(place):
                value = flat[start : start + plen]
                row = lax.broadcasted_iota(jnp.int32, value.shape, 0)
                outs[c][r0 : r0 + plen] = jnp.where(row < vlen, value, 0.0).astype(BF)


def cut(array, meta):
    rows = LEN_LARGE + SMALL_MB * LEN_SMALL
    d = array.shape[1]
    block = d // 3
    return pl.pallas_call(
        cut_kernel,
        grid_spec=pltpu.PrefetchScalarGridSpec(
            num_scalar_prefetch=1,
            grid=(3,),
            in_specs=[pl.BlockSpec((rows, block), lambda j, m: (m[0], j))],
            out_specs=[pl.BlockSpec((k * p, block), lambda j, m: (0, j)) for k, p, _ in CHUNKS],
            scratch_shapes=[pltpu.VMEM((rows + 16, block), F32)],
        ),
        out_shape=[sds((k * p, d), BF) for k, p, _ in CHUNKS],
        compiler_params=params(),
        name="cut",
    )(meta, array)


def join_kernel(meta_ref, *refs):
    count = len(CHUNKS)
    mine, theirs, out_ref, flat = refs[:count], refs[count : 2 * count], refs[-2], refs[-1]
    rows = flat.shape[0]
    for lane in range(2):
        here = meta_ref[0] == lane
        for place in range(SMALL_MB + 1):

            @pl.when(meta_ref[1 + lane] == place)
            def _():
                for start, c, r0, plen, vlen in layout(place):
                    own = mine[c][r0 : r0 + plen].astype(F32)
                    value = jnp.where(here, own, theirs[c][r0 : r0 + plen].astype(F32))
                    flat[start : start + vlen] = value[:vlen]

        out_ref[lane * rows : (lane + 1) * rows] = flat[...].astype(BF)


def join(mine, theirs, meta):
    rows = LEN_LARGE + SMALL_MB * LEN_SMALL
    d = mine[0].shape[1]
    block = d // 3
    return pl.pallas_call(
        join_kernel,
        grid_spec=pltpu.PrefetchScalarGridSpec(
            num_scalar_prefetch=1,
            grid=(3,),
            in_specs=[pl.BlockSpec((k * p, block), lambda j, m: (0, j)) for k, p, _ in CHUNKS] * 2,
            out_specs=pl.BlockSpec((2 * rows, block), lambda j, m: (0, j)),
            scratch_shapes=[pltpu.VMEM((rows, block), F32)],
        ),
        out_shape=sds((2 * rows, d), BF),
        compiler_params=params(),
        name="join",
    )(meta, *mine, *theirs)


def blank_kernel(*refs):
    pass


def blank(like):
    shapes = [sds(a.shape, a.dtype) for a in like]
    return tuple(
        pl.pallas_call(
            blank_kernel,
            out_shape=shapes,
            out_specs=[pl.BlockSpec(memory_space=pl.ANY) for _ in shapes],
            name="blank",
        )()
    )


KEPT = ("normed", "qkv", "att", "lse", "mid", "n2", "act_o", "act_p", "dg_o", "dg_p", "out")
BACK = ("g", "pre_o", "pre_p", "gb", "dqkv", "sums2", "so", "sp", "sums_qkv", "sums1", "gx")


def after(value, *earlier):
    return lax.optimization_barrier((value, earlier))[0]


def body(
    patches, out_grad, large_place, norm1_gain, norm1_bias, qkv_weight, qv_bias, proj_weight,
    proj_bias, norm2_gain, norm2_bias, up_weight, up_bias, down_weight, down_bias,
):
    d = patches.shape[1]
    half = qkv_weight.shape[-1]
    section = lax.axis_index("section")
    lane = lax.axis_index("tensor")
    both = [(0, 1), (1, 0)]
    other = lambda array: lax.ppermute(array, "tensor", both)

    wqkv, pw, up, dn = qkv_weight[0], proj_weight[0], up_weight[0], down_weight[0]
    w = {
        "g1": norm1_gain, "b1": norm1_bias, "g2": norm2_gain, "b2": norm2_bias,
        "pb": proj_bias, "db": down_bias,
        "wqkv_o": wqkv, "wqkv_p": other(wqkv), "pw_o": pw, "pw_p": other(pw),
        "up_o": up, "up_p": other(up), "dn_o": dn, "dn_p": other(dn),
        "bq_o": qv_bias[0], "bq_p": other(qv_bias[0]), "ub_o": up_bias, "ub_p": other(up_bias),
    }


    meta = jnp.concatenate([lane[None], large_place])
    large, smalls = 0, 1
    xs = cut(patches, meta)
    gs = cut(out_grad, meta)

    def fwd(c, on, x, otherwise=None):
        like = jax.eval_shape(functools.partial(forward, chunk=CHUNKS[c]), x, w)
        return lax.cond(
            section == on,
            lambda: tuple(forward(x, w, CHUNKS[c])),
            lambda: blank(like) if otherwise is None else tuple(otherwise),
        )

    def bwd(c, on, g, x, kept, otherwise=None):
        kept = dict(zip(KEPT, kept))
        like = jax.eval_shape(functools.partial(backward, chunk=CHUNKS[c]), g, x, kept, w)
        return lax.cond(
            section == on,
            lambda: tuple(backward(g, x, kept, w, CHUNKS[c])),
            lambda: blank(like) if otherwise is None else tuple(otherwise),
        )

    down = lambda array: lax.ppermute(array, "section", [(0, 1)])
    up_ = lambda array: lax.ppermute(array, "section", [(1, 0)])

    kept_s = fwd(smalls, 0, xs[smalls])
    in_s = down(kept_s[-1])
    kept_l = fwd(large, 0, after(xs[large], kept_s[-1]))
    in_l = down(kept_l[-1])
    in_s = after(in_s, kept_l[-1])
    kept_s = fwd(smalls, 1, in_s, kept_s)
    back_s = bwd(smalls, 1, gs[smalls], in_s, kept_s)
    sent_s = up_(back_s[-1])
    in_l = after(in_l, back_s[-1])
    kept_l = fwd(large, 1, in_l, kept_l)
    back_l = bwd(large, 1, gs[large], in_l, kept_l)
    sent_l = up_(back_l[-1])
    back_s = bwd(smalls, 0, after(sent_s, back_l[-1]), xs[smalls], kept_s, back_s)
    named = lambda names, values: dict(zip(names, values))
    part_mlp = wgrad_mlp(named(KEPT, kept_s), named(BACK, back_s))
    part_attn = wgrad_attn(named(KEPT, kept_s), named(BACK, back_s))
    outs = [kept_l[-1], kept_s[-1]]
    outputs = join(outs, [other(a) for a in outs], meta)
    sent_l = after(sent_l, part_mlp, part_attn, outputs)
    back_l = bwd(large, 0, sent_l, xs[large], kept_l, back_l)
    dn_o, dn_p, up_o, up_p = wgrad_mlp(named(KEPT, kept_l), named(BACK, back_l), part_mlp)
    qkv_o, qkv_p, pw_o, pw_p = wgrad_attn(named(KEPT, kept_l), named(BACK, back_l), part_attn)
    grads = [back_l[-1], back_s[-1]]
    input_grads = join(grads, [other(a) for a in grads], meta)

    rows = lambda qkv: qkv.reshape(3 * d, half)
    sums = lambda back: [named(BACK, back)[k] for k in ("sums1", "sums2", "sums_qkv", "so", "sp")]
    summed, vec = dp_sum(
        [dn_o, up_o, rows(qkv_o), pw_o], [dn_p, up_p, rows(qkv_p), pw_p], sums(back_s), sums(back_l)
    )
    g_dn, g_up, g_qkv, g_pw, g1, b1, g2, b2, pb, db, qv, ub = finish(summed, vec)
    return (
        outputs[None], input_grads[None], g1, b1, g_qkv.reshape(1, 3, d, half), qv, g_pw, pb,
        g2, b2, g_up, ub, g_dn, db,
    )


def solution(mesh):
    placed = (
        P("dp", None), P("dp", None), P("dp"), P("section", None), P("section", None),
        P("section", None, None, "tensor"), P("section", None, "tensor"),
        P("section", "tensor", None), P("section", None), P("section", None),
        P("section", None), P("section", None, "tensor"), P("section", "tensor"),
        P("section", "tensor", None), P("section", None),
    )
    return jax.shard_map(
        body,
        mesh=mesh,
        in_specs=placed,
        out_specs=(
            P("section", "dp", None), P("section", "dp", None), P("section", None),
            P("section", None), P("section", None, None, "tensor"), P("section", None, "tensor"),
            P("section", "tensor", None), P("section", None), P("section", None),
            P("section", None), P("section", None, "tensor"), P("section", "tensor"),
            P("section", "tensor", None), P("section", None),
        ),
        check_vma=False,
    )
```

```python
import functools

import jax
import jax.numpy as jnp
from jax import lax
from jax.experimental import pallas as pl
from jax.experimental.pallas import tpu as pltpu
from jax.sharding import PartitionSpec as P

HD = 64
LEN_SMALL = 197
LEN_LARGE = 577
SMALL_MB = 3
EPSILON = 1e-06
MASKED = -1e30
SCALE = HD ** (-0.5)
SCALE2 = SCALE * 1.4426950408889634
BF = jnp.bfloat16
F32 = jnp.float32
VMEM_LIMIT = 56 * 1024 * 1024
CHUNKS = ((1, 592, LEN_LARGE), (SMALL_MB, 208, LEN_SMALL))


def params(limit=VMEM_LIMIT, **more):
    return pltpu.CompilerParams(vmem_limit_bytes=limit, **more)


def nn(a, b):
    return jnp.dot(a, b, preferred_element_type=F32)


def nt(a, b):
    return lax.dot_general(a, b, (((1,), (1,)), ((), ())), preferred_element_type=F32)


def tn(a, b):
    return lax.dot_general(a, b, (((0,), (0,)), ((), ())), preferred_element_type=F32)


def whole(shape):
    zeros = (0,) * len(shape)
    return pl.BlockSpec(shape, lambda *_: zeros)


def sds(shape, dtype):
    return jax.ShapeDtypeStruct(shape, dtype)


def norm_parts(values):
    mean = jnp.mean(values, axis=-1, keepdims=True)
    centred = values - mean
    rstd = lax.rsqrt(jnp.mean(centred * centred, axis=-1, keepdims=True) + EPSILON)
    return centred * rstd, rstd


def norm_back(xhat, rstd, grad, gain):
    scaled = grad * gain
    m1 = jnp.mean(scaled, axis=-1, keepdims=True)
    m2 = jnp.mean(scaled * xhat, axis=-1, keepdims=True)
    return rstd * (scaled - m1 - xhat * m2)


def rowsum(values):
    return jnp.sum(values.astype(F32), axis=0, keepdims=True)


def fetch(pairs, sems):
    return [pltpu.make_async_copy(src, dst, sems.at[i]) for i, (src, dst) in enumerate(pairs)]


def weight_loads(w, wq, pw, up, dn):
    wqo, wqp, pwo, pwp, upo, upp, dno, dnp = w
    half, fh = wqo.shape[-1], dno.shape[0]
    return {
        "qkv": [(wqo, wq.at[:, :, :half]), (wqp, wq.at[:, :, half:])],
        "proj": [(pwo, pw.at[:half]), (pwp, pw.at[half:])],
        "up": [(upo, up.at[:, :fh]), (upp, up.at[:, fh:])],
        "down": [(dno, dn.at[:fh]), (dnp, dn.at[fh:])],
    }


def weights_of(w):
    return [w[k] for k in ("wqkv_o", "wqkv_p", "pw_o", "pw_p", "up_o", "up_p", "dn_o", "dn_p")]


def weight_scratch(d, ff):
    return [
        pltpu.VMEM((3, d, d), BF), pltpu.VMEM((d, d), BF), pltpu.VMEM((d, ff), BF),
        pltpu.VMEM((ff, d), BF),
    ]


def lanes(at, width):
    return pl.ds(pl.multiple_of(at * width, width), width)


def mask_keys(scores, vlen):
    rows = scores.shape[0]
    keep = vlen // 8 * 8
    tail = scores[keep:]
    idx = lax.broadcasted_iota(jnp.int32, tail.shape, 0) + keep
    return jnp.concatenate([scores[:keep], jnp.where(idx < vlen, tail, MASKED)], axis=0)


def qblocks(plen):
    step = min(256, plen)
    return [(q, min(step, 2 * plen - q)) for q in range(0, 2 * plen, step)]


def lse_width(chunk):
    nimg, plen, _ = chunk
    return nimg * len(qblocks(plen)) * 256


def both_heads(rows):
    head = lax.broadcasted_iota(jnp.int32, rows.shape, 1) // HD
    none = jnp.zeros_like(rows)
    return jnp.concatenate([jnp.where(head == h, rows, none) for h in range(2)], axis=0)


def one_each(stacked, plen):
    head = lax.broadcasted_iota(jnp.int32, (plen, stacked.shape[1]), 1) // HD
    return jnp.where(head == 0, stacked[:plen], stacked[plen:])


def attn_fwd_pair(p, qkv, att, lse, o_tmp, chunk):
    nimg, plen, vlen = chunk
    cols = lanes(p, 128)
    at = 0
    for im in range(nimg):
        rows = slice(im * plen, (im + 1) * plen)
        k = qkv[1, rows, cols]
        vt = qkv[2, rows, cols].T
        queries = both_heads(qkv[0, rows, cols])
        for q0, qw in qblocks(plen):
            st = mask_keys(nt(k, queries[q0 : q0 + qw]), vlen)
            top = jnp.max(st, axis=0, keepdims=True)
            e = jnp.exp2((st - top) * SCALE2)
            total = jnp.sum(e, axis=0, keepdims=True)
            o_tmp[q0 : q0 + qw] = (nn(vt, e.astype(BF)) * (1.0 / total)).T
            lse[p, :, at : at + qw] = top * SCALE2 + jnp.log2(total)
            at += 256
        att[rows, cols] = one_each(o_tmp, plen).astype(BF)


def gelu_parts(x):
    cdf = 0.5 + 0.5 * lax.erf(x * (2.0**-0.5))
    pdf = jnp.exp(-0.5 * x * x) * 0.3989422804014327
    return x * cdf, cdf + x * pdf


FF_STEPS = 2
WGRAD_STEPS = 4


def fwd_kernel(*refs, chunk):
    x_ref, g1, b1, bqo, bqp, pb, g2, b2, ubo, ubp, db = refs[:11]
    weights, outs = refs[11:19], refs[19:28]
    wq, pw, up, dn = refs[28:32]
    held = refs[32:41]
    acc, o_tmp, ub, in_sem, out_sem, ff_sem = refs[41:]
    normed, qkv, att, lse, mid, n2, act, dg, out = held
    ff = dn.shape[0]
    fb = ff // FF_STEPS
    loads = weight_loads(weights, wq, pw, up, dn)
    names = ("qkv", "proj", "up", "down")
    loads = {k: fetch(loads[k], in_sem.at[i]) for i, k in enumerate(names)}
    saves = fetch(list(zip(held[:6] + held[8:], outs[:6] + outs[8:])), out_sem)
    for c in loads["qkv"]:
        c.start()
    xhat, _ = norm_parts(x_ref[...].astype(F32))
    normed[...] = (xhat * g1[...] + b1[...]).astype(BF)
    saves[0].start()
    ub[...] = jnp.concatenate([ubo[...], ubp[...]], axis=1)
    biases = jnp.concatenate([bqo[...], bqp[...]], axis=1)
    for c in loads["qkv"]:
        c.wait()
    for k in names[1:]:
        for c in loads[k]:
            c.start()

    def project(s, carry):
        bias = jnp.where(s == 0, biases[:1], jnp.where(s == 1, 0.0, biases[1:]))
        qkv[s] = (nn(normed[...], wq[s]) + bias).astype(BF)
        return carry

    lax.fori_loop(0, 3, project, 0)
    saves[1].start()

    def attend(p, carry):
        attn_fwd_pair(p, qkv, att, lse, o_tmp, chunk)
        return carry

    lax.fori_loop(0, lse.shape[0], attend, 0)
    saves[2].start()
    saves[3].start()
    for c in loads["proj"]:
        c.wait()
    middle = x_ref[...].astype(F32) + (nn(att[...], pw[...]) + pb[...])
    mid[...] = middle
    saves[4].start()
    xhat, _ = norm_parts(middle)
    n2[...] = (xhat * g2[...] + b2[...]).astype(BF)
    saves[5].start()
    acc[...] = middle + db[...]
    for k in ("up", "down"):
        for c in loads[k]:
            c.wait()

    def block_saves(j):
        cols = lanes(j, fb)
        pairs = [(act.at[:, cols], outs[6].at[:, cols]), (dg.at[:, cols], outs[7].at[:, cols])]
        return fetch(pairs, ff_sem.at[j])

    def mlp(j, carry):
        cols = lanes(j, fb)
        value, slope = gelu_parts(nn(n2[...], up[:, cols]) + ub[:, cols])
        value = value.astype(BF)
        act[:, cols] = value
        dg[:, cols] = slope.astype(BF)
        for c in block_saves(j):
            c.start()
        acc[...] += nn(value, dn[cols])
        return carry

    lax.fori_loop(0, FF_STEPS, mlp, 0)
    out[...] = acc[...].astype(BF)
    saves[6].start()
    for c in saves:
        c.wait()
    for j in range(FF_STEPS):
        for c in block_saves(j):
            c.wait()


def forward(x, w, chunk):
    n, d = x.shape
    ff = 2 * w["dn_o"].shape[0]
    pairs = d // 128
    kept = [
        ((n, d), BF), ((3, n, d), BF), ((n, d), BF), ((pairs, 1, lse_width(chunk)), F32),
        ((n, d), F32), ((n, d), BF), ((n, ff), BF), ((n, ff), BF), ((n, d), BF),
    ]
    vmem = pl.BlockSpec(memory_space=pltpu.VMEM)
    hbm = pl.BlockSpec(memory_space=pl.ANY)
    return pl.pallas_call(
        functools.partial(fwd_kernel, chunk=chunk),
        in_specs=[vmem] * 11 + [hbm] * 8,
        out_specs=[hbm] * len(kept),
        out_shape=[sds(*k) for k in kept],
        scratch_shapes=weight_scratch(d, ff)
        + [pltpu.VMEM(*k) for k in kept]
        + [
            pltpu.VMEM((n, d), F32), pltpu.VMEM((2 * chunk[1], 128), F32),
            pltpu.VMEM((1, ff), F32), pltpu.SemaphoreType.DMA((4, 2)),
            pltpu.SemaphoreType.DMA((7,)), pltpu.SemaphoreType.DMA((FF_STEPS, 2)),
        ],
        compiler_params=params(),
        name="fwd",
    )(
        x, w["g1"], w["b1"], w["bq_o"], w["bq_p"], w["pb"], w["g2"], w["b2"], w["ub_o"],
        w["ub_p"], w["db"], *weights_of(w),
    )


def attn_bwd_pair(p, qkv, gatt, lse, dqkv, sums, dq_tmp, chunk):
    nimg, plen, vlen = chunk
    cols = lanes(p, 128)
    total_q, total_v = jnp.zeros((1, 128), F32), jnp.zeros((1, 128), F32)
    at = 0
    for im in range(nimg):
        rows = slice(im * plen, (im + 1) * plen)
        k = qkv[1, rows, cols]
        v = qkv[2, rows, cols]
        kt = k.T
        queries = both_heads(qkv[0, rows, cols])
        grads = both_heads(gatt[rows, cols])
        dk = jnp.zeros((plen, 128), F32)
        dv = jnp.zeros((plen, 128), F32)
        for q0, qw in qblocks(plen):
            q = queries[q0 : q0 + qw]
            ga = grads[q0 : q0 + qw]
            st = mask_keys(nt(k, q), vlen)
            pr = jnp.exp2(st * SCALE2 - lse[p, :, at : at + qw])
            gp = nt(v, ga)
            dv += nn(pr.astype(BF), ga)
            pg = pr * gp
            ds = (pg - pr * jnp.sum(pg, axis=0, keepdims=True)).astype(BF)
            dk += nn(ds, q)
            dq_tmp[q0 : q0 + qw] = nn(kt, ds).T
            at += 256
        dq = (one_each(dq_tmp, plen) * SCALE).astype(BF)
        dvb = dv.astype(BF)
        dqkv[0, rows, cols] = dq
        dqkv[1, rows, cols] = (dk * SCALE).astype(BF)
        dqkv[2, rows, cols] = dvb
        total_q += rowsum(dq)
        total_v += rowsum(dvb)
    sums[:, cols] = jnp.concatenate(
        [total_q, jnp.zeros_like(total_q), total_v, jnp.zeros((5, 128), F32)], axis=0
    )


def bwd_kernel(*refs, chunk):
    g_ref, g2, g1 = refs[:3]
    mid_h, dg_h, qkv_h, lse_h, x_h = refs[3:8]
    weights, outs = refs[8:16], refs[16:21]
    sums2, sff, sums_qkv, sums1 = refs[21:25]
    wq, pw, up, dn = refs[25:29]
    mid, dg, qkv, lse, x, pre, gb, dqkv, gx, gm, ga, acc, dq_tmp, in_sem, late_sem, out_sem, ff_sem = refs[29:]
    ff = dn.shape[0]
    fb = ff // FF_STEPS
    loads = weight_loads(weights, wq, pw, up, dn)
    names = ("proj", "qkv")
    loads = {k: fetch(loads[k], in_sem.at[i]) for i, k in enumerate(names)}
    late = fetch([(mid_h, mid), (qkv_h, qkv), (lse_h, lse), (x_h, x)], late_sem)
    saves = fetch(list(zip((pre, gb, dqkv, gx, g_ref), outs)), out_sem)

    def block_loads(j):
        if isinstance(j, int):
            owner, first = divmod(j * fb, ff // 2)
            rows = slice(first, first + fb)
            cols = slice(j * fb, (j + 1) * fb)
        else:
            owner, rows, cols = 0, slice(0, fb), lanes(j, fb)
        pairs = [
            (weights[6 + owner].at[rows], dn.at[cols]),
            (dg_h.at[:, cols], dg.at[:, cols]),
            (weights[4 + owner].at[:, rows], up.at[:, cols]),
        ]
        return fetch(pairs, ff_sem.at[j])

    for j in range(FF_STEPS):
        for c in block_loads(j):
            c.start()
    saves[4].start()
    for c in late:
        c.start()
    for k in ("proj", "qkv"):
        for c in loads[k]:
            c.start()
    acc[...] = jnp.zeros_like(acc)

    def mlp(j, carry):
        cols = lanes(j, fb)
        for c in block_loads(j):
            c.wait()
        value = (nt(g_ref[...], dn[cols]) * dg[:, cols].astype(F32)).astype(BF)
        pre[:, cols] = value
        sff[:, cols] = rowsum(value)
        acc[...] += nt(value, up[:, cols])
        return carry

    lax.fori_loop(0, FF_STEPS, mlp, 0)
    saves[0].start()
    late[0].wait()
    gn = acc[...]
    xhat, rstd = norm_parts(mid[...])
    grad = norm_back(xhat, rstd, gn, g2[...]) + g_ref[...].astype(F32)
    gm[...] = grad
    branch = grad.astype(BF)
    gb[...] = branch
    saves[1].start()
    sums2[...] = jnp.concatenate(
        [rowsum(gn * xhat), rowsum(gn), rowsum(branch), rowsum(g_ref[...])]
        + [jnp.zeros((4, gn.shape[1]), F32)], axis=0
    )
    for c in loads["proj"]:
        c.wait()
    ga[...] = nt(gb[...], pw[...]).astype(BF)
    late[1].wait()
    late[2].wait()

    def attend(p, carry):
        attn_bwd_pair(p, qkv, ga, lse, dqkv, sums_qkv, dq_tmp, chunk)
        return carry

    lax.fori_loop(0, lse.shape[0], attend, 0)
    saves[2].start()
    for c in loads["qkv"]:
        c.wait()
    late[3].wait()
    acc[...] = nt(dqkv[0], wq[0])

    def project(s, carry):
        acc[...] += nt(dqkv[s], wq[s])
        return carry

    lax.fori_loop(1, 3, project, 0)
    gn = acc[...]
    xhat, rstd = norm_parts(x[...].astype(F32))
    gx[...] = (norm_back(xhat, rstd, gn, g1[...]) + gm[...]).astype(BF)
    saves[3].start()
    sums1[...] = jnp.concatenate(
        [rowsum(gn * xhat), rowsum(gn), jnp.zeros((6, gn.shape[1]), F32)], axis=0
    )
    for c in saves:
        c.wait()


def backward(g, x, kept, w, chunk):
    n, d = g.shape
    ff = kept["act"].shape[1]
    vmem = pl.BlockSpec(memory_space=pltpu.VMEM)
    hbm = pl.BlockSpec(memory_space=pl.ANY)
    wide, tall = ((n, d), BF), ((n, ff), BF)
    three, flat = ((3, n, d), BF), ((n, d), F32)
    lse = (kept["lse"].shape, F32)
    dma = pltpu.SemaphoreType.DMA
    pre, gb, dqkv, gx, copy, sums2, sff, sums_qkv, sums1 = pl.pallas_call(
        functools.partial(bwd_kernel, chunk=chunk),
        in_specs=[vmem] * 3 + [hbm] * 13,
        out_specs=[hbm] * 5 + [vmem] * 4,
        out_shape=[sds(*k) for k in (tall, wide, three, wide, wide)]
        + [sds((8, d), F32), sds((1, ff), F32), sds((8, d), F32), sds((8, d), F32)],
        scratch_shapes=weight_scratch(d, ff)
        + [
            pltpu.VMEM(*k)
            for k in (flat, tall, three, lse, wide, tall, wide, three, wide, flat, wide, flat)
        ]
        + [pltpu.VMEM((2 * chunk[1], 128), F32), dma((2, 2)), dma((4,)), dma((5,)), dma((FF_STEPS, 3))],
        compiler_params=params(),
        name="bwd",
    )(
        g, w["g2"], w["g1"], kept["mid"], kept["dg"], kept["qkv"], kept["lse"], x, *weights_of(w)
    )
    return (copy, pre, gb, dqkv, sums2, sff, sums_qkv, sums1, gx)


def wgrad_mlp_kernel(act, n2, pre, g, *refs, more):
    init, outs = refs[:more], refs[more:]
    j = pl.program_id(0)
    down, up = tn(act[...], g[...]), tn(n2[...], pre[...])
    for i in range(2):

        @pl.when(j // (WGRAD_STEPS // 2) == i)
        def _():
            for at, value in ((i, down), (2 + i, up)):
                if more:
                    value = value + init[at][...].astype(F32)
                outs[at][...] = value.astype(BF)


def wgrad_mlp(kept, back, init=()):
    n, d = back["g"].shape
    ff = kept["act"].shape[1]
    fb, last = ff // WGRAD_STEPS, WGRAD_STEPS // 2 - 1
    cols = pl.BlockSpec((n, fb), lambda j: (0, j))
    at = [lambda j: jnp.minimum(j, last), lambda j: jnp.maximum(j - last - 1, 0)]
    outs = [pl.BlockSpec((fb, d), lambda j, i=i: (at[i](j), 0)) for i in range(2)]
    outs += [pl.BlockSpec((d, fb), lambda j, i=i: (0, at[i](j))) for i in range(2)]
    return pl.pallas_call(
        functools.partial(wgrad_mlp_kernel, more=len(init)),
        grid=(WGRAD_STEPS,),
        in_specs=[cols, whole((n, d)), cols, whole((n, d))] + outs[: len(init)],
        out_specs=outs,
        out_shape=[sds((ff // 2, d), BF)] * 2 + [sds((d, ff // 2), BF)] * 2,
        compiler_params=params(),
        name="wgrad_mlp",
    )(kept["act"], kept["n2"], back["pre"], back["g"], *init)


def wgrad_attn_kernel(*refs, more):
    normed, dqkv, att, gb = refs[:4]
    init = refs[4 : 4 + more]
    outs = refs[4 + more :]
    s = pl.program_id(0)
    total = tn(normed[...], dqkv[0])
    half = outs[0].shape[-1]
    for i, value in enumerate((total[:, :half], total[:, half:])):
        if more:
            value += init[i][0].astype(F32)
        outs[i][0] = value.astype(BF)
    for i in range(2):

        @pl.when(s == i)
        def _():
            value = tn(att[...], gb[...])
            if more:
                value += init[2 + i][...].astype(F32)
            outs[2 + i][...] = value.astype(BF)


def wgrad_attn(kept, back, init=()):
    n, d = kept["normed"].shape
    half = d // 2
    part = pl.BlockSpec((1, d, half), lambda s: (s, 0, 0))
    outs = [part, part, whole((half, d)), whole((half, d))]
    return pl.pallas_call(
        functools.partial(wgrad_attn_kernel, more=len(init)),
        grid=(3,),
        in_specs=[
            whole((n, d)), pl.BlockSpec((1, n, d), lambda s: (s, 0, 0)),
            pl.BlockSpec((n, half), lambda s: (0, jnp.minimum(s, 1))), whole((n, d)),
        ]
        + outs[: len(init)],
        out_specs=outs,
        out_shape=[sds((3, d, half), BF)] * 2 + [sds((half, d), BF)] * 2,
        compiler_params=params(),
        name="wgrad_attn",
    )(kept["normed"], back["dqkv"], kept["att"], back["gb"], *init)


RING = 8
VEC_ROWS = 16


def items_of(d):
    return ((0, 0, 2 * d, 1), (1, 0, d, -1), (2, 2 * d, d, -1), (2, 0, 2 * d, 1), (3, 0, d // 2, -1))


def vector_block(sums):
    s1, s2, sq, ff = sums
    d = s1.shape[1]
    wide = lambda v: [v[:, i : i + d] for i in range(0, v.shape[1], d)]
    rows = [s1[:2], s2[:4], sq[0:1], sq[2:3]] + wide(ff)
    used = 8 + ff.shape[1] // d
    return jnp.concatenate(rows + [jnp.zeros((VEC_ROWS - used, d), F32)], axis=0)


def as_own(block, fold):
    half = block.shape[1] // 2
    qv = block[6:8]
    return jnp.concatenate(
        [
            block[:6], jnp.concatenate([qv[:, half:], qv[:, :half]], axis=1),
            block[8 + fold : 8 + 2 * fold], block[8 : 8 + fold], block[8 + 2 * fold :],
        ],
        axis=0,
    )


def ring_kernel(*refs, n, items, fold):
    owns, gifts = refs[:n], refs[n : 2 * n]
    sums = refs[2 * n : 2 * n + 8]
    at = 2 * n + 8
    outs, vsum_ref = refs[at : at + n], refs[at + n]
    at += n + 1
    theirs = refs[at : at + n]
    at += n
    m = len(items)
    slots = refs[at : at + m]
    vbuf, vother, vmine, vslot, send, recv, xsend, xrecv, vsend, vrecv, vxs, vxr = refs[at + m :]
    mesh_id = pl.DeviceIdType.MESH
    me = lax.axis_index("dp")
    partner = {"tensor": 1 - lax.axis_index("tensor")}
    z, x = me // 2, me % 2
    pos = z + x * (RING - 1 - 2 * z)

    def member(p):
        p = p % RING
        return {"dp": 2 * p + (p // (RING // 2)) * (2 * RING - 1 - 4 * p)}

    barrier = pltpu.get_barrier_semaphore()
    for k in range(1, RING):
        pl.semaphore_signal(barrier, inc=1, device_id=member(pos + k), device_id_type=mesh_id)
    pl.semaphore_signal(barrier, inc=1, device_id=partner, device_id_type=mesh_id)
    pl.semaphore_wait(barrier, RING)

    def part(arrays, a, chunk):
        i, first, rows, _ = items[a]
        rows = rows // RING
        return arrays[i].at[pl.ds(pl.multiple_of(first + (chunk % RING) * rows, rows), rows)]

    def chunk_at(a, step):
        return pos + 2 * RING - items[a][3] * step

    def exchange(a, step):
        return pltpu.make_async_remote_copy(
            src_ref=part(gifts, a, chunk_at(a, step)),
            dst_ref=part(theirs, a, chunk_at(a, step)),
            send_sem=xsend.at[a, step],
            recv_sem=xrecv.at[a, step],
            device_id=partner,
            device_id_type=mesh_id,
        )

    def mine(a, step):
        exchange(a, step).wait_recv()
        chunk = chunk_at(a, step)
        return part(owns, a, chunk)[...].astype(F32) + part(theirs, a, chunk)[...].astype(F32)

    def remote(src, dst, a, step):
        return pltpu.make_async_remote_copy(
            src_ref=src,
            dst_ref=dst,
            send_sem=send.at[a, step],
            recv_sem=recv.at[a, step],
            device_id=member(pos + items[a][3] + RING),
            device_id_type=mesh_id,
        )

    def vcopy(k):
        return pltpu.make_async_remote_copy(
            src_ref=vmine,
            dst_ref=vslot.at[k - 1],
            send_sem=vsend.at[k - 1],
            recv_sem=vrecv.at[k - 1],
            device_id=member(pos + k),
            device_id_type=mesh_id,
        )

    vexchange = pltpu.make_async_remote_copy(
        src_ref=vbuf, dst_ref=vother, send_sem=vxs, recv_sem=vxr,
        device_id=partner, device_id_type=mesh_id,
    )

    for step in range(2):
        for a in range(m):
            exchange(a, step).start()
    vbuf[...] = vector_block([sums[i][...] + sums[4 + i][...] for i in range(4)])
    vexchange.start()
    for a in range(m):
        slots[a][0] = mine(a, 0).astype(BF)
        remote(slots[a].at[0], slots[a].at[1], a, 0).start()

    def scatter(s, carry):
        for a in range(m):
            exchange(a, s + 1).start()
        for a in range(m):
            here = slots[a].at[s]
            own = mine(a, s)
            remote(here, here, a, s - 1).wait_recv()
            here[...] = (here[...].astype(F32) + own).astype(BF)
            remote(here, slots[a].at[s + 1], a, s).start()
        return carry

    lax.fori_loop(1, RING - 1, scatter, 0)
    vexchange.wait()
    vmine[...] = vbuf[...] + as_own(vother[...], fold)
    for k in range(1, RING):
        vcopy(k).start()
    for a in range(m):
        last = slots[a].at[RING - 1]
        own = mine(a, RING - 1)
        remote(last, last, a, RING - 2).wait_recv()
        done = part(outs, a, chunk_at(a, RING - 1))
        done[...] = (last[...].astype(F32) + own).astype(BF)
        remote(done, done, a, RING - 1).start()

    def gather(t, carry):
        for a in range(m):
            here = part(outs, a, chunk_at(a, t - 1))
            remote(here, here, a, RING - 2 + t).wait_recv()
            remote(here, here, a, RING - 1 + t).start()
        return carry

    lax.fori_loop(1, RING - 1, gather, 0)
    total = vmine[...]
    for k in range(1, RING):
        vcopy(k).wait()
        total += vslot[k - 1]
    vsum_ref[...] = total
    for a in range(m):
        here = part(outs, a, chunk_at(a, RING - 2))
        remote(here, here, a, 2 * RING - 3).wait_recv()
    for a in range(m):
        for s in range(RING - 1):
            remote(slots[a].at[0], slots[a].at[0], a, s).wait_send()
            here = part(outs, a, pos)
            remote(here, here, a, RING - 1 + s).wait_send()
        for s in range(RING):
            exchange(a, s).wait_send()


def ring(owns, gifts, sums_s, sums_l):
    n = len(owns)
    d = owns[0].shape[1]
    items = items_of(d)
    m = len(items)
    vmem = pl.BlockSpec(memory_space=pltpu.VMEM)
    dma = pltpu.SemaphoreType.DMA
    vec = pltpu.VMEM((VEC_ROWS, d), F32)
    out = pl.pallas_call(
        functools.partial(ring_kernel, n=n, items=items, fold=sums_s[3].shape[1] // (2 * d)),
        in_specs=[vmem] * (2 * n + 8),
        out_specs=[vmem] * (n + 1),
        out_shape=[sds(a.shape, BF) for a in owns] + [sds((VEC_ROWS, d), F32)],
        scratch_shapes=[pltpu.VMEM(a.shape, BF) for a in owns]
        + [pltpu.VMEM((RING, rows // RING, owns[i].shape[1]), BF) for i, _, rows, _ in items]
        + [
            vec, vec, vec, pltpu.VMEM((RING - 1, VEC_ROWS, d), F32),
            dma((m, 2 * RING - 2)), dma((m, 2 * RING - 2)), dma((m, RING)), dma((m, RING)),
            dma((RING - 1,)), dma((RING - 1,)), dma, dma,
        ],
        compiler_params=params(collective_id=1, has_side_effects=True),
        name="ring",
    )(*owns, *gifts, *sums_s, *sums_l)
    return out[:n], out[n]


def dp_sum(owns, gifts, sums_s, sums_l):
    if lax.axis_size("dp") == RING:
        return ring(owns, gifts, sums_s, sums_l)
    other = lambda array: lax.ppermute(array, "tensor", [(0, 1), (1, 0)])
    fold = sums_s[3].shape[1] // (2 * owns[0].shape[1])
    block = vector_block([a + b for a, b in zip(sums_s, sums_l)])
    summed = [lax.psum(a + other(b), "dp") for a, b in zip(owns, gifts)]
    return summed, lax.psum(block + as_own(other(block), fold), "dp")


def finish_kernel(*refs, fold):
    grads, vec, outs = refs[:4], refs[4], refs[5:]
    for g, out in zip(grads, outs):
        out[0] = g[...].astype(F32)

    @pl.when(pl.program_id(0) == 0)
    def _():
        half = vec.shape[1] // 2
        for i in range(6):
            outs[4 + i][...] = vec[i : i + 1]
        outs[10][0] = vec[6:8, :half]
        outs[11][...] = jnp.concatenate([vec[8 + i : 9 + i] for i in range(fold)], axis=1)


def finish(grads, vec):
    d = vec.shape[1]
    fold = grads[1].shape[1] // d
    steps = 8
    rows_in = lambda a: pl.BlockSpec((a.shape[0] // steps, a.shape[1]), lambda j: (j, 0))
    rows_out = lambda a: pl.BlockSpec((1, a.shape[0] // steps, a.shape[1]), lambda j: (0, j, 0))
    small = [(1, d)] * 6 + [(1, 2, d // 2), (1, fold * d)]
    return pl.pallas_call(
        functools.partial(finish_kernel, fold=fold),
        grid=(steps,),
        in_specs=[rows_in(a) for a in grads] + [whole(vec.shape)],
        out_specs=[rows_out(a) for a in grads] + [whole(a) for a in small],
        out_shape=[sds((1,) + a.shape, F32) for a in grads] + [sds(a, F32) for a in small],
        compiler_params=params(),
        name="finish",
    )(*grads, vec)


def starts_of(place):
    slots = [j + (j >= place) for j in range(SMALL_MB)]
    return [place * LEN_SMALL] + [
        slot * LEN_SMALL + (LEN_LARGE - LEN_SMALL) * (slot > place) for slot in slots
    ]


def layout(place):
    at = 0
    starts = starts_of(place)
    for c, (nimg, plen, vlen) in enumerate(CHUNKS):
        for i in range(nimg):
            yield starts[at], c, i * plen, plen, vlen
            at += 1


def cut_kernel(meta_ref, x_ref, *refs):
    outs, flat = refs[:-1], refs[-1]
    rows = x_ref.shape[0]
    flat[:rows] = x_ref[...].astype(F32)
    flat[rows:] = jnp.zeros((flat.shape[0] - rows, flat.shape[1]), F32)
    for place in range(SMALL_MB + 1):

        @pl.when(meta_ref[1 + meta_ref[0]] == place)
        def _():
            for start, c, r0, plen, vlen in layout(place):
                value = flat[start : start + plen]
                row = lax.broadcasted_iota(jnp.int32, value.shape, 0)
                outs[c][r0 : r0 + plen] = jnp.where(row < vlen, value, 0.0).astype(BF)


def cut(array, meta):
    rows = LEN_LARGE + SMALL_MB * LEN_SMALL
    d = array.shape[1]
    block = d // 3
    return pl.pallas_call(
        cut_kernel,
        grid_spec=pltpu.PrefetchScalarGridSpec(
            num_scalar_prefetch=1,
            grid=(3,),
            in_specs=[pl.BlockSpec((rows, block), lambda j, m: (m[0], j))],
            out_specs=[pl.BlockSpec((k * p, block), lambda j, m: (0, j)) for k, p, _ in CHUNKS],
            scratch_shapes=[pltpu.VMEM((rows + 16, block), F32)],
        ),
        out_shape=[sds((k * p, d), BF) for k, p, _ in CHUNKS],
        compiler_params=params(),
        name="cut",
    )(meta, array)


def join_kernel(meta_ref, *refs):
    count = len(CHUNKS)
    mine, theirs, out_ref, flat = refs[:count], refs[count : 2 * count], refs[-2], refs[-1]
    rows = flat.shape[0]
    for lane in range(2):
        here = meta_ref[0] == lane
        for place in range(SMALL_MB + 1):

            @pl.when(meta_ref[1 + lane] == place)
            def _():
                for start, c, r0, plen, vlen in layout(place):
                    own = mine[c][r0 : r0 + plen].astype(F32)
                    value = jnp.where(here, own, theirs[c][r0 : r0 + plen].astype(F32))
                    flat[start : start + vlen] = value[:vlen]

        out_ref[lane * rows : (lane + 1) * rows] = flat[...].astype(BF)


def join(mine, theirs, meta):
    rows = LEN_LARGE + SMALL_MB * LEN_SMALL
    d = mine[0].shape[1]
    block = d // 3
    return pl.pallas_call(
        join_kernel,
        grid_spec=pltpu.PrefetchScalarGridSpec(
            num_scalar_prefetch=1,
            grid=(3,),
            in_specs=[pl.BlockSpec((k * p, block), lambda j, m: (0, j)) for k, p, _ in CHUNKS] * 2,
            out_specs=pl.BlockSpec((2 * rows, block), lambda j, m: (0, j)),
            scratch_shapes=[pltpu.VMEM((rows, block), F32)],
        ),
        out_shape=sds((2 * rows, d), BF),
        compiler_params=params(),
        name="join",
    )(meta, *mine, *theirs)


def blank_kernel(*refs):
    pass


def blank(like):
    shapes = [sds(a.shape, a.dtype) for a in like]
    return tuple(
        pl.pallas_call(
            blank_kernel,
            out_shape=shapes,
            out_specs=[pl.BlockSpec(memory_space=pl.ANY) for _ in shapes],
            name="blank",
        )()
    )


KEPT = ("normed", "qkv", "att", "lse", "mid", "n2", "act", "dg", "out")
BACK = ("g", "pre", "gb", "dqkv", "sums2", "sff", "sums_qkv", "sums1", "gx")


def after(value, *earlier):
    return lax.optimization_barrier((value, earlier))[0]


def body(
    patches, out_grad, large_place, norm1_gain, norm1_bias, qkv_weight, qv_bias, proj_weight,
    proj_bias, norm2_gain, norm2_bias, up_weight, up_bias, down_weight, down_bias,
):
    d = patches.shape[1]
    half = qkv_weight.shape[-1]
    section = lax.axis_index("section")
    lane = lax.axis_index("tensor")
    both = [(0, 1), (1, 0)]
    other = lambda array: lax.ppermute(array, "tensor", both)

    wqkv, pw, up, dn = qkv_weight[0], proj_weight[0], up_weight[0], down_weight[0]
    meta = jnp.concatenate([lane[None], large_place])
    xs = cut(patches, meta)
    w = {
        "g1": norm1_gain, "b1": norm1_bias, "g2": norm2_gain, "b2": norm2_bias,
        "pb": proj_bias, "db": down_bias,
        "wqkv_o": wqkv, "wqkv_p": other(wqkv), "pw_o": pw, "pw_p": other(pw),
        "up_o": up, "up_p": other(up), "dn_o": dn, "dn_p": other(dn),
        "bq_o": qv_bias[0], "bq_p": other(qv_bias[0]), "ub_o": up_bias, "ub_p": other(up_bias),
    }


    large, smalls = 0, 1
    gs = cut(out_grad, meta)

    def pick(on, make, otherwise=None):
        like = jax.eval_shape(make)
        return lax.cond(
            section == on,
            lambda: tuple(make()),
            lambda: blank(like) if otherwise is None else tuple(otherwise),
        )

    def fwd(c, on, x, otherwise=None):
        return pick(on, lambda: forward(x, w, CHUNKS[c]), otherwise)

    def bwd(c, on, g, x, kept, otherwise=None):
        kept = dict(zip(KEPT, kept))
        return pick(on, lambda: backward(g, x, kept, w, CHUNKS[c]), otherwise)

    down = lambda array: lax.ppermute(array, "section", [(0, 1)])
    up_ = lambda array: lax.ppermute(array, "section", [(1, 0)])

    kept_s = fwd(smalls, 0, xs[smalls])
    in_s = down(kept_s[-1])
    x_l = after(xs[large], kept_s[-1])
    kept_l = fwd(large, 0, x_l)
    in_l = down(kept_l[-1])
    in_s = after(in_s, kept_l[-1])
    kept_s = fwd(smalls, 1, in_s, kept_s)
    back_s = bwd(smalls, 1, gs[smalls], in_s, kept_s)
    sent_s = up_(back_s[-1])
    in_l = after(in_l, back_s[-1])
    kept_l = fwd(large, 1, in_l, kept_l)
    back_l = bwd(large, 1, gs[large], in_l, kept_l)
    sent_l = up_(back_l[-1])
    back_s = bwd(smalls, 0, after(sent_s, back_l[-1]), xs[smalls], kept_s, back_s)
    named = lambda names, values: dict(zip(names, values))
    part_mlp = wgrad_mlp(named(KEPT, kept_s), named(BACK, back_s))
    part_attn = wgrad_attn(named(KEPT, kept_s), named(BACK, back_s))
    outs = [kept_l[-1], kept_s[-1]]
    outputs = join(outs, [other(a) for a in outs], meta)
    sent_l = after(sent_l, part_mlp, part_attn, outputs)
    back_l = bwd(large, 0, sent_l, xs[large], kept_l, back_l)
    dn_o, dn_p, up_o, up_p = wgrad_mlp(named(KEPT, kept_l), named(BACK, back_l), part_mlp)
    qkv_o, qkv_p, pw_o, pw_p = wgrad_attn(named(KEPT, kept_l), named(BACK, back_l), part_attn)
    grads = [back_l[-1], back_s[-1]]
    input_grads = join(grads, [other(a) for a in grads], meta)

    rows = lambda qkv: qkv.reshape(3 * d, half)
    sums = lambda back: [named(BACK, back)[k] for k in ("sums1", "sums2", "sums_qkv", "sff")]
    summed, vec = dp_sum(
        [dn_o, up_o, rows(qkv_o), pw_o], [dn_p, up_p, rows(qkv_p), pw_p], sums(back_s), sums(back_l)
    )
    g_dn, g_up, g_qkv, g_pw, g1, b1, g2, b2, pb, db, qv, ub = finish(summed, vec)
    return (
        outputs[None], input_grads[None], g1, b1, g_qkv.reshape(1, 3, d, half), qv, g_pw, pb,
        g2, b2, g_up, ub, g_dn, db,
    )


def solution(mesh):
    placed = (
        P("dp", None), P("dp", None), P("dp"), P("section", None), P("section", None),
        P("section", None, None, "tensor"), P("section", None, "tensor"),
        P("section", "tensor", None), P("section", None), P("section", None),
        P("section", None), P("section", None, "tensor"), P("section", "tensor"),
        P("section", "tensor", None), P("section", None),
    )
    return jax.shard_map(
        body,
        mesh=mesh,
        in_specs=placed,
        out_specs=(
            P("section", "dp", None), P("section", "dp", None), P("section", None),
            P("section", None), P("section", None, None, "tensor"), P("section", None, "tensor"),
            P("section", "tensor", None), P("section", None), P("section", None),
            P("section", None), P("section", None, "tensor"), P("section", "tensor"),
            P("section", "tensor", None), P("section", None),
        ),
        check_vma=False,
    )
```

```python
import functools

import jax
import jax.numpy as jnp
from jax import lax
from jax.experimental import pallas as pl
from jax.experimental.pallas import tpu as pltpu
from jax.sharding import PartitionSpec as P

HD = 64
LEN_SMALL = 197
LEN_LARGE = 577
SMALL_MB = 3
EPSILON = 1e-06
MASKED = -1e30
SCALE = HD ** (-0.5)
SCALE2 = SCALE * 1.4426950408889634
BF = jnp.bfloat16
F32 = jnp.float32
VMEM_LIMIT = 56 * 1024 * 1024
CHUNKS = ((1, 592, LEN_LARGE), (SMALL_MB, 208, LEN_SMALL))


def params(limit=VMEM_LIMIT, **more):
    return pltpu.CompilerParams(vmem_limit_bytes=limit, **more)


def nn(a, b):
    return jnp.dot(a, b, preferred_element_type=F32)


def nt(a, b):
    return lax.dot_general(a, b, (((1,), (1,)), ((), ())), preferred_element_type=F32)


def tn(a, b):
    return lax.dot_general(a, b, (((0,), (0,)), ((), ())), preferred_element_type=F32)


def whole(shape):
    zeros = (0,) * len(shape)
    return pl.BlockSpec(shape, lambda *_: zeros)


def sds(shape, dtype):
    return jax.ShapeDtypeStruct(shape, dtype)


def norm_parts(values):
    mean = jnp.mean(values, axis=-1, keepdims=True)
    centred = values - mean
    rstd = lax.rsqrt(jnp.mean(centred * centred, axis=-1, keepdims=True) + EPSILON)
    return centred * rstd, rstd


def norm_back(xhat, rstd, grad, gain):
    scaled = grad * gain
    m1 = jnp.mean(scaled, axis=-1, keepdims=True)
    m2 = jnp.mean(scaled * xhat, axis=-1, keepdims=True)
    return rstd * (scaled - m1 - xhat * m2)


def rowsum(values):
    return jnp.sum(values.astype(F32), axis=0, keepdims=True)


def fetch(pairs, sems):
    return [pltpu.make_async_copy(src, dst, sems.at[i]) for i, (src, dst) in enumerate(pairs)]


def weight_loads(w, wq, pw, up, dn):
    wqo, wqp, pwo, pwp, upo, upp, dno, dnp = w
    half, fh = wqo.shape[-1], dno.shape[0]
    return {
        "qkv": [(wqo, wq.at[:, :, :half]), (wqp, wq.at[:, :, half:])],
        "proj": [(pwo, pw.at[:half]), (pwp, pw.at[half:])],
        "up": [(upo, up.at[:, :fh]), (upp, up.at[:, fh:])],
        "down": [(dno, dn.at[:fh]), (dnp, dn.at[fh:])],
    }


def weights_of(w):
    return [w[k] for k in ("wqkv_o", "wqkv_p", "pw_o", "pw_p", "up_o", "up_p", "dn_o", "dn_p")]


def weight_scratch(d, ff):
    return [
        pltpu.VMEM((3, d, d), BF), pltpu.VMEM((d, d), BF), pltpu.VMEM((d, ff), BF),
        pltpu.VMEM((ff, d), BF),
    ]


def lanes(at, width):
    return pl.ds(pl.multiple_of(at * width, width), width)


def mask_keys(scores, vlen):
    rows = scores.shape[0]
    keep = vlen // 8 * 8
    tail = scores[keep:]
    idx = lax.broadcasted_iota(jnp.int32, tail.shape, 0) + keep
    return jnp.concatenate([scores[:keep], jnp.where(idx < vlen, tail, MASKED)], axis=0)


def qblocks(plen):
    step = min(256, plen)
    return [(q, min(step, 2 * plen - q)) for q in range(0, 2 * plen, step)]


def lse_width(chunk):
    nimg, plen, _ = chunk
    return nimg * len(qblocks(plen)) * 256


def both_heads(rows):
    head = lax.broadcasted_iota(jnp.int32, rows.shape, 1) // HD
    none = jnp.zeros_like(rows)
    return jnp.concatenate([jnp.where(head == h, rows, none) for h in range(2)], axis=0)


def one_each(stacked, plen):
    head = lax.broadcasted_iota(jnp.int32, (plen, stacked.shape[1]), 1) // HD
    return jnp.where(head == 0, stacked[:plen], stacked[plen:])


def blocks_of(chunk):
    nimg, plen, _ = chunk
    return [(im, q0, qw) for im in range(nimg) for q0, qw in qblocks(plen)]


def attn_fwd_pair(p, qkv, att, lse, o_tmp, chunk):
    nimg, plen, vlen = chunk
    cols = lanes(p, 128)
    images = [slice(im * plen, (im + 1) * plen) for im in range(nimg)]
    k = [qkv[1, rows, cols] for rows in images]
    vt = [qkv[2, rows, cols].T for rows in images]
    queries = [both_heads(qkv[0, rows, cols]) for rows in images]
    blocks = blocks_of(chunk)
    scores = lambda im, q0, qw: nt(k[im], queries[im][q0 : q0 + qw])
    coming = scores(*blocks[0])
    for i, (im, q0, qw) in enumerate(blocks):
        st = mask_keys(coming, vlen)
        if i + 1 < len(blocks):
            coming = scores(*blocks[i + 1])
        top = jnp.max(st, axis=0, keepdims=True)
        e = jnp.exp2((st - top) * SCALE2)
        total = jnp.sum(e, axis=0, keepdims=True)
        o_tmp[q0 : q0 + qw] = (nn(vt[im], e.astype(BF)) * (1.0 / total)).T
        lse[p, :, i * 256 : i * 256 + qw] = top * SCALE2 + jnp.log2(total)
        if q0 + qw == 2 * plen:
            att[images[im], cols] = one_each(o_tmp, plen).astype(BF)


def gelu_parts(x):
    cdf = 0.5 + 0.5 * lax.erf(x * (2.0**-0.5))
    pdf = jnp.exp(-0.5 * x * x) * 0.3989422804014327
    return x * cdf, cdf + x * pdf


FF_STEPS = 2
WGRAD_STEPS = 4


def fwd_kernel(*refs, chunk):
    x_ref, g1, b1, own_bias, other_bias, pb, g2, b2, db = refs[:9]
    weights, outs = refs[9:17], refs[17:26]
    wq, pw, up, dn = refs[26:30]
    held = refs[30:39]
    acc, o_tmp, ub, in_sem, out_sem, ff_sem = refs[39:]
    normed, qkv, att, lse, mid, n2, act, dg, out = held
    ff = dn.shape[0]
    fb = ff // FF_STEPS
    loads = weight_loads(weights, wq, pw, up, dn)
    names = ("qkv", "proj", "up", "down")
    loads = {k: fetch(loads[k], in_sem.at[i]) for i, k in enumerate(names)}
    saves = fetch(list(zip(held[:6] + held[8:], outs[:6] + outs[8:])), out_sem)
    for c in loads["qkv"]:
        c.start()
    xhat, _ = norm_parts(x_ref[...].astype(F32))
    normed[...] = (xhat * g1[...] + b1[...]).astype(BF)
    saves[0].start()
    half = wq.shape[1] // 2

    def bias_of(first, last):
        return jnp.concatenate([own_bias[:, first:last], other_bias[:, first:last]], axis=1)

    q_bias, v_bias = bias_of(0, half), bias_of(half, 2 * half)
    ub[...] = bias_of(2 * half, own_bias.shape[1])
    for c in loads["qkv"]:
        c.wait()
    for k in names[1:]:
        for c in loads[k]:
            c.start()

    def project(s, carry):
        bias = jnp.where(s == 0, q_bias, jnp.where(s == 1, 0.0, v_bias))
        qkv[s] = (nn(normed[...], wq[s]) + bias).astype(BF)
        return carry

    lax.fori_loop(0, 3, project, 0)
    saves[1].start()

    def attend(p, carry):
        attn_fwd_pair(p, qkv, att, lse, o_tmp, chunk)
        return carry

    lax.fori_loop(0, lse.shape[0], attend, 0)
    saves[2].start()
    saves[3].start()
    for c in loads["proj"]:
        c.wait()
    middle = x_ref[...].astype(F32) + (nn(att[...], pw[...]) + pb[...])
    mid[...] = middle
    saves[4].start()
    xhat, _ = norm_parts(middle)
    n2[...] = (xhat * g2[...] + b2[...]).astype(BF)
    saves[5].start()
    acc[...] = middle + db[...]
    for k in ("up", "down"):
        for c in loads[k]:
            c.wait()

    def block_saves(j):
        cols = lanes(j, fb)
        pairs = [(act.at[:, cols], outs[6].at[:, cols]), (dg.at[:, cols], outs[7].at[:, cols])]
        return fetch(pairs, ff_sem.at[j])

    def mlp(j, carry):
        cols = lanes(j, fb)
        value, slope = gelu_parts(nn(n2[...], up[:, cols]) + ub[:, cols])
        value = value.astype(BF)
        act[:, cols] = value
        dg[:, cols] = slope.astype(BF)
        for c in block_saves(j):
            c.start()
        acc[...] += nn(value, dn[cols])
        return carry

    lax.fori_loop(0, FF_STEPS, mlp, 0)
    out[...] = acc[...].astype(BF)
    saves[6].start()
    for c in saves:
        c.wait()
    for j in range(FF_STEPS):
        for c in block_saves(j):
            c.wait()


def forward(x, w, chunk):
    n, d = x.shape
    ff = 2 * w["dn_o"].shape[0]
    pairs = d // 128
    kept = [
        ((n, d), BF), ((3, n, d), BF), ((n, d), BF), ((pairs, 1, lse_width(chunk)), F32),
        ((n, d), F32), ((n, d), BF), ((n, ff), BF), ((n, ff), BF), ((n, d), BF),
    ]
    vmem = pl.BlockSpec(memory_space=pltpu.VMEM)
    hbm = pl.BlockSpec(memory_space=pl.ANY)
    return pl.pallas_call(
        functools.partial(fwd_kernel, chunk=chunk),
        in_specs=[vmem] * 9 + [hbm] * 8,
        out_specs=[hbm] * len(kept),
        out_shape=[sds(*k) for k in kept],
        scratch_shapes=weight_scratch(d, ff)
        + [pltpu.VMEM(*k) for k in kept]
        + [
            pltpu.VMEM((n, d), F32), pltpu.VMEM((2 * chunk[1], 128), F32),
            pltpu.VMEM((1, ff), F32), pltpu.SemaphoreType.DMA((4, 2)),
            pltpu.SemaphoreType.DMA((7,)), pltpu.SemaphoreType.DMA((FF_STEPS, 2)),
        ],
        compiler_params=params(),
        name="fwd",
    )(
        x, w["g1"], w["b1"], w["bias_o"], w["bias_p"], w["pb"], w["g2"], w["b2"], w["db"],
        *weights_of(w),
    )


def attn_bwd_pair(p, qkv, att, gatt, lse, dqkv, sums, dq_tmp, chunk):
    nimg, plen, vlen = chunk
    cols = lanes(p, 128)
    images = [slice(im * plen, (im + 1) * plen) for im in range(nimg)]
    k = [qkv[1, rows, cols] for rows in images]
    v = [qkv[2, rows, cols] for rows in images]
    queries = [both_heads(qkv[0, rows, cols]) for rows in images]
    grads = [both_heads(gatt[rows, cols]) for rows in images]
    blocks = blocks_of(chunk)

    def scores(im, q0, qw):
        return nt(k[im], queries[im][q0 : q0 + qw]), nt(v[im], grads[im][q0 : q0 + qw])

    total_q, total_v = jnp.zeros((1, 128), F32), jnp.zeros((1, 128), F32)
    coming = scores(*blocks[0])
    for i, (im, q0, qw) in enumerate(blocks):
        rows = images[im]
        if q0 == 0:
            kt = k[im].T
            products = both_heads(gatt[rows, cols].astype(F32) * att[rows, cols].astype(F32))
            dk = jnp.zeros((plen, 128), F32)
            dv = jnp.zeros((plen, 128), F32)
        q = queries[im][q0 : q0 + qw]
        ga = grads[im][q0 : q0 + qw]
        st, gp = mask_keys(coming[0], vlen), coming[1]
        if i + 1 < len(blocks):
            coming = scores(*blocks[i + 1])
        pr = jnp.exp2(st * SCALE2 - lse[p, :, i * 256 : i * 256 + qw])
        dv += nn(pr.astype(BF), ga)
        delta = jnp.sum(products[q0 : q0 + qw].T, axis=0, keepdims=True)
        ds = (pr * (gp - delta)).astype(BF)
        dk += nn(ds, q)
        dq_tmp[q0 : q0 + qw] = nn(kt, ds).T
        if q0 + qw == 2 * plen:
            dq = (one_each(dq_tmp, plen) * SCALE).astype(BF)
            dvb = dv.astype(BF)
            dqkv[0, rows, cols] = dq
            dqkv[1, rows, cols] = (dk * SCALE).astype(BF)
            dqkv[2, rows, cols] = dvb
            total_q += rowsum(dq)
            total_v += rowsum(dvb)
    sums[:, cols] = jnp.concatenate(
        [total_q, jnp.zeros_like(total_q), total_v, jnp.zeros((5, 128), F32)], axis=0
    )


def bwd_kernel(*refs, chunk):
    g_ref, g2, g1 = refs[:3]
    mid_h, dg_h, qkv_h, lse_h, x_h, att_h = refs[3:9]
    weights, outs = refs[9:17], refs[17:22]
    sums2, sff, sums_qkv, sums1 = refs[22:26]
    wq, pw, up, dn = refs[26:30]
    mid, dg, qkv, lse, x, att, pre, gb, dqkv, gx, gm, ga, acc, dq_tmp, in_sem, late_sem, out_sem, ff_sem = refs[30:]
    ff = dn.shape[0]
    fb = ff // FF_STEPS
    loads = weight_loads(weights, wq, pw, up, dn)
    names = ("proj", "qkv")
    loads = {k: fetch(loads[k], in_sem.at[i]) for i, k in enumerate(names)}
    late = fetch([(mid_h, mid), (qkv_h, qkv), (lse_h, lse), (att_h, att), (x_h, x)], late_sem)
    saves = fetch(list(zip((pre, gb, dqkv, gx, g_ref), outs)), out_sem)

    def block_loads(j):
        if isinstance(j, int):
            owner, first = divmod(j * fb, ff // 2)
            rows = slice(first, first + fb)
            cols = slice(j * fb, (j + 1) * fb)
        else:
            owner, rows, cols = 0, slice(0, fb), lanes(j, fb)
        pairs = [
            (weights[6 + owner].at[rows], dn.at[cols]),
            (dg_h.at[:, cols], dg.at[:, cols]),
            (weights[4 + owner].at[:, rows], up.at[:, cols]),
        ]
        return fetch(pairs, ff_sem.at[j])

    for j in range(FF_STEPS):
        for c in block_loads(j):
            c.start()
    saves[4].start()
    for c in late:
        c.start()
    for k in ("proj", "qkv"):
        for c in loads[k]:
            c.start()
    acc[...] = jnp.zeros_like(acc)

    def mlp(j, carry):
        cols = lanes(j, fb)
        for c in block_loads(j):
            c.wait()
        value = (nt(g_ref[...], dn[cols]) * dg[:, cols].astype(F32)).astype(BF)
        pre[:, cols] = value
        sff[:, cols] = rowsum(value)
        acc[...] += nt(value, up[:, cols])
        return carry

    lax.fori_loop(0, FF_STEPS, mlp, 0)
    saves[0].start()
    late[0].wait()
    gn = acc[...]
    xhat, rstd = norm_parts(mid[...])
    grad = norm_back(xhat, rstd, gn, g2[...]) + g_ref[...].astype(F32)
    gm[...] = grad
    branch = grad.astype(BF)
    gb[...] = branch
    saves[1].start()
    sums2[...] = jnp.concatenate(
        [rowsum(gn * xhat), rowsum(gn), rowsum(branch), rowsum(g_ref[...])]
        + [jnp.zeros((4, gn.shape[1]), F32)], axis=0
    )
    for c in loads["proj"]:
        c.wait()
    ga[...] = nt(gb[...], pw[...]).astype(BF)
    for c in late[1:4]:
        c.wait()

    def attend(p, carry):
        attn_bwd_pair(p, qkv, att, ga, lse, dqkv, sums_qkv, dq_tmp, chunk)
        return carry

    lax.fori_loop(0, lse.shape[0], attend, 0)
    saves[2].start()
    for c in loads["qkv"]:
        c.wait()
    late[4].wait()
    acc[...] = nt(dqkv[0], wq[0])

    def project(s, carry):
        acc[...] += nt(dqkv[s], wq[s])
        return carry

    lax.fori_loop(1, 3, project, 0)
    gn = acc[...]
    xhat, rstd = norm_parts(x[...].astype(F32))
    gx[...] = (norm_back(xhat, rstd, gn, g1[...]) + gm[...]).astype(BF)
    saves[3].start()
    sums1[...] = jnp.concatenate(
        [rowsum(gn * xhat), rowsum(gn), jnp.zeros((6, gn.shape[1]), F32)], axis=0
    )
    for c in saves:
        c.wait()


def backward(g, x, kept, w, chunk):
    n, d = g.shape
    ff = kept["act"].shape[1]
    vmem = pl.BlockSpec(memory_space=pltpu.VMEM)
    hbm = pl.BlockSpec(memory_space=pl.ANY)
    wide, tall = ((n, d), BF), ((n, ff), BF)
    three, flat = ((3, n, d), BF), ((n, d), F32)
    lse = (kept["lse"].shape, F32)
    dma = pltpu.SemaphoreType.DMA
    pre, gb, dqkv, gx, copy, sums2, sff, sums_qkv, sums1 = pl.pallas_call(
        functools.partial(bwd_kernel, chunk=chunk),
        in_specs=[vmem] * 3 + [hbm] * 14,
        out_specs=[hbm] * 5 + [vmem] * 4,
        out_shape=[sds(*k) for k in (tall, wide, three, wide, wide)]
        + [sds((8, d), F32), sds((1, ff), F32), sds((8, d), F32), sds((8, d), F32)],
        scratch_shapes=weight_scratch(d, ff)
        + [
            pltpu.VMEM(*k)
            for k in (flat, tall, three, lse, wide, wide, tall, wide, three, wide, flat, wide, flat)
        ]
        + [pltpu.VMEM((2 * chunk[1], 128), F32), dma((2, 2)), dma((5,)), dma((5,)), dma((FF_STEPS, 3))],
        compiler_params=params(),
        name="bwd",
    )(
        g, w["g2"], w["g1"], kept["mid"], kept["dg"], kept["qkv"], kept["lse"], x, kept["att"], *weights_of(w)
    )
    return (copy, pre, gb, dqkv, sums2, sff, sums_qkv, sums1, gx)


def wgrad_mlp_kernel(act, n2, pre, g, *refs, more):
    init, outs = refs[:more], refs[more:]
    j = pl.program_id(0)
    down, up = tn(act[...], g[...]), tn(n2[...], pre[...])
    for i in range(2):

        @pl.when(j // (WGRAD_STEPS // 2) == i)
        def _():
            for at, value in ((i, down), (2 + i, up)):
                if more:
                    value = value + init[at][...].astype(F32)
                outs[at][...] = value.astype(BF)


def wgrad_mlp(kept, back, init=()):
    n, d = back["g"].shape
    ff = kept["act"].shape[1]
    fb, last = ff // WGRAD_STEPS, WGRAD_STEPS // 2 - 1
    cols = pl.BlockSpec((n, fb), lambda j: (0, j))
    at = [lambda j: jnp.minimum(j, last), lambda j: jnp.maximum(j - last - 1, 0)]
    outs = [pl.BlockSpec((fb, d), lambda j, i=i: (at[i](j), 0)) for i in range(2)]
    outs += [pl.BlockSpec((d, fb), lambda j, i=i: (0, at[i](j))) for i in range(2)]
    return pl.pallas_call(
        functools.partial(wgrad_mlp_kernel, more=len(init)),
        grid=(WGRAD_STEPS,),
        in_specs=[cols, whole((n, d)), cols, whole((n, d))] + outs[: len(init)],
        out_specs=outs,
        out_shape=[sds((ff // 2, d), BF)] * 2 + [sds((d, ff // 2), BF)] * 2,
        compiler_params=params(),
        name="wgrad_mlp",
    )(kept["act"], kept["n2"], back["pre"], back["g"], *init)


def wgrad_attn_kernel(*refs, more):
    normed, dqkv, att, gb = refs[:4]
    init = refs[4 : 4 + more]
    outs = refs[4 + more :]
    s = pl.program_id(0)
    total = tn(normed[...], dqkv[0])
    half = outs[0].shape[-1]
    for i, value in enumerate((total[:, :half], total[:, half:])):
        if more:
            value += init[i][0].astype(F32)
        outs[i][0] = value.astype(BF)
    for i in range(2):

        @pl.when(s == i)
        def _():
            value = tn(att[...], gb[...])
            if more:
                value += init[2 + i][...].astype(F32)
            outs[2 + i][...] = value.astype(BF)


def wgrad_attn(kept, back, init=()):
    n, d = kept["normed"].shape
    half = d // 2
    part = pl.BlockSpec((1, d, half), lambda s: (s, 0, 0))
    outs = [part, part, whole((half, d)), whole((half, d))]
    return pl.pallas_call(
        functools.partial(wgrad_attn_kernel, more=len(init)),
        grid=(3,),
        in_specs=[
            whole((n, d)), pl.BlockSpec((1, n, d), lambda s: (s, 0, 0)),
            pl.BlockSpec((n, half), lambda s: (0, jnp.minimum(s, 1))), whole((n, d)),
        ]
        + outs[: len(init)],
        out_specs=outs,
        out_shape=[sds((3, d, half), BF)] * 2 + [sds((half, d), BF)] * 2,
        compiler_params=params(),
        name="wgrad_attn",
    )(kept["normed"], back["dqkv"], kept["att"], back["gb"], *init)


RING = 8
VEC_ROWS = 16


def items_of(d):
    return ((0, 0, 2 * d, 1), (1, 0, d, -1), (2, 2 * d, d, -1), (2, 0, 2 * d, 1), (3, 0, d // 2, -1))


def vector_block(sums):
    s1, s2, sq, ff = sums
    d = s1.shape[1]
    wide = lambda v: [v[:, i : i + d] for i in range(0, v.shape[1], d)]
    rows = [s1[:2], s2[:4], sq[0:1], sq[2:3]] + wide(ff)
    used = 8 + ff.shape[1] // d
    return jnp.concatenate(rows + [jnp.zeros((VEC_ROWS - used, d), F32)], axis=0)


def as_own(block, fold):
    half = block.shape[1] // 2
    qv = block[6:8]
    return jnp.concatenate(
        [
            block[:6], jnp.concatenate([qv[:, half:], qv[:, :half]], axis=1),
            block[8 + fold : 8 + 2 * fold], block[8 : 8 + fold], block[8 + 2 * fold :],
        ],
        axis=0,
    )


def ring_kernel(*refs, n, items, fold):
    owns, gifts = refs[:n], refs[n : 2 * n]
    sums = refs[2 * n : 2 * n + 8]
    at = 2 * n + 8
    outs, vsum_ref = refs[at : at + n], refs[at + n]
    at += n + 1
    theirs = refs[at : at + n]
    at += n
    m = len(items)
    slots = refs[at : at + m]
    vbuf, vother, vmine, vslot, send, recv, xsend, xrecv, vsend, vrecv, vxs, vxr = refs[at + m :]
    mesh_id = pl.DeviceIdType.MESH
    me = lax.axis_index("dp")
    partner = {"tensor": 1 - lax.axis_index("tensor")}
    z, x = me // 2, me % 2
    pos = z + x * (RING - 1 - 2 * z)

    def member(p):
        p = p % RING
        return {"dp": 2 * p + (p // (RING // 2)) * (2 * RING - 1 - 4 * p)}

    barrier = pltpu.get_barrier_semaphore()
    for k in range(1, RING):
        pl.semaphore_signal(barrier, inc=1, device_id=member(pos + k), device_id_type=mesh_id)
    pl.semaphore_signal(barrier, inc=1, device_id=partner, device_id_type=mesh_id)
    pl.semaphore_wait(barrier, RING)

    def part(arrays, a, chunk):
        i, first, rows, _ = items[a]
        rows = rows // RING
        return arrays[i].at[pl.ds(pl.multiple_of(first + (chunk % RING) * rows, rows), rows)]

    def chunk_at(a, step):
        return pos + 2 * RING - items[a][3] * step

    def exchange(a, step):
        return pltpu.make_async_remote_copy(
            src_ref=part(gifts, a, chunk_at(a, step)),
            dst_ref=part(theirs, a, chunk_at(a, step)),
            send_sem=xsend.at[a, step],
            recv_sem=xrecv.at[a, step],
            device_id=partner,
            device_id_type=mesh_id,
        )

    def mine(a, step):
        exchange(a, step).wait_recv()
        chunk = chunk_at(a, step)
        return part(owns, a, chunk)[...].astype(F32) + part(theirs, a, chunk)[...].astype(F32)

    def remote(src, dst, a, step):
        return pltpu.make_async_remote_copy(
            src_ref=src,
            dst_ref=dst,
            send_sem=send.at[a, step],
            recv_sem=recv.at[a, step],
            device_id=member(pos + items[a][3] + RING),
            device_id_type=mesh_id,
        )

    def vcopy(k):
        return pltpu.make_async_remote_copy(
            src_ref=vmine,
            dst_ref=vslot.at[k - 1],
            send_sem=vsend.at[k - 1],
            recv_sem=vrecv.at[k - 1],
            device_id=member(pos + k),
            device_id_type=mesh_id,
        )

    vexchange = pltpu.make_async_remote_copy(
        src_ref=vbuf, dst_ref=vother, send_sem=vxs, recv_sem=vxr,
        device_id=partner, device_id_type=mesh_id,
    )

    for step in range(2):
        for a in range(m):
            exchange(a, step).start()
    vbuf[...] = vector_block([sums[i][...] + sums[4 + i][...] for i in range(4)])
    vexchange.start()
    for a in range(m):
        slots[a][0] = mine(a, 0).astype(BF)
        remote(slots[a].at[0], slots[a].at[1], a, 0).start()

    def scatter(s, carry):
        for a in range(m):
            exchange(a, s + 1).start()
        for a in range(m):
            here = slots[a].at[s]
            own = mine(a, s)
            remote(here, here, a, s - 1).wait_recv()
            here[...] = (here[...].astype(F32) + own).astype(BF)
            remote(here, slots[a].at[s + 1], a, s).start()
        return carry

    lax.fori_loop(1, RING - 1, scatter, 0)
    vexchange.wait()
    vmine[...] = vbuf[...] + as_own(vother[...], fold)
    for k in range(1, RING):
        vcopy(k).start()
    for a in range(m):
        last = slots[a].at[RING - 1]
        own = mine(a, RING - 1)
        remote(last, last, a, RING - 2).wait_recv()
        done = part(outs, a, chunk_at(a, RING - 1))
        done[...] = (last[...].astype(F32) + own).astype(BF)
        remote(done, done, a, RING - 1).start()

    def gather(t, carry):
        for a in range(m):
            here = part(outs, a, chunk_at(a, t - 1))
            remote(here, here, a, RING - 2 + t).wait_recv()
            remote(here, here, a, RING - 1 + t).start()
        return carry

    lax.fori_loop(1, RING - 1, gather, 0)
    total = vmine[...]
    for k in range(1, RING):
        vcopy(k).wait()
        total += vslot[k - 1]
    vsum_ref[...] = total
    for a in range(m):
        here = part(outs, a, chunk_at(a, RING - 2))
        remote(here, here, a, 2 * RING - 3).wait_recv()
    for a in range(m):
        for s in range(RING - 1):
            remote(slots[a].at[0], slots[a].at[0], a, s).wait_send()
            here = part(outs, a, pos)
            remote(here, here, a, RING - 1 + s).wait_send()
        for s in range(RING):
            exchange(a, s).wait_send()


def ring(owns, gifts, sums_s, sums_l):
    n = len(owns)
    d = owns[0].shape[1]
    items = items_of(d)
    m = len(items)
    vmem = pl.BlockSpec(memory_space=pltpu.VMEM)
    dma = pltpu.SemaphoreType.DMA
    vec = pltpu.VMEM((VEC_ROWS, d), F32)
    out = pl.pallas_call(
        functools.partial(ring_kernel, n=n, items=items, fold=sums_s[3].shape[1] // (2 * d)),
        in_specs=[vmem] * (2 * n + 8),
        out_specs=[vmem] * (n + 1),
        out_shape=[sds(a.shape, BF) for a in owns] + [sds((VEC_ROWS, d), F32)],
        scratch_shapes=[pltpu.VMEM(a.shape, BF) for a in owns]
        + [pltpu.VMEM((RING, rows // RING, owns[i].shape[1]), BF) for i, _, rows, _ in items]
        + [
            vec, vec, vec, pltpu.VMEM((RING - 1, VEC_ROWS, d), F32),
            dma((m, 2 * RING - 2)), dma((m, 2 * RING - 2)), dma((m, RING)), dma((m, RING)),
            dma((RING - 1,)), dma((RING - 1,)), dma, dma,
        ],
        compiler_params=params(collective_id=1, has_side_effects=True),
        name="ring",
    )(*owns, *gifts, *sums_s, *sums_l)
    return out[:n], out[n]


def dp_sum(owns, gifts, sums_s, sums_l):
    if lax.axis_size("dp") == RING:
        return ring(owns, gifts, sums_s, sums_l)
    other = lambda array: lax.ppermute(array, "tensor", [(0, 1), (1, 0)])
    fold = sums_s[3].shape[1] // (2 * owns[0].shape[1])
    block = vector_block([a + b for a, b in zip(sums_s, sums_l)])
    summed = [lax.psum(a + other(b), "dp") for a, b in zip(owns, gifts)]
    return summed, lax.psum(block + as_own(other(block), fold), "dp")


def finish_kernel(*refs, fold):
    grads, vec, outs = refs[:4], refs[4], refs[5:]
    for g, out in zip(grads, outs):
        out[0] = g[...].astype(F32)

    @pl.when(pl.program_id(0) == 0)
    def _():
        half = vec.shape[1] // 2
        for i in range(6):
            outs[4 + i][...] = vec[i : i + 1]
        outs[10][0] = vec[6:8, :half]
        outs[11][...] = jnp.concatenate([vec[8 + i : 9 + i] for i in range(fold)], axis=1)


def finish(grads, vec):
    d = vec.shape[1]
    fold = grads[1].shape[1] // d
    steps = 8
    rows_in = lambda a: pl.BlockSpec((a.shape[0] // steps, a.shape[1]), lambda j: (j, 0))
    rows_out = lambda a: pl.BlockSpec((1, a.shape[0] // steps, a.shape[1]), lambda j: (0, j, 0))
    small = [(1, d)] * 6 + [(1, 2, d // 2), (1, fold * d)]
    return pl.pallas_call(
        functools.partial(finish_kernel, fold=fold),
        grid=(steps,),
        in_specs=[rows_in(a) for a in grads] + [whole(vec.shape)],
        out_specs=[rows_out(a) for a in grads] + [whole(a) for a in small],
        out_shape=[sds((1,) + a.shape, F32) for a in grads] + [sds(a, F32) for a in small],
        compiler_params=params(),
        name="finish",
    )(*grads, vec)


def starts_of(place):
    slots = [j + (j >= place) for j in range(SMALL_MB)]
    return [place * LEN_SMALL] + [
        slot * LEN_SMALL + (LEN_LARGE - LEN_SMALL) * (slot > place) for slot in slots
    ]


def layout(place):
    at = 0
    starts = starts_of(place)
    for c, (nimg, plen, vlen) in enumerate(CHUNKS):
        for i in range(nimg):
            yield starts[at], c, i * plen, plen, vlen
            at += 1


def cut_kernel(meta_ref, x_ref, *refs):
    outs, flat = refs[:-1], refs[-1]
    rows = x_ref.shape[0]
    flat[:rows] = x_ref[...].astype(F32)
    flat[rows:] = jnp.zeros((flat.shape[0] - rows, flat.shape[1]), F32)
    for place in range(SMALL_MB + 1):

        @pl.when(meta_ref[1 + meta_ref[0]] == place)
        def _():
            for start, c, r0, plen, vlen in layout(place):
                value = flat[start : start + plen]
                row = lax.broadcasted_iota(jnp.int32, value.shape, 0)
                outs[c][r0 : r0 + plen] = jnp.where(row < vlen, value, 0.0).astype(BF)


def cut(array, meta):
    rows = LEN_LARGE + SMALL_MB * LEN_SMALL
    d = array.shape[1]
    block = d // 3
    return pl.pallas_call(
        cut_kernel,
        grid_spec=pltpu.PrefetchScalarGridSpec(
            num_scalar_prefetch=1,
            grid=(3,),
            in_specs=[pl.BlockSpec((rows, block), lambda j, m: (m[0], j))],
            out_specs=[pl.BlockSpec((k * p, block), lambda j, m: (0, j)) for k, p, _ in CHUNKS],
            scratch_shapes=[pltpu.VMEM((rows + 16, block), F32)],
        ),
        out_shape=[sds((k * p, d), BF) for k, p, _ in CHUNKS],
        compiler_params=params(),
        name="cut",
    )(meta, array)


def join_kernel(meta_ref, *refs):
    count = len(CHUNKS)
    mine, theirs, out_ref, flat = refs[:count], refs[count : 2 * count], refs[-2], refs[-1]
    rows = flat.shape[0]
    for lane in range(2):
        here = meta_ref[0] == lane
        for place in range(SMALL_MB + 1):

            @pl.when(meta_ref[1 + lane] == place)
            def _():
                for start, c, r0, plen, vlen in layout(place):
                    own = mine[c][r0 : r0 + plen].astype(F32)
                    value = jnp.where(here, own, theirs[c][r0 : r0 + plen].astype(F32))
                    flat[start : start + vlen] = value[:vlen]

        out_ref[lane * rows : (lane + 1) * rows] = flat[...].astype(BF)


def join(mine, theirs, meta):
    rows = LEN_LARGE + SMALL_MB * LEN_SMALL
    d = mine[0].shape[1]
    block = d // 3
    return pl.pallas_call(
        join_kernel,
        grid_spec=pltpu.PrefetchScalarGridSpec(
            num_scalar_prefetch=1,
            grid=(3,),
            in_specs=[pl.BlockSpec((k * p, block), lambda j, m: (0, j)) for k, p, _ in CHUNKS] * 2,
            out_specs=pl.BlockSpec((2 * rows, block), lambda j, m: (0, j)),
            scratch_shapes=[pltpu.VMEM((rows, block), F32)],
        ),
        out_shape=sds((2 * rows, d), BF),
        compiler_params=params(),
        name="join",
    )(meta, *mine, *theirs)


def blank_kernel(*refs):
    pass


def blank(like):
    shapes = [sds(a.shape, a.dtype) for a in like]
    return tuple(
        pl.pallas_call(
            blank_kernel,
            out_shape=shapes,
            out_specs=[pl.BlockSpec(memory_space=pl.ANY) for _ in shapes],
            name="blank",
        )()
    )


KEPT = ("normed", "qkv", "att", "lse", "mid", "n2", "act", "dg", "out")
BACK = ("g", "pre", "gb", "dqkv", "sums2", "sff", "sums_qkv", "sums1", "gx")


def after(value, *earlier):
    return lax.optimization_barrier((value, earlier))[0]


def body(
    patches, out_grad, large_place, norm1_gain, norm1_bias, qkv_weight, qv_bias, proj_weight,
    proj_bias, norm2_gain, norm2_bias, up_weight, up_bias, down_weight, down_bias,
):
    d = patches.shape[1]
    half = qkv_weight.shape[-1]
    section = lax.axis_index("section")
    lane = lax.axis_index("tensor")
    both = [(0, 1), (1, 0)]
    other = lambda array: lax.ppermute(array, "tensor", both)

    wqkv, pw, up, dn = qkv_weight[0], proj_weight[0], up_weight[0], down_weight[0]
    meta = jnp.concatenate([lane[None], large_place])
    xs = cut(patches, meta)
    bias = jnp.concatenate([qv_bias.reshape(1, 2 * half), up_bias], axis=1)
    bias_parts = after((bias, other(bias)), xs)
    w = {
        "g1": norm1_gain, "b1": norm1_bias, "g2": norm2_gain, "b2": norm2_bias,
        "pb": proj_bias, "db": down_bias,
        "wqkv_o": wqkv, "wqkv_p": other(wqkv), "pw_o": pw, "pw_p": other(pw),
        "up_o": up, "up_p": other(up), "dn_o": dn, "dn_p": other(dn),
        **dict(zip(("bias_o", "bias_p"), bias_parts)),
    }


    large, smalls = 0, 1
    gs = cut(out_grad, meta)

    def pick(on, make, otherwise=None):
        like = jax.eval_shape(make)
        return lax.cond(
            section == on,
            lambda: tuple(make()),
            lambda: blank(like) if otherwise is None else tuple(otherwise),
        )

    def fwd(c, on, x, otherwise=None):
        return pick(on, lambda: forward(x, w, CHUNKS[c]), otherwise)

    def bwd(c, on, g, x, kept, otherwise=None):
        kept = dict(zip(KEPT, kept))
        return pick(on, lambda: backward(g, x, kept, w, CHUNKS[c]), otherwise)

    down = lambda array: lax.ppermute(array, "section", [(0, 1)])
    up_ = lambda array: lax.ppermute(array, "section", [(1, 0)])

    kept_s = fwd(smalls, 0, xs[smalls])
    in_s = down(kept_s[-1])
    x_l = after(xs[large], kept_s[-1])
    kept_l = fwd(large, 0, x_l)
    in_l = down(kept_l[-1])
    in_s = after(in_s, kept_l[-1])
    kept_s = fwd(smalls, 1, in_s, kept_s)
    back_s = bwd(smalls, 1, gs[smalls], in_s, kept_s)
    sent_s = up_(back_s[-1])
    in_l = after(in_l, back_s[-1])
    kept_l = fwd(large, 1, in_l, kept_l)
    back_l = bwd(large, 1, gs[large], in_l, kept_l)
    sent_l = up_(back_l[-1])
    back_s = bwd(smalls, 0, after(sent_s, back_l[-1]), xs[smalls], kept_s, back_s)
    named = lambda names, values: dict(zip(names, values))
    part_mlp = wgrad_mlp(named(KEPT, kept_s), named(BACK, back_s))
    part_attn = wgrad_attn(named(KEPT, kept_s), named(BACK, back_s))
    outs = [kept_l[-1], kept_s[-1]]
    outputs = join(outs, [other(a) for a in outs], meta)
    sent_l = after(sent_l, part_mlp, part_attn, outputs)
    back_l = bwd(large, 0, sent_l, xs[large], kept_l, back_l)
    dn_o, dn_p, up_o, up_p = wgrad_mlp(named(KEPT, kept_l), named(BACK, back_l), part_mlp)
    qkv_o, qkv_p, pw_o, pw_p = wgrad_attn(named(KEPT, kept_l), named(BACK, back_l), part_attn)
    grads = [back_l[-1], back_s[-1]]
    input_grads = join(grads, [other(a) for a in grads], meta)

    rows = lambda qkv: qkv.reshape(3 * d, half)
    sums = lambda back: [named(BACK, back)[k] for k in ("sums1", "sums2", "sums_qkv", "sff")]
    summed, vec = dp_sum(
        [dn_o, up_o, rows(qkv_o), pw_o], [dn_p, up_p, rows(qkv_p), pw_p], sums(back_s), sums(back_l)
    )
    g_dn, g_up, g_qkv, g_pw, g1, b1, g2, b2, pb, db, qv, ub = finish(summed, vec)
    return (
        outputs[None], input_grads[None], g1, b1, g_qkv.reshape(1, 3, d, half), qv, g_pw, pb,
        g2, b2, g_up, ub, g_dn, db,
    )


def solution(mesh):
    placed = (
        P("dp", None), P("dp", None), P("dp"), P("section", None), P("section", None),
        P("section", None, None, "tensor"), P("section", None, "tensor"),
        P("section", "tensor", None), P("section", None), P("section", None),
        P("section", None), P("section", None, "tensor"), P("section", "tensor"),
        P("section", "tensor", None), P("section", None),
    )
    return jax.shard_map(
        body,
        mesh=mesh,
        in_specs=placed,
        out_specs=(
            P("section", "dp", None), P("section", "dp", None), P("section", None),
            P("section", None), P("section", None, None, "tensor"), P("section", None, "tensor"),
            P("section", "tensor", None), P("section", None), P("section", None),
            P("section", None), P("section", None, "tensor"), P("section", "tensor"),
            P("section", "tensor", None), P("section", None),
        ),
        check_vma=False,
    )
```

```python
import functools

import jax
import jax.numpy as jnp
from jax import lax
from jax.experimental import pallas as pl
from jax.experimental.pallas import tpu as pltpu
from jax.sharding import PartitionSpec as P

HD = 64
LEN_SMALL = 197
LEN_LARGE = 577
SMALL_MB = 3
EPSILON = 1e-06
MASKED = -1e30
SCALE = HD ** (-0.5)
SCALE2 = SCALE * 1.4426950408889634
BF = jnp.bfloat16
F32 = jnp.float32
VMEM_LIMIT = 56 * 1024 * 1024
CHUNKS = ((1, 592, LEN_LARGE), (SMALL_MB, 208, LEN_SMALL))


def params(limit=VMEM_LIMIT, **more):
    return pltpu.CompilerParams(vmem_limit_bytes=limit, **more)


def nn(a, b):
    return jnp.dot(a, b, preferred_element_type=F32)


def nt(a, b):
    return lax.dot_general(a, b, (((1,), (1,)), ((), ())), preferred_element_type=F32)


def tn(a, b):
    return lax.dot_general(a, b, (((0,), (0,)), ((), ())), preferred_element_type=F32)


def whole(shape):
    zeros = (0,) * len(shape)
    return pl.BlockSpec(shape, lambda *_: zeros)


def sds(shape, dtype):
    return jax.ShapeDtypeStruct(shape, dtype)


def norm_parts(values):
    mean = jnp.mean(values, axis=-1, keepdims=True)
    centred = values - mean
    rstd = lax.rsqrt(jnp.mean(centred * centred, axis=-1, keepdims=True) + EPSILON)
    return centred * rstd, rstd


def norm_back(xhat, rstd, grad, gain):
    scaled = grad * gain
    m1 = jnp.mean(scaled, axis=-1, keepdims=True)
    m2 = jnp.mean(scaled * xhat, axis=-1, keepdims=True)
    return rstd * (scaled - m1 - xhat * m2)


def rowsum(values):
    return jnp.sum(values.astype(F32), axis=0, keepdims=True)


def fetch(pairs, sems):
    return [pltpu.make_async_copy(src, dst, sems.at[i]) for i, (src, dst) in enumerate(pairs)]


def weight_loads(w, wq, pw, up, dn):
    wqo, wqp, pwo, pwp, upo, upp, dno, dnp = w
    half, fh = wqo.shape[-1], dno.shape[0]
    return {
        "qkv": [(wqo, wq.at[:, :, :half]), (wqp, wq.at[:, :, half:])],
        "proj": [(pwo, pw.at[:half]), (pwp, pw.at[half:])],
        "up": [(upo, up.at[:, :fh]), (upp, up.at[:, fh:])],
        "down": [(dno, dn.at[:fh]), (dnp, dn.at[fh:])],
    }


def weights_of(w):
    return [w[k] for k in ("wqkv_o", "wqkv_p", "pw_o", "pw_p", "up_o", "up_p", "dn_o", "dn_p")]


def weight_scratch(d, ff):
    return [
        pltpu.VMEM((3, d, d), BF), pltpu.VMEM((d, d), BF), pltpu.VMEM((d, ff), BF),
        pltpu.VMEM((ff, d), BF),
    ]


def lanes(at, width):
    return pl.ds(pl.multiple_of(at * width, width), width)


def mask_keys(scores, vlen):
    rows = scores.shape[0]
    keep = vlen // 8 * 8
    tail = scores[keep:]
    idx = lax.broadcasted_iota(jnp.int32, tail.shape, 0) + keep
    return jnp.concatenate([scores[:keep], jnp.where(idx < vlen, tail, MASKED)], axis=0)


def qblocks(plen):
    step = min(256, plen)
    return [(q, min(step, 2 * plen - q)) for q in range(0, 2 * plen, step)]


def lse_width(chunk):
    nimg, plen, _ = chunk
    return nimg * len(qblocks(plen)) * 256


def both_heads(rows):
    head = lax.broadcasted_iota(jnp.int32, rows.shape, 1) // HD
    none = jnp.zeros_like(rows)
    return jnp.concatenate([jnp.where(head == h, rows, none) for h in range(2)], axis=0)


def one_each(stacked, plen):
    head = lax.broadcasted_iota(jnp.int32, (plen, stacked.shape[1]), 1) // HD
    return jnp.where(head == 0, stacked[:plen], stacked[plen:])


def blocks_of(chunk):
    nimg, plen, _ = chunk
    return [(im, q0, qw) for im in range(nimg) for q0, qw in qblocks(plen)]


def attn_fwd_pair(p, qkv, att, lse, o_tmp, chunk):
    nimg, plen, vlen = chunk
    cols = lanes(p, 128)
    images = [slice(im * plen, (im + 1) * plen) for im in range(nimg)]
    k = [qkv[1, rows, cols] for rows in images]
    vt = [qkv[2, rows, cols].T for rows in images]
    queries = [both_heads(qkv[0, rows, cols]) for rows in images]
    blocks = blocks_of(chunk)
    scores = lambda im, q0, qw: nt(k[im], queries[im][q0 : q0 + qw])
    coming = scores(*blocks[0])
    for i, (im, q0, qw) in enumerate(blocks):
        st = mask_keys(coming, vlen)
        if i + 1 < len(blocks):
            coming = scores(*blocks[i + 1])
        top = jnp.max(st, axis=0, keepdims=True)
        e = jnp.exp2((st - top) * SCALE2)
        total = jnp.sum(e, axis=0, keepdims=True)
        o_tmp[q0 : q0 + qw] = (nn(vt[im], e.astype(BF)) * (1.0 / total)).T
        lse[p, :, i * 256 : i * 256 + qw] = top * SCALE2 + jnp.log2(total)
        if q0 + qw == 2 * plen:
            att[images[im], cols] = one_each(o_tmp, plen).astype(BF)


def gelu_parts(x):
    cdf = 0.5 + 0.5 * lax.erf(x * (2.0**-0.5))
    pdf = jnp.exp(-0.5 * x * x) * 0.3989422804014327
    return x * cdf, cdf + x * pdf


FF_STEPS = 2
WGRAD_STEPS = 4


def fwd_kernel(*refs, chunk):
    x_ref, g1, b1, own_bias, other_bias, pb, g2, b2, db = refs[:9]
    weights, outs = refs[9:17], refs[17:26]
    wq, pw, up, dn = refs[26:30]
    held = refs[30:39]
    acc, o_tmp, ub, in_sem, out_sem, ff_sem = refs[39:]
    normed, qkv, att, lse, mid, n2, act, dg, out = held
    ff = dn.shape[0]
    fb = ff // FF_STEPS
    loads = weight_loads(weights, wq, pw, up, dn)
    names = ("qkv", "proj", "up", "down")
    loads = {k: fetch(loads[k], in_sem.at[i]) for i, k in enumerate(names)}
    saves = fetch(list(zip(held[:6] + held[8:], outs[:6] + outs[8:])), out_sem)
    for c in loads["qkv"]:
        c.start()
    xhat, _ = norm_parts(x_ref[...].astype(F32))
    normed[...] = (xhat * g1[...] + b1[...]).astype(BF)
    saves[0].start()
    half = wq.shape[1] // 2

    def bias_of(first, last):
        return jnp.concatenate([own_bias[:, first:last], other_bias[:, first:last]], axis=1)

    q_bias, v_bias = bias_of(0, half), bias_of(half, 2 * half)
    ub[...] = bias_of(2 * half, own_bias.shape[1])
    for c in loads["qkv"]:
        c.wait()
    for k in names[1:]:
        for c in loads[k]:
            c.start()

    def project(s, carry):
        bias = jnp.where(s == 0, q_bias, jnp.where(s == 1, 0.0, v_bias))
        qkv[s] = (nn(normed[...], wq[s]) + bias).astype(BF)
        return carry

    lax.fori_loop(0, 3, project, 0)
    saves[1].start()

    def attend(p, carry):
        attn_fwd_pair(p, qkv, att, lse, o_tmp, chunk)
        return carry

    lax.fori_loop(0, lse.shape[0], attend, 0)
    saves[2].start()
    saves[3].start()
    for c in loads["proj"]:
        c.wait()
    middle = x_ref[...].astype(F32) + (nn(att[...], pw[...]) + pb[...])
    mid[...] = middle
    saves[4].start()
    xhat, _ = norm_parts(middle)
    n2[...] = (xhat * g2[...] + b2[...]).astype(BF)
    saves[5].start()
    acc[...] = middle + db[...]
    for k in ("up", "down"):
        for c in loads[k]:
            c.wait()

    def block_saves(j):
        cols = lanes(j, fb)
        pairs = [(act.at[:, cols], outs[6].at[:, cols]), (dg.at[:, cols], outs[7].at[:, cols])]
        return fetch(pairs, ff_sem.at[j])

    def mlp(j, carry):
        cols = lanes(j, fb)
        value, slope = gelu_parts(nn(n2[...], up[:, cols]) + ub[:, cols])
        value = value.astype(BF)
        act[:, cols] = value
        dg[:, cols] = slope.astype(BF)
        for c in block_saves(j):
            c.start()
        acc[...] += nn(value, dn[cols])
        return carry

    lax.fori_loop(0, FF_STEPS, mlp, 0)
    out[...] = acc[...].astype(BF)
    saves[6].start()
    for c in saves:
        c.wait()
    for j in range(FF_STEPS):
        for c in block_saves(j):
            c.wait()


def forward(x, w, chunk):
    n, d = x.shape
    ff = 2 * w["dn_o"].shape[0]
    pairs = d // 128
    kept = [
        ((n, d), BF), ((3, n, d), BF), ((n, d), BF), ((pairs, 1, lse_width(chunk)), F32),
        ((n, d), F32), ((n, d), BF), ((n, ff), BF), ((n, ff), BF), ((n, d), BF),
    ]
    vmem = pl.BlockSpec(memory_space=pltpu.VMEM)
    hbm = pl.BlockSpec(memory_space=pl.ANY)
    return pl.pallas_call(
        functools.partial(fwd_kernel, chunk=chunk),
        in_specs=[vmem] * 9 + [hbm] * 8,
        out_specs=[hbm] * len(kept),
        out_shape=[sds(*k) for k in kept],
        scratch_shapes=weight_scratch(d, ff)
        + [pltpu.VMEM(*k) for k in kept]
        + [
            pltpu.VMEM((n, d), F32), pltpu.VMEM((2 * chunk[1], 128), F32),
            pltpu.VMEM((1, ff), F32), pltpu.SemaphoreType.DMA((4, 2)),
            pltpu.SemaphoreType.DMA((7,)), pltpu.SemaphoreType.DMA((FF_STEPS, 2)),
        ],
        compiler_params=params(),
        name="fwd",
    )(
        x, w["g1"], w["b1"], w["bias_o"], w["bias_p"], w["pb"], w["g2"], w["b2"], w["db"],
        *weights_of(w),
    )


def attn_bwd_pair(p, qkv, att, gatt, lse, dqkv, sums, dq_tmp, chunk):
    nimg, plen, vlen = chunk
    cols = lanes(p, 128)
    images = [slice(im * plen, (im + 1) * plen) for im in range(nimg)]
    k = [qkv[1, rows, cols] for rows in images]
    v = [qkv[2, rows, cols] for rows in images]
    queries = [both_heads(qkv[0, rows, cols]) for rows in images]
    grads = [both_heads(gatt[rows, cols]) for rows in images]
    blocks = blocks_of(chunk)

    def scores(im, q0, qw):
        return nt(k[im], queries[im][q0 : q0 + qw]), nt(v[im], grads[im][q0 : q0 + qw])

    total_q, total_v = jnp.zeros((1, 128), F32), jnp.zeros((1, 128), F32)
    coming = scores(*blocks[0])
    for i, (im, q0, qw) in enumerate(blocks):
        rows = images[im]
        if q0 == 0:
            kt = k[im].T
            products = both_heads(gatt[rows, cols].astype(F32) * att[rows, cols].astype(F32))
            dk = jnp.zeros((plen, 128), F32)
            dv = jnp.zeros((plen, 128), F32)
        q = queries[im][q0 : q0 + qw]
        ga = grads[im][q0 : q0 + qw]
        st, gp = mask_keys(coming[0], vlen), coming[1]
        if i + 1 < len(blocks):
            coming = scores(*blocks[i + 1])
        pr = jnp.exp2(st * SCALE2 - lse[p, :, i * 256 : i * 256 + qw])
        dv += nn(pr.astype(BF), ga)
        delta = jnp.sum(products[q0 : q0 + qw].T, axis=0, keepdims=True)
        ds = (pr * (gp - delta)).astype(BF)
        dk += nn(ds, q)
        dq_tmp[q0 : q0 + qw] = nn(kt, ds).T
        if q0 + qw == 2 * plen:
            dq = (one_each(dq_tmp, plen) * SCALE).astype(BF)
            dvb = dv.astype(BF)
            dqkv[0, rows, cols] = dq
            dqkv[1, rows, cols] = (dk * SCALE).astype(BF)
            dqkv[2, rows, cols] = dvb
            total_q += rowsum(dq)
            total_v += rowsum(dvb)
    sums[:, cols] = jnp.concatenate(
        [total_q, jnp.zeros_like(total_q), total_v, jnp.zeros((5, 128), F32)], axis=0
    )


def bwd_kernel(*refs, chunk):
    g_ref, g2, g1 = refs[:3]
    mid_h, dg_h, qkv_h, lse_h, x_h, att_h = refs[3:9]
    weights, outs = refs[9:17], refs[17:22]
    sums2, sff, sums_qkv, sums1 = refs[22:26]
    wq, pw, up, dn = refs[26:30]
    mid, dg, qkv, lse, x, att, pre, gb, dqkv, gx, gm, ga, acc, dq_tmp, in_sem, late_sem, out_sem, ff_sem = refs[30:]
    ff = dn.shape[0]
    fb = ff // FF_STEPS
    loads = weight_loads(weights, wq, pw, up, dn)
    names = ("proj", "qkv")
    loads = {k: fetch(loads[k], in_sem.at[i]) for i, k in enumerate(names)}
    late = fetch([(mid_h, mid), (qkv_h, qkv), (lse_h, lse), (att_h, att), (x_h, x)], late_sem)
    saves = fetch(list(zip((pre, gb, dqkv, gx, g_ref), outs)), out_sem)

    def block_loads(j):
        if isinstance(j, int):
            owner, first = divmod(j * fb, ff // 2)
            rows = slice(first, first + fb)
            cols = slice(j * fb, (j + 1) * fb)
        else:
            owner, rows, cols = 0, slice(0, fb), lanes(j, fb)
        pairs = [
            (weights[6 + owner].at[rows], dn.at[cols]),
            (dg_h.at[:, cols], dg.at[:, cols]),
            (weights[4 + owner].at[:, rows], up.at[:, cols]),
        ]
        return fetch(pairs, ff_sem.at[j])

    for j in range(FF_STEPS):
        for c in block_loads(j):
            c.start()
    saves[4].start()
    for c in late:
        c.start()
    for k in ("proj", "qkv"):
        for c in loads[k]:
            c.start()
    acc[...] = jnp.zeros_like(acc)

    def mlp(j, carry):
        cols = lanes(j, fb)
        for c in block_loads(j):
            c.wait()
        value = (nt(g_ref[...], dn[cols]) * dg[:, cols].astype(F32)).astype(BF)
        pre[:, cols] = value
        sff[:, cols] = rowsum(value)
        acc[...] += nt(value, up[:, cols])
        return carry

    lax.fori_loop(0, FF_STEPS, mlp, 0)
    saves[0].start()
    late[0].wait()
    gn = acc[...]
    xhat, rstd = norm_parts(mid[...])
    grad = norm_back(xhat, rstd, gn, g2[...]) + g_ref[...].astype(F32)
    gm[...] = grad
    branch = grad.astype(BF)
    gb[...] = branch
    saves[1].start()
    sums2[...] = jnp.concatenate(
        [rowsum(gn * xhat), rowsum(gn), rowsum(branch), rowsum(g_ref[...])]
        + [jnp.zeros((4, gn.shape[1]), F32)], axis=0
    )
    for c in loads["proj"]:
        c.wait()
    ga[...] = nt(gb[...], pw[...]).astype(BF)
    for c in late[1:4]:
        c.wait()

    def attend(p, carry):
        attn_bwd_pair(p, qkv, att, ga, lse, dqkv, sums_qkv, dq_tmp, chunk)
        return carry

    lax.fori_loop(0, lse.shape[0], attend, 0)
    saves[2].start()
    for c in loads["qkv"]:
        c.wait()
    late[4].wait()
    acc[...] = nt(dqkv[0], wq[0])

    def project(s, carry):
        acc[...] += nt(dqkv[s], wq[s])
        return carry

    lax.fori_loop(1, 3, project, 0)
    gn = acc[...]
    xhat, rstd = norm_parts(x[...].astype(F32))
    gx[...] = (norm_back(xhat, rstd, gn, g1[...]) + gm[...]).astype(BF)
    saves[3].start()
    sums1[...] = jnp.concatenate(
        [rowsum(gn * xhat), rowsum(gn), jnp.zeros((6, gn.shape[1]), F32)], axis=0
    )
    for c in saves:
        c.wait()


def backward(g, x, kept, w, chunk):
    n, d = g.shape
    ff = kept["act"].shape[1]
    vmem = pl.BlockSpec(memory_space=pltpu.VMEM)
    hbm = pl.BlockSpec(memory_space=pl.ANY)
    wide, tall = ((n, d), BF), ((n, ff), BF)
    three, flat = ((3, n, d), BF), ((n, d), F32)
    lse = (kept["lse"].shape, F32)
    dma = pltpu.SemaphoreType.DMA
    pre, gb, dqkv, gx, copy, sums2, sff, sums_qkv, sums1 = pl.pallas_call(
        functools.partial(bwd_kernel, chunk=chunk),
        in_specs=[vmem] * 3 + [hbm] * 14,
        out_specs=[hbm] * 5 + [vmem] * 4,
        out_shape=[sds(*k) for k in (tall, wide, three, wide, wide)]
        + [sds((8, d), F32), sds((1, ff), F32), sds((8, d), F32), sds((8, d), F32)],
        scratch_shapes=weight_scratch(d, ff)
        + [
            pltpu.VMEM(*k)
            for k in (flat, tall, three, lse, wide, wide, tall, wide, three, wide, flat, wide, flat)
        ]
        + [pltpu.VMEM((2 * chunk[1], 128), F32), dma((2, 2)), dma((5,)), dma((5,)), dma((FF_STEPS, 3))],
        compiler_params=params(),
        name="bwd",
    )(
        g, w["g2"], w["g1"], kept["mid"], kept["dg"], kept["qkv"], kept["lse"], x, kept["att"], *weights_of(w)
    )
    return (copy, pre, gb, dqkv, sums2, sff, sums_qkv, sums1, gx)


def wgrad_mlp_kernel(act, n2, pre, g, *refs, more):
    init, outs = refs[:more], refs[more:]
    j = pl.program_id(0)
    down, up = tn(act[...], g[...]), tn(n2[...], pre[...])
    for i in range(2):

        @pl.when(j // (WGRAD_STEPS // 2) == i)
        def _():
            for at, value in ((i, down), (2 + i, up)):
                if more:
                    value = value + init[at][...].astype(F32)
                outs[at][...] = value.astype(BF)


def wgrad_mlp(kept, back, init=()):
    n, d = back["g"].shape
    ff = kept["act"].shape[1]
    fb, last = ff // WGRAD_STEPS, WGRAD_STEPS // 2 - 1
    cols = pl.BlockSpec((n, fb), lambda j: (0, j))
    at = [lambda j: jnp.minimum(j, last), lambda j: jnp.maximum(j - last - 1, 0)]
    outs = [pl.BlockSpec((fb, d), lambda j, i=i: (at[i](j), 0)) for i in range(2)]
    outs += [pl.BlockSpec((d, fb), lambda j, i=i: (0, at[i](j))) for i in range(2)]
    return pl.pallas_call(
        functools.partial(wgrad_mlp_kernel, more=len(init)),
        grid=(WGRAD_STEPS,),
        in_specs=[cols, whole((n, d)), cols, whole((n, d))] + outs[: len(init)],
        out_specs=outs,
        out_shape=[sds((ff // 2, d), BF)] * 2 + [sds((d, ff // 2), BF)] * 2,
        compiler_params=params(),
        name="wgrad_mlp",
    )(kept["act"], kept["n2"], back["pre"], back["g"], *init)


def wgrad_attn_kernel(*refs, more):
    normed, dqkv, att, gb = refs[:4]
    init = refs[4 : 4 + more]
    outs = refs[4 + more :]
    s = pl.program_id(0)
    total = tn(normed[...], dqkv[0])
    half = outs[0].shape[-1]
    for i, value in enumerate((total[:, :half], total[:, half:])):
        if more:
            value += init[i][0].astype(F32)
        outs[i][0] = value.astype(BF)
    for i in range(2):

        @pl.when(s == i)
        def _():
            value = tn(att[...], gb[...])
            if more:
                value += init[2 + i][...].astype(F32)
            outs[2 + i][...] = value.astype(BF)


def wgrad_attn(kept, back, init=()):
    n, d = kept["normed"].shape
    half = d // 2
    part = pl.BlockSpec((1, d, half), lambda s: (s, 0, 0))
    outs = [part, part, whole((half, d)), whole((half, d))]
    return pl.pallas_call(
        functools.partial(wgrad_attn_kernel, more=len(init)),
        grid=(3,),
        in_specs=[
            whole((n, d)), pl.BlockSpec((1, n, d), lambda s: (s, 0, 0)),
            pl.BlockSpec((n, half), lambda s: (0, jnp.minimum(s, 1))), whole((n, d)),
        ]
        + outs[: len(init)],
        out_specs=outs,
        out_shape=[sds((3, d, half), BF)] * 2 + [sds((half, d), BF)] * 2,
        compiler_params=params(),
        name="wgrad_attn",
    )(kept["normed"], back["dqkv"], kept["att"], back["gb"], *init)


RING = 8
VEC_ROWS = 16


def items_of(d):
    return ((0, 0, 2 * d, 1), (1, 0, d, -1), (2, 2 * d, d, -1), (2, 0, 2 * d, 1), (3, 0, d // 2, -1))


def vector_block(sums):
    s1, s2, sq, ff = sums
    d = s1.shape[1]
    wide = lambda v: [v[:, i : i + d] for i in range(0, v.shape[1], d)]
    rows = [s1[:2], s2[:4], sq[0:1], sq[2:3]] + wide(ff)
    used = 8 + ff.shape[1] // d
    return jnp.concatenate(rows + [jnp.zeros((VEC_ROWS - used, d), F32)], axis=0)


def as_own(block, fold):
    half = block.shape[1] // 2
    qv = block[6:8]
    return jnp.concatenate(
        [
            block[:6], jnp.concatenate([qv[:, half:], qv[:, :half]], axis=1),
            block[8 + fold : 8 + 2 * fold], block[8 : 8 + fold], block[8 + 2 * fold :],
        ],
        axis=0,
    )


def ring_kernel(*refs, n, items, fold):
    normed, dqkv, att, gb = refs[:4]
    parts, sums = refs[4:8], refs[12:20]
    at = 20
    outs, vsum_ref = refs[at : at + n], refs[at + n]
    at += n + 1
    theirs = refs[at : at + n]
    at += n
    own_qkv, own_pw, gift_qkv, gift_pw = refs[at : at + 4]
    owns = refs[8:10] + (own_qkv, own_pw)
    gifts = refs[10:12] + (gift_qkv, gift_pw)
    at += 4
    m = len(items)
    slots = refs[at : at + m]
    vbuf, vother, vmine, vslot, send, recv, xsend, xrecv, vsend, vrecv, vxs, vxr = refs[at + m :]
    mesh_id = pl.DeviceIdType.MESH
    me = lax.axis_index("dp")
    partner = {"tensor": 1 - lax.axis_index("tensor")}
    z, x = me // 2, me % 2
    pos = z + x * (RING - 1 - 2 * z)

    def member(p):
        p = p % RING
        return {"dp": 2 * p + (p // (RING // 2)) * (2 * RING - 1 - 4 * p)}

    barrier = pltpu.get_barrier_semaphore()
    for k in range(1, RING):
        pl.semaphore_signal(barrier, inc=1, device_id=member(pos + k), device_id_type=mesh_id)
    pl.semaphore_signal(barrier, inc=1, device_id=partner, device_id_type=mesh_id)
    pl.semaphore_wait(barrier, RING)

    def part(arrays, a, chunk):
        i, first, rows, _ = items[a]
        rows = rows // RING
        return arrays[i].at[pl.ds(pl.multiple_of(first + (chunk % RING) * rows, rows), rows)]

    def chunk_at(a, step):
        return pos + 2 * RING - items[a][3] * step

    def exchange(a, step):
        return pltpu.make_async_remote_copy(
            src_ref=part(gifts, a, chunk_at(a, step)),
            dst_ref=part(theirs, a, chunk_at(a, step)),
            send_sem=xsend.at[a, step],
            recv_sem=xrecv.at[a, step],
            device_id=partner,
            device_id_type=mesh_id,
        )

    def mine(a, step):
        exchange(a, step).wait_recv()
        chunk = chunk_at(a, step)
        return part(owns, a, chunk)[...].astype(F32) + part(theirs, a, chunk)[...].astype(F32)

    def remote(src, dst, a, step):
        return pltpu.make_async_remote_copy(
            src_ref=src,
            dst_ref=dst,
            send_sem=send.at[a, step],
            recv_sem=recv.at[a, step],
            device_id=member(pos + items[a][3] + RING),
            device_id_type=mesh_id,
        )

    def vcopy(k):
        return pltpu.make_async_remote_copy(
            src_ref=vmine,
            dst_ref=vslot.at[k - 1],
            send_sem=vsend.at[k - 1],
            recv_sem=vrecv.at[k - 1],
            device_id=member(pos + k),
            device_id_type=mesh_id,
        )

    vexchange = pltpu.make_async_remote_copy(
        src_ref=vbuf, dst_ref=vother, send_sem=vxs, recv_sem=vxr,
        device_id=partner, device_id_type=mesh_id,
    )

    def begin(arrays):
        for step in range(2):
            for a in arrays:
                exchange(a, step).start()
        for a in arrays:
            slots[a][0] = mine(a, 0).astype(BF)
            remote(slots[a].at[0], slots[a].at[1], a, 0).start()

    begin(range(2))
    vbuf[...] = vector_block([sums[i][...] + sums[4 + i][...] for i in range(4)])
    vexchange.start()
    d = normed.shape[1]
    half = d // 2
    for s in range(3):
        total = tn(normed[...], dqkv[s])
        rows = slice(s * d, (s + 1) * d)
        own_qkv[rows] = (total[:, :half] + parts[0][s].astype(F32)).astype(BF)
        gift_qkv[rows] = (total[:, half:] + parts[1][s].astype(F32)).astype(BF)
    own_pw[...] = (tn(att[:, :half], gb[...]) + parts[2][...].astype(F32)).astype(BF)
    gift_pw[...] = (tn(att[:, half:], gb[...]) + parts[3][...].astype(F32)).astype(BF)
    begin(range(2, m))

    def scatter(s, carry):
        for a in range(m):
            exchange(a, s + 1).start()
        for a in range(m):
            here = slots[a].at[s]
            own = mine(a, s)
            remote(here, here, a, s - 1).wait_recv()
            here[...] = (here[...].astype(F32) + own).astype(BF)
            remote(here, slots[a].at[s + 1], a, s).start()
        return carry

    lax.fori_loop(1, RING - 1, scatter, 0)
    vexchange.wait()
    vmine[...] = vbuf[...] + as_own(vother[...], fold)
    for k in range(1, RING):
        vcopy(k).start()
    for a in range(m):
        last = slots[a].at[RING - 1]
        own = mine(a, RING - 1)
        remote(last, last, a, RING - 2).wait_recv()
        done = part(outs, a, chunk_at(a, RING - 1))
        done[...] = (last[...].astype(F32) + own).astype(BF)
        remote(done, done, a, RING - 1).start()

    def gather(t, carry):
        for a in range(m):
            here = part(outs, a, chunk_at(a, t - 1))
            remote(here, here, a, RING - 2 + t).wait_recv()
            remote(here, here, a, RING - 1 + t).start()
        return carry

    lax.fori_loop(1, RING - 1, gather, 0)
    total = vmine[...]
    for k in range(1, RING):
        vcopy(k).wait()
        total += vslot[k - 1]
    vsum_ref[...] = total
    for a in range(m):
        here = part(outs, a, chunk_at(a, RING - 2))
        remote(here, here, a, 2 * RING - 3).wait_recv()
    for a in range(m):
        for s in range(RING - 1):
            remote(slots[a].at[0], slots[a].at[0], a, s).wait_send()
            here = part(outs, a, pos)
            remote(here, here, a, RING - 1 + s).wait_send()
        for s in range(RING):
            exchange(a, s).wait_send()


def ring(mlp, kept, back, parts, sums):
    d = kept["normed"].shape[1]
    shapes = [mlp[0].shape, mlp[2].shape, (3 * d, d // 2), (d // 2, d)]
    n = len(shapes)
    items = items_of(d)
    m = len(items)
    vmem = pl.BlockSpec(memory_space=pltpu.VMEM)
    hbm = pl.BlockSpec(memory_space=pl.ANY)
    dma = pltpu.SemaphoreType.DMA
    vec = pltpu.VMEM((VEC_ROWS, d), F32)
    out = pl.pallas_call(
        functools.partial(ring_kernel, n=n, items=items, fold=sums[3].shape[1] // (2 * d)),
        in_specs=[vmem] * 10 + [hbm] * 2 + [vmem] * 8,
        out_specs=[vmem] * (n + 1),
        out_shape=[sds(a, BF) for a in shapes] + [sds((VEC_ROWS, d), F32)],
        scratch_shapes=[pltpu.VMEM(a, BF) for a in shapes + 2 * shapes[2:]]
        + [pltpu.VMEM((RING, rows // RING, shapes[i][1]), BF) for i, _, rows, _ in items]
        + [
            vec, vec, vec, pltpu.VMEM((RING - 1, VEC_ROWS, d), F32),
            dma((m, 2 * RING - 2)), dma((m, 2 * RING - 2)), dma((m, RING)), dma((m, RING)),
            dma((RING - 1,)), dma((RING - 1,)), dma, dma,
        ],
        compiler_params=params(collective_id=1, has_side_effects=True),
        name="ring",
    )(
        kept["normed"], back["dqkv"], kept["att"], back["gb"], *parts, mlp[0], mlp[2], mlp[1],
        mlp[3], *sums,
    )
    return out[:n], out[n]


def dp_sum(mlp, kept, back, parts, sums):
    if lax.axis_size("dp") == RING:
        return ring(mlp, kept, back, parts, sums)
    other = lambda array: lax.ppermute(array, "tensor", [(0, 1), (1, 0)])
    qkv_o, qkv_p, pw_o, pw_p = wgrad_attn(kept, back, parts)
    rows = lambda qkv: qkv.reshape(-1, qkv.shape[2])
    owns = [mlp[0], mlp[2], rows(qkv_o), pw_o]
    gifts = [mlp[1], mlp[3], rows(qkv_p), pw_p]
    fold = sums[3].shape[1] // (2 * pw_o.shape[1])
    block = vector_block([a + b for a, b in zip(sums[:4], sums[4:])])
    summed = [lax.psum(a + other(b), "dp") for a, b in zip(owns, gifts)]
    return summed, lax.psum(block + as_own(other(block), fold), "dp")


def finish_kernel(*refs, fold):
    grads, vec, outs = refs[:4], refs[4], refs[5:]
    for g, out in zip(grads, outs):
        out[0] = g[...].astype(F32)

    @pl.when(pl.program_id(0) == 0)
    def _():
        half = vec.shape[1] // 2
        for i in range(6):
            outs[4 + i][...] = vec[i : i + 1]
        outs[10][0] = vec[6:8, :half]
        outs[11][...] = jnp.concatenate([vec[8 + i : 9 + i] for i in range(fold)], axis=1)


def finish(grads, vec):
    d = vec.shape[1]
    fold = grads[1].shape[1] // d
    steps = 8
    rows_in = lambda a: pl.BlockSpec((a.shape[0] // steps, a.shape[1]), lambda j: (j, 0))
    rows_out = lambda a: pl.BlockSpec((1, a.shape[0] // steps, a.shape[1]), lambda j: (0, j, 0))
    small = [(1, d)] * 6 + [(1, 2, d // 2), (1, fold * d)]
    return pl.pallas_call(
        functools.partial(finish_kernel, fold=fold),
        grid=(steps,),
        in_specs=[rows_in(a) for a in grads] + [whole(vec.shape)],
        out_specs=[rows_out(a) for a in grads] + [whole(a) for a in small],
        out_shape=[sds((1,) + a.shape, F32) for a in grads] + [sds(a, F32) for a in small],
        compiler_params=params(),
        name="finish",
    )(*grads, vec)


def starts_of(place):
    slots = [j + (j >= place) for j in range(SMALL_MB)]
    return [place * LEN_SMALL] + [
        slot * LEN_SMALL + (LEN_LARGE - LEN_SMALL) * (slot > place) for slot in slots
    ]


def layout(place):
    at = 0
    starts = starts_of(place)
    for c, (nimg, plen, vlen) in enumerate(CHUNKS):
        for i in range(nimg):
            yield starts[at], c, i * plen, plen, vlen
            at += 1


def cut_kernel(meta_ref, x_ref, *refs):
    outs, flat = refs[:-1], refs[-1]
    rows = x_ref.shape[0]
    flat[:rows] = x_ref[...].astype(F32)
    flat[rows:] = jnp.zeros((flat.shape[0] - rows, flat.shape[1]), F32)
    for place in range(SMALL_MB + 1):

        @pl.when(meta_ref[1 + meta_ref[0]] == place)
        def _():
            for start, c, r0, plen, vlen in layout(place):
                value = flat[start : start + plen]
                row = lax.broadcasted_iota(jnp.int32, value.shape, 0)
                outs[c][r0 : r0 + plen] = jnp.where(row < vlen, value, 0.0).astype(BF)


def cut(array, meta):
    rows = LEN_LARGE + SMALL_MB * LEN_SMALL
    d = array.shape[1]
    block = d // 3
    return pl.pallas_call(
        cut_kernel,
        grid_spec=pltpu.PrefetchScalarGridSpec(
            num_scalar_prefetch=1,
            grid=(3,),
            in_specs=[pl.BlockSpec((rows, block), lambda j, m: (m[0], j))],
            out_specs=[pl.BlockSpec((k * p, block), lambda j, m: (0, j)) for k, p, _ in CHUNKS],
            scratch_shapes=[pltpu.VMEM((rows + 16, block), F32)],
        ),
        out_shape=[sds((k * p, d), BF) for k, p, _ in CHUNKS],
        compiler_params=params(),
        name="cut",
    )(meta, array)


def join_kernel(meta_ref, *refs):
    count = len(CHUNKS)
    mine, theirs, out_ref, flat = refs[:count], refs[count : 2 * count], refs[-2], refs[-1]
    rows = flat.shape[0]
    for lane in range(2):
        here = meta_ref[0] == lane
        for place in range(SMALL_MB + 1):

            @pl.when(meta_ref[1 + lane] == place)
            def _():
                for start, c, r0, plen, vlen in layout(place):
                    own = mine[c][r0 : r0 + plen].astype(F32)
                    value = jnp.where(here, own, theirs[c][r0 : r0 + plen].astype(F32))
                    flat[start : start + vlen] = value[:vlen]

        out_ref[lane * rows : (lane + 1) * rows] = flat[...].astype(BF)


def join(mine, theirs, meta):
    rows = LEN_LARGE + SMALL_MB * LEN_SMALL
    d = mine[0].shape[1]
    block = d // 3
    return pl.pallas_call(
        join_kernel,
        grid_spec=pltpu.PrefetchScalarGridSpec(
            num_scalar_prefetch=1,
            grid=(3,),
            in_specs=[pl.BlockSpec((k * p, block), lambda j, m: (0, j)) for k, p, _ in CHUNKS] * 2,
            out_specs=pl.BlockSpec((2 * rows, block), lambda j, m: (0, j)),
            scratch_shapes=[pltpu.VMEM((rows, block), F32)],
        ),
        out_shape=sds((2 * rows, d), BF),
        compiler_params=params(),
        name="join",
    )(meta, *mine, *theirs)


def blank_kernel(*refs):
    pass


def blank(like):
    shapes = [sds(a.shape, a.dtype) for a in like]
    return tuple(
        pl.pallas_call(
            blank_kernel,
            out_shape=shapes,
            out_specs=[pl.BlockSpec(memory_space=pl.ANY) for _ in shapes],
            name="blank",
        )()
    )


KEPT = ("normed", "qkv", "att", "lse", "mid", "n2", "act", "dg", "out")
BACK = ("g", "pre", "gb", "dqkv", "sums2", "sff", "sums_qkv", "sums1", "gx")


def after(value, *earlier):
    return lax.optimization_barrier((value, earlier))[0]


def body(
    patches, out_grad, large_place, norm1_gain, norm1_bias, qkv_weight, qv_bias, proj_weight,
    proj_bias, norm2_gain, norm2_bias, up_weight, up_bias, down_weight, down_bias,
):
    d = patches.shape[1]
    half = qkv_weight.shape[-1]
    section = lax.axis_index("section")
    lane = lax.axis_index("tensor")
    both = [(0, 1), (1, 0)]
    other = lambda array: lax.ppermute(array, "tensor", both)

    wqkv, pw, up, dn = qkv_weight[0], proj_weight[0], up_weight[0], down_weight[0]
    meta = jnp.concatenate([lane[None], large_place])
    xs = cut(patches, meta)
    bias = jnp.concatenate([qv_bias.reshape(1, 2 * half), up_bias], axis=1)
    bias_parts = after((bias, other(bias)), xs)
    w = {
        "g1": norm1_gain, "b1": norm1_bias, "g2": norm2_gain, "b2": norm2_bias,
        "pb": proj_bias, "db": down_bias,
        "wqkv_o": wqkv, "wqkv_p": other(wqkv), "pw_o": pw, "pw_p": other(pw),
        "up_o": up, "up_p": other(up), "dn_o": dn, "dn_p": other(dn),
        **dict(zip(("bias_o", "bias_p"), bias_parts)),
    }


    large, smalls = 0, 1
    gs = cut(out_grad, meta)

    def pick(on, make, otherwise=None):
        like = jax.eval_shape(make)
        return lax.cond(
            section == on,
            lambda: tuple(make()),
            lambda: blank(like) if otherwise is None else tuple(otherwise),
        )

    def fwd(c, on, x, otherwise=None):
        return pick(on, lambda: forward(x, w, CHUNKS[c]), otherwise)

    def bwd(c, on, g, x, kept, otherwise=None):
        kept = dict(zip(KEPT, kept))
        return pick(on, lambda: backward(g, x, kept, w, CHUNKS[c]), otherwise)

    down = lambda array: lax.ppermute(array, "section", [(0, 1)])
    up_ = lambda array: lax.ppermute(array, "section", [(1, 0)])

    kept_s = fwd(smalls, 0, xs[smalls])
    in_s = down(kept_s[-1])
    x_l = after(xs[large], kept_s[-1])
    kept_l = fwd(large, 0, x_l)
    in_l = down(kept_l[-1])
    in_s = after(in_s, kept_l[-1])
    kept_s = fwd(smalls, 1, in_s, kept_s)
    back_s = bwd(smalls, 1, gs[smalls], in_s, kept_s)
    sent_s = up_(back_s[-1])
    in_l = after(in_l, back_s[-1])
    kept_l = fwd(large, 1, in_l, kept_l)
    back_l = bwd(large, 1, gs[large], in_l, kept_l)
    sent_l = up_(back_l[-1])
    back_s = bwd(smalls, 0, after(sent_s, back_l[-1]), xs[smalls], kept_s, back_s)
    named = lambda names, values: dict(zip(names, values))
    part_mlp = wgrad_mlp(named(KEPT, kept_s), named(BACK, back_s))
    part_attn = wgrad_attn(named(KEPT, kept_s), named(BACK, back_s))
    outs = [kept_l[-1], kept_s[-1]]
    outputs = join(outs, [other(a) for a in outs], meta)
    sent_l = after(sent_l, part_mlp, part_attn, outputs)
    back_l = bwd(large, 0, sent_l, xs[large], kept_l, back_l)
    mlp = wgrad_mlp(named(KEPT, kept_l), named(BACK, back_l), part_mlp)
    grads = [back_l[-1], back_s[-1]]
    input_grads = join(grads, [other(a) for a in grads], meta)

    sums = lambda back: [named(BACK, back)[k] for k in ("sums1", "sums2", "sums_qkv", "sff")]
    summed, vec = dp_sum(
        mlp, named(KEPT, kept_l), named(BACK, back_l), part_attn, sums(back_s) + sums(back_l)
    )
    g_dn, g_up, g_qkv, g_pw, g1, b1, g2, b2, pb, db, qv, ub = finish(summed, vec)
    return (
        outputs[None], input_grads[None], g1, b1, g_qkv.reshape(1, 3, d, half), qv, g_pw, pb,
        g2, b2, g_up, ub, g_dn, db,
    )


def solution(mesh):
    placed = (
        P("dp", None), P("dp", None), P("dp"), P("section", None), P("section", None),
        P("section", None, None, "tensor"), P("section", None, "tensor"),
        P("section", "tensor", None), P("section", None), P("section", None),
        P("section", None), P("section", None, "tensor"), P("section", "tensor"),
        P("section", "tensor", None), P("section", None),
    )
    return jax.shard_map(
        body,
        mesh=mesh,
        in_specs=placed,
        out_specs=(
            P("section", "dp", None), P("section", "dp", None), P("section", None),
            P("section", None), P("section", None, None, "tensor"), P("section", None, "tensor"),
            P("section", "tensor", None), P("section", None), P("section", None),
            P("section", None), P("section", None, "tensor"), P("section", "tensor"),
            P("section", "tensor", None), P("section", None),
        ),
        check_vma=False,
    )
```

```python
import functools

import jax
import jax.numpy as jnp
from jax import lax
from jax.experimental import pallas as pl
from jax.experimental.pallas import tpu as pltpu
from jax.sharding import PartitionSpec as P

HD = 64
LEN_SMALL = 197
LEN_LARGE = 577
SMALL_MB = 3
EPSILON = 1e-06
MASKED = -1e30
SCALE = HD ** (-0.5)
SCALE2 = SCALE * 1.4426950408889634
BF = jnp.bfloat16
F32 = jnp.float32
VMEM_LIMIT = 56 * 1024 * 1024
CHUNKS = ((1, 592, LEN_LARGE), (SMALL_MB, 208, LEN_SMALL))


def params(limit=VMEM_LIMIT, **more):
    return pltpu.CompilerParams(vmem_limit_bytes=limit, **more)


def nn(a, b):
    return jnp.dot(a, b, preferred_element_type=F32)


def nt(a, b):
    return lax.dot_general(a, b, (((1,), (1,)), ((), ())), preferred_element_type=F32)


def tn(a, b):
    return lax.dot_general(a, b, (((0,), (0,)), ((), ())), preferred_element_type=F32)


def whole(shape):
    zeros = (0,) * len(shape)
    return pl.BlockSpec(shape, lambda *_: zeros)


def sds(shape, dtype):
    return jax.ShapeDtypeStruct(shape, dtype)


def norm_parts(values):
    mean = jnp.mean(values, axis=-1, keepdims=True)
    centred = values - mean
    rstd = lax.rsqrt(jnp.mean(centred * centred, axis=-1, keepdims=True) + EPSILON)
    return centred * rstd, rstd


def norm_back(xhat, rstd, grad, gain):
    scaled = grad * gain
    m1 = jnp.mean(scaled, axis=-1, keepdims=True)
    m2 = jnp.mean(scaled * xhat, axis=-1, keepdims=True)
    return rstd * (scaled - m1 - xhat * m2)


def rowsum(values):
    return jnp.sum(values.astype(F32), axis=0, keepdims=True)


def fetch(pairs, sems):
    return [pltpu.make_async_copy(src, dst, sems.at[i]) for i, (src, dst) in enumerate(pairs)]


def weight_loads(w, wq, pw, up, dn):
    wqo, wqp, pwo, pwp, upo, upp, dno, dnp = w
    half, fh = wqo.shape[-1], dno.shape[0]
    return {
        "qkv": [(wqo, wq.at[:, :, :half]), (wqp, wq.at[:, :, half:])],
        "proj": [(pwo, pw.at[:half]), (pwp, pw.at[half:])],
        "up": [(upo, up.at[:, :fh]), (upp, up.at[:, fh:])],
        "down": [(dno, dn.at[:fh]), (dnp, dn.at[fh:])],
    }


def weights_of(w):
    return [w[k] for k in ("wqkv_o", "wqkv_p", "pw_o", "pw_p", "up_o", "up_p", "dn_o", "dn_p")]


def weight_scratch(d, ff):
    return [
        pltpu.VMEM((3, d, d), BF), pltpu.VMEM((d, d), BF), pltpu.VMEM((d, ff), BF),
        pltpu.VMEM((ff, d), BF),
    ]


def lanes(at, width):
    return pl.ds(pl.multiple_of(at * width, width), width)


def mask_keys(scores, vlen):
    rows = scores.shape[0]
    keep = vlen // 8 * 8
    tail = scores[keep:]
    idx = lax.broadcasted_iota(jnp.int32, tail.shape, 0) + keep
    return jnp.concatenate([scores[:keep], jnp.where(idx < vlen, tail, MASKED)], axis=0)


def qblocks(plen):
    step = min(256, plen)
    return [(q, min(step, 2 * plen - q)) for q in range(0, 2 * plen, step)]


def lse_width(chunk):
    nimg, plen, _ = chunk
    return nimg * len(qblocks(plen)) * 256


def both_heads(rows):
    head = lax.broadcasted_iota(jnp.int32, rows.shape, 1) // HD
    none = jnp.zeros_like(rows)
    return jnp.concatenate([jnp.where(head == h, rows, none) for h in range(2)], axis=0)


def one_each(stacked, plen):
    head = lax.broadcasted_iota(jnp.int32, (plen, stacked.shape[1]), 1) // HD
    return jnp.where(head == 0, stacked[:plen], stacked[plen:])


def blocks_of(chunk):
    nimg, plen, _ = chunk
    return [(im, q0, qw) for im in range(nimg) for q0, qw in qblocks(plen)]


def attn_fwd_pair(p, qkv, att, lse, o_tmp, chunk):
    nimg, plen, vlen = chunk
    cols = lanes(p, 128)
    images = [slice(im * plen, (im + 1) * plen) for im in range(nimg)]
    k = [qkv[1, rows, cols] for rows in images]
    vt = [qkv[2, rows, cols].T for rows in images]
    queries = [both_heads(qkv[0, rows, cols]) for rows in images]
    blocks = blocks_of(chunk)
    scores = lambda im, q0, qw: nt(k[im], queries[im][q0 : q0 + qw])
    coming = scores(*blocks[0])
    for i, (im, q0, qw) in enumerate(blocks):
        st = mask_keys(coming, vlen)
        if i + 1 < len(blocks):
            coming = scores(*blocks[i + 1])
        top = jnp.max(st, axis=0, keepdims=True)
        e = jnp.exp2((st - top) * SCALE2)
        total = jnp.sum(e, axis=0, keepdims=True)
        o_tmp[q0 : q0 + qw] = (nn(vt[im], e.astype(BF)) * (1.0 / total)).T
        lse[p, :, i * 256 : i * 256 + qw] = top * SCALE2 + jnp.log2(total)
        if q0 + qw == 2 * plen:
            att[images[im], cols] = one_each(o_tmp, plen).astype(BF)


def gelu_parts(x):
    cdf = 0.5 + 0.5 * lax.erf(x * (2.0**-0.5))
    pdf = jnp.exp(-0.5 * x * x) * 0.3989422804014327
    return x * cdf, cdf + x * pdf


FF_STEPS = 2
WGRAD_STEPS = 4


def fwd_kernel(*refs, chunk):
    x_ref, g1, b1, own_bias, other_bias, pb, g2, b2, db = refs[:9]
    weights, outs = refs[9:17], refs[17:26]
    wq, pw, up, dn = refs[26:30]
    held = refs[30:39]
    acc, o_tmp, ub, in_sem, out_sem, ff_sem = refs[39:]
    normed, qkv, att, lse, mid, n2, act, dg, out = held
    ff = dn.shape[0]
    fb = ff // FF_STEPS
    loads = weight_loads(weights, wq, pw, up, dn)
    names = ("qkv", "proj", "up", "down")
    loads = {k: fetch(loads[k], in_sem.at[i]) for i, k in enumerate(names)}
    saves = fetch(list(zip(held[:6] + held[8:], outs[:6] + outs[8:])), out_sem)
    for c in loads["qkv"]:
        c.start()
    xhat, _ = norm_parts(x_ref[...].astype(F32))
    normed[...] = (xhat * g1[...] + b1[...]).astype(BF)
    saves[0].start()
    half = wq.shape[1] // 2

    def bias_of(first, last):
        return jnp.concatenate([own_bias[:, first:last], other_bias[:, first:last]], axis=1)

    q_bias, v_bias = bias_of(0, half), bias_of(half, 2 * half)
    ub[...] = bias_of(2 * half, own_bias.shape[1])
    for c in loads["qkv"]:
        c.wait()
    for k in names[1:]:
        for c in loads[k]:
            c.start()

    def project(s, carry):
        bias = jnp.where(s == 0, q_bias, jnp.where(s == 1, 0.0, v_bias))
        qkv[s] = (nn(normed[...], wq[s]) + bias).astype(BF)
        return carry

    lax.fori_loop(0, 3, project, 0)
    saves[1].start()

    def attend(p, carry):
        attn_fwd_pair(p, qkv, att, lse, o_tmp, chunk)
        return carry

    lax.fori_loop(0, lse.shape[0], attend, 0)
    saves[2].start()
    saves[3].start()
    for c in loads["proj"]:
        c.wait()
    middle = x_ref[...].astype(F32) + (nn(att[...], pw[...]) + pb[...])
    mid[...] = middle
    saves[4].start()
    xhat, _ = norm_parts(middle)
    n2[...] = (xhat * g2[...] + b2[...]).astype(BF)
    saves[5].start()
    acc[...] = middle + db[...]
    for k in ("up", "down"):
        for c in loads[k]:
            c.wait()

    def block_saves(j):
        cols = lanes(j, fb)
        pairs = [(act.at[:, cols], outs[6].at[:, cols]), (dg.at[:, cols], outs[7].at[:, cols])]
        return fetch(pairs, ff_sem.at[j])

    def mlp(j, carry):
        cols = lanes(j, fb)
        value, slope = gelu_parts(nn(n2[...], up[:, cols]) + ub[:, cols])
        value = value.astype(BF)
        act[:, cols] = value
        dg[:, cols] = slope.astype(BF)
        for c in block_saves(j):
            c.start()
        acc[...] += nn(value, dn[cols])
        return carry

    lax.fori_loop(0, FF_STEPS, mlp, 0)
    out[...] = acc[...].astype(BF)
    saves[6].start()
    for c in saves:
        c.wait()
    for j in range(FF_STEPS):
        for c in block_saves(j):
            c.wait()


def forward(x, w, chunk):
    n, d = x.shape
    ff = 2 * w["dn_o"].shape[0]
    pairs = d // 128
    kept = [
        ((n, d), BF), ((3, n, d), BF), ((n, d), BF), ((pairs, 1, lse_width(chunk)), F32),
        ((n, d), F32), ((n, d), BF), ((n, ff), BF), ((n, ff), BF), ((n, d), BF),
    ]
    vmem = pl.BlockSpec(memory_space=pltpu.VMEM)
    hbm = pl.BlockSpec(memory_space=pl.ANY)
    return pl.pallas_call(
        functools.partial(fwd_kernel, chunk=chunk),
        in_specs=[vmem] * 9 + [hbm] * 8,
        out_specs=[hbm] * len(kept),
        out_shape=[sds(*k) for k in kept],
        scratch_shapes=weight_scratch(d, ff)
        + [pltpu.VMEM(*k) for k in kept]
        + [
            pltpu.VMEM((n, d), F32), pltpu.VMEM((2 * chunk[1], 128), F32),
            pltpu.VMEM((1, ff), F32), pltpu.SemaphoreType.DMA((4, 2)),
            pltpu.SemaphoreType.DMA((7,)), pltpu.SemaphoreType.DMA((FF_STEPS, 2)),
        ],
        compiler_params=params(),
        name="fwd",
    )(
        x, w["g1"], w["b1"], w["bias_o"], w["bias_p"], w["pb"], w["g2"], w["b2"], w["db"],
        *weights_of(w),
    )


def attn_bwd_pair(p, qkv, att, gatt, lse, dqkv, sums, dq_tmp, chunk):
    nimg, plen, vlen = chunk
    cols = lanes(p, 128)
    images = [slice(im * plen, (im + 1) * plen) for im in range(nimg)]
    k = [qkv[1, rows, cols] for rows in images]
    v = [qkv[2, rows, cols] for rows in images]
    queries = [both_heads(qkv[0, rows, cols]) for rows in images]
    grads = [both_heads(gatt[rows, cols]) for rows in images]
    blocks = blocks_of(chunk)

    def scores(im, q0, qw):
        return nt(k[im], queries[im][q0 : q0 + qw]), nt(v[im], grads[im][q0 : q0 + qw])

    total_q, total_v = jnp.zeros((1, 128), F32), jnp.zeros((1, 128), F32)
    coming = scores(*blocks[0])
    for i, (im, q0, qw) in enumerate(blocks):
        rows = images[im]
        if q0 == 0:
            kt = k[im].T
            products = both_heads(gatt[rows, cols].astype(F32) * att[rows, cols].astype(F32))
            dk = jnp.zeros((plen, 128), F32)
            dv = jnp.zeros((plen, 128), F32)
        q = queries[im][q0 : q0 + qw]
        ga = grads[im][q0 : q0 + qw]
        st, gp = mask_keys(coming[0], vlen), coming[1]
        if i + 1 < len(blocks):
            coming = scores(*blocks[i + 1])
        pr = jnp.exp2(st * SCALE2 - lse[p, :, i * 256 : i * 256 + qw])
        dv += nn(pr.astype(BF), ga)
        delta = jnp.sum(products[q0 : q0 + qw].T, axis=0, keepdims=True)
        ds = (pr * (gp - delta)).astype(BF)
        dk += nn(ds, q)
        dq_tmp[q0 : q0 + qw] = nn(kt, ds).T
        if q0 + qw == 2 * plen:
            dq = (one_each(dq_tmp, plen) * SCALE).astype(BF)
            dvb = dv.astype(BF)
            dqkv[0, rows, cols] = dq
            dqkv[1, rows, cols] = (dk * SCALE).astype(BF)
            dqkv[2, rows, cols] = dvb
            total_q += rowsum(dq)
            total_v += rowsum(dvb)
    sums[:, cols] = jnp.concatenate(
        [total_q, jnp.zeros_like(total_q), total_v, jnp.zeros((5, 128), F32)], axis=0
    )


def bwd_kernel(*refs, chunk):
    g_ref, g2, g1 = refs[:3]
    mid_h, dg_h, qkv_h, lse_h, x_h, att_h = refs[3:9]
    weights, outs = refs[9:17], refs[17:22]
    sums2, sff, sums_qkv, sums1 = refs[22:26]
    wq, pw, up, dn = refs[26:30]
    mid, dg, qkv, lse, x, att, pre, gb, dqkv, gx, gm, ga, acc, dq_tmp, in_sem, late_sem, out_sem, ff_sem = refs[30:]
    ff = dn.shape[0]
    fb = ff // FF_STEPS
    loads = weight_loads(weights, wq, pw, up, dn)
    names = ("proj", "qkv")
    loads = {k: fetch(loads[k], in_sem.at[i]) for i, k in enumerate(names)}
    late = fetch([(mid_h, mid), (qkv_h, qkv), (lse_h, lse), (att_h, att), (x_h, x)], late_sem)
    saves = fetch(list(zip((pre, gb, dqkv, gx, g_ref), outs)), out_sem)

    def block_loads(j):
        if isinstance(j, int):
            owner, first = divmod(j * fb, ff // 2)
            rows = slice(first, first + fb)
            cols = slice(j * fb, (j + 1) * fb)
        else:
            owner, rows, cols = 0, slice(0, fb), lanes(j, fb)
        pairs = [
            (weights[6 + owner].at[rows], dn.at[cols]),
            (dg_h.at[:, cols], dg.at[:, cols]),
            (weights[4 + owner].at[:, rows], up.at[:, cols]),
        ]
        return fetch(pairs, ff_sem.at[j])

    for j in range(FF_STEPS):
        for c in block_loads(j):
            c.start()
    saves[4].start()
    for c in late:
        c.start()
    for k in ("proj", "qkv"):
        for c in loads[k]:
            c.start()
    acc[...] = jnp.zeros_like(acc)

    def mlp(j, carry):
        cols = lanes(j, fb)
        for c in block_loads(j):
            c.wait()
        value = (nt(g_ref[...], dn[cols]) * dg[:, cols].astype(F32)).astype(BF)
        pre[:, cols] = value
        sff[:, cols] = rowsum(value)
        acc[...] += nt(value, up[:, cols])
        return carry

    lax.fori_loop(0, FF_STEPS, mlp, 0)
    saves[0].start()
    late[0].wait()
    gn = acc[...]
    xhat, rstd = norm_parts(mid[...])
    grad = norm_back(xhat, rstd, gn, g2[...]) + g_ref[...].astype(F32)
    gm[...] = grad
    branch = grad.astype(BF)
    gb[...] = branch
    saves[1].start()
    sums2[...] = jnp.concatenate(
        [rowsum(gn * xhat), rowsum(gn), rowsum(branch), rowsum(g_ref[...])]
        + [jnp.zeros((4, gn.shape[1]), F32)], axis=0
    )
    for c in loads["proj"]:
        c.wait()
    ga[...] = nt(gb[...], pw[...]).astype(BF)
    for c in late[1:4]:
        c.wait()

    def attend(p, carry):
        attn_bwd_pair(p, qkv, att, ga, lse, dqkv, sums_qkv, dq_tmp, chunk)
        return carry

    lax.fori_loop(0, lse.shape[0], attend, 0)
    saves[2].start()
    for c in loads["qkv"]:
        c.wait()
    late[4].wait()
    acc[...] = nt(dqkv[0], wq[0])

    def project(s, carry):
        acc[...] += nt(dqkv[s], wq[s])
        return carry

    lax.fori_loop(1, 3, project, 0)
    gn = acc[...]
    xhat, rstd = norm_parts(x[...].astype(F32))
    gx[...] = (norm_back(xhat, rstd, gn, g1[...]) + gm[...]).astype(BF)
    saves[3].start()
    sums1[...] = jnp.concatenate(
        [rowsum(gn * xhat), rowsum(gn), jnp.zeros((6, gn.shape[1]), F32)], axis=0
    )
    for c in saves:
        c.wait()


def backward(g, x, kept, w, chunk):
    n, d = g.shape
    ff = kept["act"].shape[1]
    vmem = pl.BlockSpec(memory_space=pltpu.VMEM)
    hbm = pl.BlockSpec(memory_space=pl.ANY)
    wide, tall = ((n, d), BF), ((n, ff), BF)
    three, flat = ((3, n, d), BF), ((n, d), F32)
    lse = (kept["lse"].shape, F32)
    dma = pltpu.SemaphoreType.DMA
    pre, gb, dqkv, gx, copy, sums2, sff, sums_qkv, sums1 = pl.pallas_call(
        functools.partial(bwd_kernel, chunk=chunk),
        in_specs=[vmem] * 3 + [hbm] * 14,
        out_specs=[hbm] * 5 + [vmem] * 4,
        out_shape=[sds(*k) for k in (tall, wide, three, wide, wide)]
        + [sds((8, d), F32), sds((1, ff), F32), sds((8, d), F32), sds((8, d), F32)],
        scratch_shapes=weight_scratch(d, ff)
        + [
            pltpu.VMEM(*k)
            for k in (flat, tall, three, lse, wide, wide, tall, wide, three, wide, flat, wide, flat)
        ]
        + [pltpu.VMEM((2 * chunk[1], 128), F32), dma((2, 2)), dma((5,)), dma((5,)), dma((FF_STEPS, 3))],
        compiler_params=params(),
        name="bwd",
    )(
        g, w["g2"], w["g1"], kept["mid"], kept["dg"], kept["qkv"], kept["lse"], x, kept["att"], *weights_of(w)
    )
    return (copy, pre, gb, dqkv, sums2, sff, sums_qkv, sums1, gx)


def wgrad_mlp_kernel(act, n2, pre, g, *refs, more):
    init, outs = refs[:more], refs[more:]
    j = pl.program_id(0)
    down, up = tn(act[...], g[...]), tn(n2[...], pre[...])
    for i in range(2):

        @pl.when(j // (WGRAD_STEPS // 2) == i)
        def _():
            for at, value in ((i, down), (2 + i, up)):
                if more:
                    value = value + init[at][...].astype(F32)
                outs[at][...] = value.astype(BF)


def wgrad_mlp(kept, back, init=()):
    n, d = back["g"].shape
    ff = kept["act"].shape[1]
    fb, last = ff // WGRAD_STEPS, WGRAD_STEPS // 2 - 1
    cols = pl.BlockSpec((n, fb), lambda j: (0, j))
    at = [lambda j: jnp.minimum(j, last), lambda j: jnp.maximum(j - last - 1, 0)]
    outs = [pl.BlockSpec((fb, d), lambda j, i=i: (at[i](j), 0)) for i in range(2)]
    outs += [pl.BlockSpec((d, fb), lambda j, i=i: (0, at[i](j))) for i in range(2)]
    return pl.pallas_call(
        functools.partial(wgrad_mlp_kernel, more=len(init)),
        grid=(WGRAD_STEPS,),
        in_specs=[cols, whole((n, d)), cols, whole((n, d))] + outs[: len(init)],
        out_specs=outs,
        out_shape=[sds((ff // 2, d), BF)] * 2 + [sds((d, ff // 2), BF)] * 2,
        compiler_params=params(),
        name="wgrad_mlp",
    )(kept["act"], kept["n2"], back["pre"], back["g"], *init)


def wgrad_attn_kernel(*refs, more):
    normed, dqkv, att, gb = refs[:4]
    init = refs[4 : 4 + more]
    outs = refs[4 + more :]
    s = pl.program_id(0)
    total = tn(normed[...], dqkv[0])
    half = outs[0].shape[-1]
    for i, value in enumerate((total[:, :half], total[:, half:])):
        if more:
            value += init[i][0].astype(F32)
        outs[i][0] = value.astype(BF)
    for i in range(2):

        @pl.when(s == i)
        def _():
            value = tn(att[...], gb[...])
            if more:
                value += init[2 + i][...].astype(F32)
            outs[2 + i][...] = value.astype(BF)


def wgrad_attn(kept, back, init=()):
    n, d = kept["normed"].shape
    half = d // 2
    part = pl.BlockSpec((1, d, half), lambda s: (s, 0, 0))
    outs = [part, part, whole((half, d)), whole((half, d))]
    return pl.pallas_call(
        functools.partial(wgrad_attn_kernel, more=len(init)),
        grid=(3,),
        in_specs=[
            whole((n, d)), pl.BlockSpec((1, n, d), lambda s: (s, 0, 0)),
            pl.BlockSpec((n, half), lambda s: (0, jnp.minimum(s, 1))), whole((n, d)),
        ]
        + outs[: len(init)],
        out_specs=outs,
        out_shape=[sds((3, d, half), BF)] * 2 + [sds((half, d), BF)] * 2,
        compiler_params=params(),
        name="wgrad_attn",
    )(kept["normed"], back["dqkv"], kept["att"], back["gb"], *init)


RING = 8
VEC_ROWS = 16


def items_of(d):
    return ((0, 0, 2 * d, 1), (1, 0, d, -1), (2, 2 * d, d, -1), (2, 0, 2 * d, 1), (3, 0, d // 2, -1))


def vector_block(sums):
    s1, s2, sq, ff = sums
    d = s1.shape[1]
    wide = lambda v: [v[:, i : i + d] for i in range(0, v.shape[1], d)]
    rows = [s1[:2], s2[:4], sq[0:1], sq[2:3]] + wide(ff)
    used = 8 + ff.shape[1] // d
    return jnp.concatenate(rows + [jnp.zeros((VEC_ROWS - used, d), F32)], axis=0)


def as_own(block, fold):
    half = block.shape[1] // 2
    qv = block[6:8]
    return jnp.concatenate(
        [
            block[:6], jnp.concatenate([qv[:, half:], qv[:, :half]], axis=1),
            block[8 + fold : 8 + 2 * fold], block[8 : 8 + fold], block[8 + 2 * fold :],
        ],
        axis=0,
    )


def ring_kernel(*refs, n, items, fold):
    normed, dqkv, att, gb = refs[:4]
    parts, sums = refs[4:8], refs[12:20]
    at = 20
    results, vsum_ref = refs[at : at + n], refs[at + n]
    at += n + 1
    outs, theirs = refs[at : at + n], refs[at + n : at + 2 * n]
    at += 2 * n
    own_qkv, own_pw, gift_qkv, gift_pw = refs[at : at + 4]
    owns = refs[8:10] + (own_qkv, own_pw)
    gifts = refs[10:12] + (gift_qkv, gift_pw)
    at += 4
    m = len(items)
    slots = refs[at : at + m]
    vbuf, vother, vmine, vslot, send, recv, xsend, xrecv, flushed, vsend, vrecv, vxs, vxr = refs[
        at + m :
    ]
    mesh_id = pl.DeviceIdType.MESH
    me = lax.axis_index("dp")
    partner = {"tensor": 1 - lax.axis_index("tensor")}
    z, x = me // 2, me % 2
    pos = z + x * (RING - 1 - 2 * z)

    def member(p):
        p = p % RING
        return {"dp": 2 * p + (p // (RING // 2)) * (2 * RING - 1 - 4 * p)}

    barrier = pltpu.get_barrier_semaphore()
    for k in range(1, RING):
        pl.semaphore_signal(barrier, inc=1, device_id=member(pos + k), device_id_type=mesh_id)
    pl.semaphore_signal(barrier, inc=1, device_id=partner, device_id_type=mesh_id)
    pl.semaphore_wait(barrier, RING)

    def part(arrays, a, chunk):
        i, first, rows, _ = items[a]
        rows = rows // RING
        return arrays[i].at[pl.ds(pl.multiple_of(first + (chunk % RING) * rows, rows), rows)]

    def chunk_at(a, step):
        return pos + 2 * RING - items[a][3] * step

    def exchange(a, step):
        return pltpu.make_async_remote_copy(
            src_ref=part(gifts, a, chunk_at(a, step)),
            dst_ref=part(theirs, a, chunk_at(a, step)),
            send_sem=xsend.at[a, step],
            recv_sem=xrecv.at[a, step],
            device_id=partner,
            device_id_type=mesh_id,
        )

    def mine(a, step):
        exchange(a, step).wait_recv()
        chunk = chunk_at(a, step)
        return part(owns, a, chunk)[...].astype(F32) + part(theirs, a, chunk)[...].astype(F32)

    def remote(src, dst, a, step):
        return pltpu.make_async_remote_copy(
            src_ref=src,
            dst_ref=dst,
            send_sem=send.at[a, step],
            recv_sem=recv.at[a, step],
            device_id=member(pos + items[a][3] + RING),
            device_id_type=mesh_id,
        )

    def flush(a, k):
        chunk = chunk_at(a, k - 1)
        return pltpu.make_async_copy(
            part(outs, a, chunk), part(results, a, chunk), flushed.at[a, k]
        )

    def vcopy(k):
        return pltpu.make_async_remote_copy(
            src_ref=vmine,
            dst_ref=vslot.at[k - 1],
            send_sem=vsend.at[k - 1],
            recv_sem=vrecv.at[k - 1],
            device_id=member(pos + k),
            device_id_type=mesh_id,
        )

    vexchange = pltpu.make_async_remote_copy(
        src_ref=vbuf, dst_ref=vother, send_sem=vxs, recv_sem=vxr,
        device_id=partner, device_id_type=mesh_id,
    )

    def begin(arrays):
        for step in range(2):
            for a in arrays:
                exchange(a, step).start()
        for a in arrays:
            slots[a][0] = mine(a, 0).astype(BF)
            remote(slots[a].at[0], slots[a].at[1], a, 0).start()

    begin(range(2))
    vbuf[...] = vector_block([sums[i][...] + sums[4 + i][...] for i in range(4)])
    vexchange.start()
    d = normed.shape[1]
    half = d // 2
    for s in range(3):
        total = tn(normed[...], dqkv[s])
        rows = slice(s * d, (s + 1) * d)
        own_qkv[rows] = (total[:, :half] + parts[0][s].astype(F32)).astype(BF)
        gift_qkv[rows] = (total[:, half:] + parts[1][s].astype(F32)).astype(BF)
    own_pw[...] = (tn(att[:, :half], gb[...]) + parts[2][...].astype(F32)).astype(BF)
    gift_pw[...] = (tn(att[:, half:], gb[...]) + parts[3][...].astype(F32)).astype(BF)
    begin(range(2, m))

    def scatter(s, carry):
        for a in range(m):
            exchange(a, s + 1).start()
        for a in range(m):
            here = slots[a].at[s]
            own = mine(a, s)
            remote(here, here, a, s - 1).wait_recv()
            here[...] = (here[...].astype(F32) + own).astype(BF)
            remote(here, slots[a].at[s + 1], a, s).start()
        return carry

    lax.fori_loop(1, RING - 1, scatter, 0)
    vexchange.wait()
    vmine[...] = vbuf[...] + as_own(vother[...], fold)
    for k in range(1, RING):
        vcopy(k).start()
    for a in range(m):
        last = slots[a].at[RING - 1]
        own = mine(a, RING - 1)
        remote(last, last, a, RING - 2).wait_recv()
        done = part(outs, a, chunk_at(a, RING - 1))
        done[...] = (last[...].astype(F32) + own).astype(BF)
        remote(done, done, a, RING - 1).start()
        flush(a, 0).start()

    def gather(t, carry):
        for a in range(m):
            here = part(outs, a, chunk_at(a, t - 1))
            remote(here, here, a, RING - 2 + t).wait_recv()
            remote(here, here, a, RING - 1 + t).start()
            flush(a, t).start()
        return carry

    lax.fori_loop(1, RING - 1, gather, 0)
    total = vmine[...]
    for k in range(1, RING):
        vcopy(k).wait()
        total += vslot[k - 1]
    vsum_ref[...] = total
    for a in range(m):
        here = part(outs, a, chunk_at(a, RING - 2))
        remote(here, here, a, 2 * RING - 3).wait_recv()
        flush(a, RING - 1).start()
    for a in range(m):
        for s in range(RING - 1):
            remote(slots[a].at[0], slots[a].at[0], a, s).wait_send()
            here = part(outs, a, pos)
            remote(here, here, a, RING - 1 + s).wait_send()
        for s in range(RING):
            exchange(a, s).wait_send()
            flush(a, s).wait()


def ring(mlp, kept, back, parts, sums):
    d = kept["normed"].shape[1]
    shapes = [mlp[0].shape, mlp[2].shape, (3 * d, d // 2), (d // 2, d)]
    n = len(shapes)
    items = items_of(d)
    m = len(items)
    vmem = pl.BlockSpec(memory_space=pltpu.VMEM)
    hbm = pl.BlockSpec(memory_space=pl.ANY)
    dma = pltpu.SemaphoreType.DMA
    vec = pltpu.VMEM((VEC_ROWS, d), F32)
    out = pl.pallas_call(
        functools.partial(ring_kernel, n=n, items=items, fold=sums[3].shape[1] // (2 * d)),
        in_specs=[vmem] * 10 + [hbm] * 2 + [vmem] * 8,
        out_specs=[hbm] * n + [vmem],
        out_shape=[sds(a, BF) for a in shapes] + [sds((VEC_ROWS, d), F32)],
        scratch_shapes=[pltpu.VMEM(a, BF) for a in 2 * shapes + 2 * shapes[2:]]
        + [pltpu.VMEM((RING, rows // RING, shapes[i][1]), BF) for i, _, rows, _ in items]
        + [
            vec, vec, vec, pltpu.VMEM((RING - 1, VEC_ROWS, d), F32),
            dma((m, 2 * RING - 2)), dma((m, 2 * RING - 2)), dma((m, RING)), dma((m, RING)),
            dma((m, RING)),
            dma((RING - 1,)), dma((RING - 1,)), dma, dma,
        ],
        compiler_params=params(collective_id=1, has_side_effects=True),
        name="ring",
    )(
        kept["normed"], back["dqkv"], kept["att"], back["gb"], *parts, mlp[0], mlp[2], mlp[1],
        mlp[3], *sums,
    )
    return out[:n], out[n]


def dp_sum(mlp, kept, back, parts, sums):
    if lax.axis_size("dp") == RING:
        return ring(mlp, kept, back, parts, sums)
    other = lambda array: lax.ppermute(array, "tensor", [(0, 1), (1, 0)])
    qkv_o, qkv_p, pw_o, pw_p = wgrad_attn(kept, back, parts)
    rows = lambda qkv: qkv.reshape(-1, qkv.shape[2])
    owns = [mlp[0], mlp[2], rows(qkv_o), pw_o]
    gifts = [mlp[1], mlp[3], rows(qkv_p), pw_p]
    fold = sums[3].shape[1] // (2 * pw_o.shape[1])
    block = vector_block([a + b for a, b in zip(sums[:4], sums[4:])])
    summed = [lax.psum(a + other(b), "dp") for a, b in zip(owns, gifts)]
    return summed, lax.psum(block + as_own(other(block), fold), "dp")


def finish_kernel(*refs, fold):
    grads, vec, outs = refs[:4], refs[4], refs[5:]
    for g, out in zip(grads, outs):
        out[0] = g[...].astype(F32)

    @pl.when(pl.program_id(0) == 0)
    def _():
        half = vec.shape[1] // 2
        for i in range(6):
            outs[4 + i][...] = vec[i : i + 1]
        outs[10][0] = vec[6:8, :half]
        outs[11][...] = jnp.concatenate([vec[8 + i : 9 + i] for i in range(fold)], axis=1)


def finish(grads, vec):
    d = vec.shape[1]
    fold = grads[1].shape[1] // d
    steps = 8
    rows_in = lambda a: pl.BlockSpec((a.shape[0] // steps, a.shape[1]), lambda j: (j, 0))
    rows_out = lambda a: pl.BlockSpec((1, a.shape[0] // steps, a.shape[1]), lambda j: (0, j, 0))
    small = [(1, d)] * 6 + [(1, 2, d // 2), (1, fold * d)]
    return pl.pallas_call(
        functools.partial(finish_kernel, fold=fold),
        grid=(steps,),
        in_specs=[rows_in(a) for a in grads] + [whole(vec.shape)],
        out_specs=[rows_out(a) for a in grads] + [whole(a) for a in small],
        out_shape=[sds((1,) + a.shape, F32) for a in grads] + [sds(a, F32) for a in small],
        compiler_params=params(),
        name="finish",
    )(*grads, vec)


def starts_of(place):
    slots = [j + (j >= place) for j in range(SMALL_MB)]
    return [place * LEN_SMALL] + [
        slot * LEN_SMALL + (LEN_LARGE - LEN_SMALL) * (slot > place) for slot in slots
    ]


def layout(place):
    at = 0
    starts = starts_of(place)
    for c, (nimg, plen, vlen) in enumerate(CHUNKS):
        for i in range(nimg):
            yield starts[at], c, i * plen, plen, vlen
            at += 1


def cut_kernel(meta_ref, x_ref, *refs):
    outs, flat = refs[:-1], refs[-1]
    rows = x_ref.shape[0]
    flat[:rows] = x_ref[...].astype(F32)
    flat[rows:] = jnp.zeros((flat.shape[0] - rows, flat.shape[1]), F32)
    for place in range(SMALL_MB + 1):

        @pl.when(meta_ref[1 + meta_ref[0]] == place)
        def _():
            for start, c, r0, plen, vlen in layout(place):
                value = flat[start : start + plen]
                row = lax.broadcasted_iota(jnp.int32, value.shape, 0)
                outs[c][r0 : r0 + plen] = jnp.where(row < vlen, value, 0.0).astype(BF)


def cut(array, meta):
    rows = LEN_LARGE + SMALL_MB * LEN_SMALL
    d = array.shape[1]
    block = d // 3
    return pl.pallas_call(
        cut_kernel,
        grid_spec=pltpu.PrefetchScalarGridSpec(
            num_scalar_prefetch=1,
            grid=(3,),
            in_specs=[pl.BlockSpec((rows, block), lambda j, m: (m[0], j))],
            out_specs=[pl.BlockSpec((k * p, block), lambda j, m: (0, j)) for k, p, _ in CHUNKS],
            scratch_shapes=[pltpu.VMEM((rows + 16, block), F32)],
        ),
        out_shape=[sds((k * p, d), BF) for k, p, _ in CHUNKS],
        compiler_params=params(),
        name="cut",
    )(meta, array)


def join_kernel(meta_ref, *refs):
    count = len(CHUNKS)
    mine, theirs, out_ref, flat = refs[:count], refs[count : 2 * count], refs[-2], refs[-1]
    rows = flat.shape[0]
    for lane in range(2):
        for place in range(SMALL_MB + 1):
            for own, source in ((True, mine), (False, theirs)):

                @pl.when((meta_ref[1 + lane] == place) & ((meta_ref[0] == lane) == own))
                def _():
                    for start, c, r0, plen, vlen in layout(place):
                        value = source[c][r0 : r0 + plen].astype(F32)
                        flat[start : start + vlen] = value[:vlen]

        out_ref[lane * rows : (lane + 1) * rows] = flat[...].astype(BF)


def join(mine, theirs, meta):
    rows = LEN_LARGE + SMALL_MB * LEN_SMALL
    d = mine[0].shape[1]
    block = d // 3
    return pl.pallas_call(
        join_kernel,
        grid_spec=pltpu.PrefetchScalarGridSpec(
            num_scalar_prefetch=1,
            grid=(3,),
            in_specs=[pl.BlockSpec((k * p, block), lambda j, m: (0, j)) for k, p, _ in CHUNKS] * 2,
            out_specs=pl.BlockSpec((2 * rows, block), lambda j, m: (0, j)),
            scratch_shapes=[pltpu.VMEM((rows, block), F32)],
        ),
        out_shape=sds((2 * rows, d), BF),
        compiler_params=params(),
        name="join",
    )(meta, *mine, *theirs)


def blank_kernel(*refs):
    pass


def blank(like):
    shapes = [sds(a.shape, a.dtype) for a in like]
    return tuple(
        pl.pallas_call(
            blank_kernel,
            out_shape=shapes,
            out_specs=[pl.BlockSpec(memory_space=pl.ANY) for _ in shapes],
            name="blank",
        )()
    )


KEPT = ("normed", "qkv", "att", "lse", "mid", "n2", "act", "dg", "out")
BACK = ("g", "pre", "gb", "dqkv", "sums2", "sff", "sums_qkv", "sums1", "gx")


def after(value, *earlier):
    return lax.optimization_barrier((value, earlier))[0]


def body(
    patches, out_grad, large_place, norm1_gain, norm1_bias, qkv_weight, qv_bias, proj_weight,
    proj_bias, norm2_gain, norm2_bias, up_weight, up_bias, down_weight, down_bias,
):
    d = patches.shape[1]
    half = qkv_weight.shape[-1]
    section = lax.axis_index("section")
    lane = lax.axis_index("tensor")
    both = [(0, 1), (1, 0)]
    other = lambda array: lax.ppermute(array, "tensor", both)

    wqkv, pw, up, dn = qkv_weight[0], proj_weight[0], up_weight[0], down_weight[0]
    meta = jnp.concatenate([lane[None], large_place])
    xs = cut(patches, meta)
    bias = jnp.concatenate([qv_bias.reshape(1, 2 * half), up_bias], axis=1)
    bias_parts = after((bias, other(bias)), xs)
    w = {
        "g1": norm1_gain, "b1": norm1_bias, "g2": norm2_gain, "b2": norm2_bias,
        "pb": proj_bias, "db": down_bias,
        "wqkv_o": wqkv, "wqkv_p": other(wqkv), "pw_o": pw, "pw_p": other(pw),
        "up_o": up, "up_p": other(up), "dn_o": dn, "dn_p": other(dn),
        **dict(zip(("bias_o", "bias_p"), bias_parts)),
    }


    large, smalls = 0, 1
    gs = cut(out_grad, meta)

    def pick(on, make, otherwise=None):
        like = jax.eval_shape(make)
        return lax.cond(
            section == on,
            lambda: tuple(make()),
            lambda: blank(like) if otherwise is None else tuple(otherwise),
        )

    def fwd(c, on, x, otherwise=None):
        return pick(on, lambda: forward(x, w, CHUNKS[c]), otherwise)

    def bwd(c, on, g, x, kept, otherwise=None):
        kept = dict(zip(KEPT, kept))
        return pick(on, lambda: backward(g, x, kept, w, CHUNKS[c]), otherwise)

    down = lambda array: lax.ppermute(array, "section", [(0, 1)])
    up_ = lambda array: lax.ppermute(array, "section", [(1, 0)])

    kept_s = fwd(smalls, 0, xs[smalls])
    in_s = down(kept_s[-1])
    x_l = after(xs[large], kept_s[-1])
    kept_l = fwd(large, 0, x_l)
    in_l = down(kept_l[-1])
    in_s = after(in_s, kept_l[-1])
    kept_s = fwd(smalls, 1, in_s, kept_s)
    back_s = bwd(smalls, 1, gs[smalls], in_s, kept_s)
    sent_s = up_(back_s[-1])
    in_l = after(in_l, back_s[-1])
    kept_l = fwd(large, 1, in_l, kept_l)
    back_l = bwd(large, 1, gs[large], in_l, kept_l)
    sent_l = up_(back_l[-1])
    back_s = bwd(smalls, 0, after(sent_s, back_l[-1]), xs[smalls], kept_s, back_s)
    named = lambda names, values: dict(zip(names, values))
    part_mlp = wgrad_mlp(named(KEPT, kept_s), named(BACK, back_s))
    part_attn = wgrad_attn(named(KEPT, kept_s), named(BACK, back_s))
    outs = [kept_l[-1], kept_s[-1]]
    outputs = join(outs, [other(a) for a in outs], meta)
    sent_l = after(sent_l, part_mlp, part_attn, outputs)
    back_l = bwd(large, 0, sent_l, xs[large], kept_l, back_l)
    mlp = wgrad_mlp(named(KEPT, kept_l), named(BACK, back_l), part_mlp)
    grads = [back_l[-1], back_s[-1]]
    input_grads = join(grads, [other(a) for a in grads], meta)

    sums = lambda back: [named(BACK, back)[k] for k in ("sums1", "sums2", "sums_qkv", "sff")]
    summed, vec = dp_sum(
        mlp, named(KEPT, kept_l), named(BACK, back_l), part_attn, sums(back_s) + sums(back_l)
    )
    g_dn, g_up, g_qkv, g_pw, g1, b1, g2, b2, pb, db, qv, ub = finish(summed, vec)
    return (
        outputs[None], input_grads[None], g1, b1, g_qkv.reshape(1, 3, d, half), qv, g_pw, pb,
        g2, b2, g_up, ub, g_dn, db,
    )


def solution(mesh):
    placed = (
        P("dp", None), P("dp", None), P("dp"), P("section", None), P("section", None),
        P("section", None, None, "tensor"), P("section", None, "tensor"),
        P("section", "tensor", None), P("section", None), P("section", None),
        P("section", None), P("section", None, "tensor"), P("section", "tensor"),
        P("section", "tensor", None), P("section", None),
    )
    return jax.shard_map(
        body,
        mesh=mesh,
        in_specs=placed,
        out_specs=(
            P("section", "dp", None), P("section", "dp", None), P("section", None),
            P("section", None), P("section", None, None, "tensor"), P("section", None, "tensor"),
            P("section", "tensor", None), P("section", None), P("section", None),
            P("section", None), P("section", None, "tensor"), P("section", "tensor"),
            P("section", "tensor", None), P("section", None),
        ),
        check_vma=False,
    )
```

```python
import functools

import jax
import jax.numpy as jnp
from jax import lax
from jax.experimental import pallas as pl
from jax.experimental.pallas import tpu as pltpu
from jax.sharding import PartitionSpec as P

HD = 64
LEN_SMALL = 197
LEN_LARGE = 577
SMALL_MB = 3
EPSILON = 1e-06
MASKED = -1e30
SCALE = HD ** (-0.5)
SCALE2 = SCALE * 1.4426950408889634
BF = jnp.bfloat16
F32 = jnp.float32
VMEM_LIMIT = 56 * 1024 * 1024
CHUNKS = ((1, 592, LEN_LARGE), (SMALL_MB, 208, LEN_SMALL))


def params(limit=VMEM_LIMIT, **more):
    return pltpu.CompilerParams(vmem_limit_bytes=limit, **more)


def nn(a, b):
    return jnp.dot(a, b, preferred_element_type=F32)


def nt(a, b):
    return lax.dot_general(a, b, (((1,), (1,)), ((), ())), preferred_element_type=F32)


def tn(a, b):
    return lax.dot_general(a, b, (((0,), (0,)), ((), ())), preferred_element_type=F32)


def whole(shape):
    zeros = (0,) * len(shape)
    return pl.BlockSpec(shape, lambda *_: zeros)


def sds(shape, dtype):
    return jax.ShapeDtypeStruct(shape, dtype)


def norm_parts(values):
    mean = jnp.mean(values, axis=-1, keepdims=True)
    centred = values - mean
    rstd = lax.rsqrt(jnp.mean(centred * centred, axis=-1, keepdims=True) + EPSILON)
    return centred * rstd, rstd


def norm_back(xhat, rstd, grad, gain):
    scaled = grad * gain
    m1 = jnp.mean(scaled, axis=-1, keepdims=True)
    m2 = jnp.mean(scaled * xhat, axis=-1, keepdims=True)
    return rstd * (scaled - m1 - xhat * m2)


def rowsum(values):
    return jnp.sum(values.astype(F32), axis=0, keepdims=True)


def fetch(pairs, sems):
    return [pltpu.make_async_copy(src, dst, sems.at[i]) for i, (src, dst) in enumerate(pairs)]


def weight_loads(w, wq, pw, up, dn):
    wqo, wqp, pwo, pwp, upo, upp, dno, dnp = w
    half, fh = wqo.shape[-1], dno.shape[0]
    return {
        "qkv": [(wqo, wq.at[:, :, :half]), (wqp, wq.at[:, :, half:])],
        "proj": [(pwo, pw.at[:half]), (pwp, pw.at[half:])],
        "up": [(upo, up.at[:, :fh]), (upp, up.at[:, fh:])],
        "down": [(dno, dn.at[:fh]), (dnp, dn.at[fh:])],
    }


def weights_of(w):
    return [w[k] for k in ("wqkv_o", "wqkv_p", "pw_o", "pw_p", "up_o", "up_p", "dn_o", "dn_p")]


def weight_scratch(d, ff):
    return [
        pltpu.VMEM((3, d, d), BF), pltpu.VMEM((d, d), BF), pltpu.VMEM((d, ff), BF),
        pltpu.VMEM((ff, d), BF),
    ]


def lanes(at, width):
    return pl.ds(pl.multiple_of(at * width, width), width)


def mask_keys(scores, vlen):
    rows = scores.shape[0]
    keep = vlen // 8 * 8
    tail = scores[keep:]
    idx = lax.broadcasted_iota(jnp.int32, tail.shape, 0) + keep
    return jnp.concatenate([scores[:keep], jnp.where(idx < vlen, tail, MASKED)], axis=0)


def qblocks(plen):
    step = min(256, plen)
    return [(q, min(step, 2 * plen - q)) for q in range(0, 2 * plen, step)]


def lse_width(chunk):
    nimg, plen, _ = chunk
    return nimg * len(qblocks(plen)) * 256


def both_heads(rows):
    head = lax.broadcasted_iota(jnp.int32, rows.shape, 1) // HD
    none = jnp.zeros_like(rows)
    return jnp.concatenate([jnp.where(head == h, rows, none) for h in range(2)], axis=0)


def one_each(stacked, plen):
    head = lax.broadcasted_iota(jnp.int32, (plen, stacked.shape[1]), 1) // HD
    return jnp.where(head == 0, stacked[:plen], stacked[plen:])


def blocks_of(chunk):
    nimg, plen, _ = chunk
    return [(im, q0, qw) for im in range(nimg) for q0, qw in qblocks(plen)]


def attn_fwd_pair(p, qkv, att, lse, o_tmp, chunk):
    nimg, plen, vlen = chunk
    cols = lanes(p, 128)
    images = [slice(im * plen, (im + 1) * plen) for im in range(nimg)]
    k = [qkv[1, rows, cols] for rows in images]
    vt = [qkv[2, rows, cols].T for rows in images]
    queries = [both_heads(qkv[0, rows, cols]) for rows in images]
    blocks = blocks_of(chunk)
    scores = lambda im, q0, qw: nt(k[im], queries[im][q0 : q0 + qw])
    coming = scores(*blocks[0])
    for i, (im, q0, qw) in enumerate(blocks):
        st = mask_keys(coming, vlen)
        if i + 1 < len(blocks):
            coming = scores(*blocks[i + 1])
        top = jnp.max(st, axis=0, keepdims=True)
        e = jnp.exp2((st - top) * SCALE2)
        total = jnp.sum(e, axis=0, keepdims=True)
        o_tmp[q0 : q0 + qw] = (nn(vt[im], e.astype(BF)) * (1.0 / total)).T
        lse[p, :, i * 256 : i * 256 + qw] = top * SCALE2 + jnp.log2(total)
        if q0 + qw == 2 * plen:
            att[images[im], cols] = one_each(o_tmp, plen).astype(BF)


def gelu_parts(x):
    cdf = 0.5 + 0.5 * lax.erf(x * (2.0**-0.5))
    pdf = jnp.exp(-0.5 * x * x) * 0.3989422804014327
    return x * cdf, cdf + x * pdf


FF_STEPS = 2
WGRAD_STEPS = 4


def fwd_kernel(*refs, chunk):
    x_ref, g1, b1, own_bias, other_bias, pb, g2, b2, db = refs[:9]
    weights, outs = refs[9:17], refs[17:26]
    wq, pw, up, dn = refs[26:30]
    held = refs[30:39]
    acc, o_tmp, ub, in_sem, out_sem, ff_sem = refs[39:]
    normed, qkv, att, lse, mid, n2, act, dg, out = held
    ff = dn.shape[0]
    fb = ff // FF_STEPS
    loads = weight_loads(weights, wq, pw, up, dn)
    names = ("qkv", "proj", "up", "down")
    loads = {k: fetch(loads[k], in_sem.at[i]) for i, k in enumerate(names)}
    saves = fetch(list(zip(held[:6] + held[8:], outs[:6] + outs[8:])), out_sem)
    for c in loads["qkv"]:
        c.start()
    xhat, _ = norm_parts(x_ref[...].astype(F32))
    normed[...] = (xhat * g1[...] + b1[...]).astype(BF)
    saves[0].start()
    half = wq.shape[1] // 2

    def bias_of(first, last):
        return jnp.concatenate([own_bias[:, first:last], other_bias[:, first:last]], axis=1)

    q_bias, v_bias = bias_of(0, half), bias_of(half, 2 * half)
    ub[...] = bias_of(2 * half, own_bias.shape[1])
    for c in loads["qkv"]:
        c.wait()
    for k in names[1:]:
        for c in loads[k]:
            c.start()

    def project(s, carry):
        bias = jnp.where(s == 0, q_bias, jnp.where(s == 1, 0.0, v_bias))
        qkv[s] = (nn(normed[...], wq[s]) + bias).astype(BF)
        return carry

    lax.fori_loop(0, 3, project, 0)
    saves[1].start()

    def attend(p, carry):
        attn_fwd_pair(p, qkv, att, lse, o_tmp, chunk)
        return carry

    lax.fori_loop(0, lse.shape[0], attend, 0)
    saves[2].start()
    saves[3].start()
    for c in loads["proj"]:
        c.wait()
    middle = x_ref[...].astype(F32) + (nn(att[...], pw[...]) + pb[...])
    mid[...] = middle
    saves[4].start()
    xhat, _ = norm_parts(middle)
    n2[...] = (xhat * g2[...] + b2[...]).astype(BF)
    saves[5].start()
    acc[...] = middle + db[...]
    for k in ("up", "down"):
        for c in loads[k]:
            c.wait()

    def block_saves(j):
        cols = lanes(j, fb)
        pairs = [(act.at[:, cols], outs[6].at[:, cols]), (dg.at[:, cols], outs[7].at[:, cols])]
        return fetch(pairs, ff_sem.at[j])

    def mlp(j, carry):
        cols = lanes(j, fb)
        value, slope = gelu_parts(nn(n2[...], up[:, cols]) + ub[:, cols])
        value = value.astype(BF)
        act[:, cols] = value
        dg[:, cols] = slope.astype(BF)
        for c in block_saves(j):
            c.start()
        acc[...] += nn(value, dn[cols])
        return carry

    lax.fori_loop(0, FF_STEPS, mlp, 0)
    out[...] = acc[...].astype(BF)
    saves[6].start()
    for c in saves:
        c.wait()
    for j in range(FF_STEPS):
        for c in block_saves(j):
            c.wait()


def forward(x, w, chunk):
    n, d = x.shape
    ff = 2 * w["dn_o"].shape[0]
    pairs = d // 128
    kept = [
        ((n, d), BF), ((3, n, d), BF), ((n, d), BF), ((pairs, 1, lse_width(chunk)), F32),
        ((n, d), F32), ((n, d), BF), ((n, ff), BF), ((n, ff), BF), ((n, d), BF),
    ]
    vmem = pl.BlockSpec(memory_space=pltpu.VMEM)
    hbm = pl.BlockSpec(memory_space=pl.ANY)
    return pl.pallas_call(
        functools.partial(fwd_kernel, chunk=chunk),
        in_specs=[vmem] * 9 + [hbm] * 8,
        out_specs=[hbm] * len(kept),
        out_shape=[sds(*k) for k in kept],
        scratch_shapes=weight_scratch(d, ff)
        + [pltpu.VMEM(*k) for k in kept]
        + [
            pltpu.VMEM((n, d), F32), pltpu.VMEM((2 * chunk[1], 128), F32),
            pltpu.VMEM((1, ff), F32), pltpu.SemaphoreType.DMA((4, 2)),
            pltpu.SemaphoreType.DMA((7,)), pltpu.SemaphoreType.DMA((FF_STEPS, 2)),
        ],
        compiler_params=params(),
        name="fwd",
    )(
        x, w["g1"], w["b1"], w["bias_o"], w["bias_p"], w["pb"], w["g2"], w["b2"], w["db"],
        *weights_of(w),
    )


def attn_bwd_pair(p, qkv, att, gatt, lse, dqkv, sums, dq_tmp, chunk):
    nimg, plen, vlen = chunk
    cols = lanes(p, 128)
    images = [slice(im * plen, (im + 1) * plen) for im in range(nimg)]
    k = [qkv[1, rows, cols] for rows in images]
    v = [qkv[2, rows, cols] for rows in images]
    queries = [both_heads(qkv[0, rows, cols]) for rows in images]
    grads = [both_heads(gatt[rows, cols]) for rows in images]
    blocks = blocks_of(chunk)

    def scores(im, q0, qw):
        return nt(k[im], queries[im][q0 : q0 + qw]), nt(v[im], grads[im][q0 : q0 + qw])

    total_q, total_v = jnp.zeros((1, 128), F32), jnp.zeros((1, 128), F32)
    coming = scores(*blocks[0])
    for i, (im, q0, qw) in enumerate(blocks):
        rows = images[im]
        if q0 == 0:
            kt = k[im].T
            products = both_heads(gatt[rows, cols].astype(F32) * att[rows, cols].astype(F32))
            dk = jnp.zeros((plen, 128), F32)
            dv = jnp.zeros((plen, 128), F32)
        q = queries[im][q0 : q0 + qw]
        ga = grads[im][q0 : q0 + qw]
        st, gp = mask_keys(coming[0], vlen), coming[1]
        if i + 1 < len(blocks):
            coming = scores(*blocks[i + 1])
        pr = jnp.exp2(st * SCALE2 - lse[p, :, i * 256 : i * 256 + qw])
        dv += nn(pr.astype(BF), ga)
        delta = jnp.sum(products[q0 : q0 + qw].T, axis=0, keepdims=True)
        ds = (pr * (gp - delta)).astype(BF)
        dk += nn(ds, q)
        dq_tmp[q0 : q0 + qw] = nn(kt, ds).T
        if q0 + qw == 2 * plen:
            dq = (one_each(dq_tmp, plen) * SCALE).astype(BF)
            dvb = dv.astype(BF)
            dqkv[0, rows, cols] = dq
            dqkv[1, rows, cols] = (dk * SCALE).astype(BF)
            dqkv[2, rows, cols] = dvb
            total_q += rowsum(dq)
            total_v += rowsum(dvb)
    sums[:, cols] = jnp.concatenate(
        [total_q, jnp.zeros_like(total_q), total_v, jnp.zeros((5, 128), F32)], axis=0
    )


def bwd_kernel(*refs, chunk):
    g_ref, g2, g1 = refs[:3]
    mid_h, dg_h, qkv_h, lse_h, x_h, att_h = refs[3:9]
    weights, outs = refs[9:17], refs[17:22]
    sums2, sff, sums_qkv, sums1 = refs[22:26]
    wq, pw, up, dn = refs[26:30]
    mid, dg, qkv, lse, x, att, pre, gb, dqkv, gx, gm, ga, acc, dq_tmp, in_sem, late_sem, out_sem, ff_sem = refs[30:]
    ff = dn.shape[0]
    fb = ff // FF_STEPS
    loads = weight_loads(weights, wq, pw, up, dn)
    names = ("proj", "qkv")
    loads = {k: fetch(loads[k], in_sem.at[i]) for i, k in enumerate(names)}
    late = fetch([(mid_h, mid), (qkv_h, qkv), (lse_h, lse), (att_h, att), (x_h, x)], late_sem)
    saves = fetch(list(zip((pre, gb, dqkv, gx, g_ref), outs)), out_sem)

    def block_loads(j):
        if isinstance(j, int):
            owner, first = divmod(j * fb, ff // 2)
            rows = slice(first, first + fb)
            cols = slice(j * fb, (j + 1) * fb)
        else:
            owner, rows, cols = 0, slice(0, fb), lanes(j, fb)
        pairs = [
            (weights[6 + owner].at[rows], dn.at[cols]),
            (dg_h.at[:, cols], dg.at[:, cols]),
            (weights[4 + owner].at[:, rows], up.at[:, cols]),
        ]
        return fetch(pairs, ff_sem.at[j])

    for j in range(FF_STEPS):
        for c in block_loads(j):
            c.start()
    saves[4].start()
    for c in late:
        c.start()
    for k in ("proj", "qkv"):
        for c in loads[k]:
            c.start()
    acc[...] = jnp.zeros_like(acc)

    def mlp(j, carry):
        cols = lanes(j, fb)
        for c in block_loads(j):
            c.wait()
        value = (nt(g_ref[...], dn[cols]) * dg[:, cols].astype(F32)).astype(BF)
        pre[:, cols] = value
        sff[:, cols] = rowsum(value)
        acc[...] += nt(value, up[:, cols])
        return carry

    lax.fori_loop(0, FF_STEPS, mlp, 0)
    saves[0].start()
    late[0].wait()
    gn = acc[...]
    xhat, rstd = norm_parts(mid[...])
    grad = norm_back(xhat, rstd, gn, g2[...]) + g_ref[...].astype(F32)
    gm[...] = grad
    branch = grad.astype(BF)
    gb[...] = branch
    saves[1].start()
    sums2[...] = jnp.concatenate(
        [rowsum(gn * xhat), rowsum(gn), rowsum(branch), rowsum(g_ref[...])]
        + [jnp.zeros((4, gn.shape[1]), F32)], axis=0
    )
    for c in loads["proj"]:
        c.wait()
    ga[...] = nt(gb[...], pw[...]).astype(BF)
    for c in late[1:4]:
        c.wait()

    def attend(p, carry):
        attn_bwd_pair(p, qkv, att, ga, lse, dqkv, sums_qkv, dq_tmp, chunk)
        return carry

    lax.fori_loop(0, lse.shape[0], attend, 0)
    saves[2].start()
    for c in loads["qkv"]:
        c.wait()
    late[4].wait()
    acc[...] = nt(dqkv[0], wq[0])

    def project(s, carry):
        acc[...] += nt(dqkv[s], wq[s])
        return carry

    lax.fori_loop(1, 3, project, 0)
    gn = acc[...]
    xhat, rstd = norm_parts(x[...].astype(F32))
    gx[...] = (norm_back(xhat, rstd, gn, g1[...]) + gm[...]).astype(BF)
    saves[3].start()
    sums1[...] = jnp.concatenate(
        [rowsum(gn * xhat), rowsum(gn), jnp.zeros((6, gn.shape[1]), F32)], axis=0
    )
    for c in saves:
        c.wait()


def backward(g, x, kept, w, chunk):
    n, d = g.shape
    ff = kept["act"].shape[1]
    vmem = pl.BlockSpec(memory_space=pltpu.VMEM)
    hbm = pl.BlockSpec(memory_space=pl.ANY)
    wide, tall = ((n, d), BF), ((n, ff), BF)
    three, flat = ((3, n, d), BF), ((n, d), F32)
    lse = (kept["lse"].shape, F32)
    dma = pltpu.SemaphoreType.DMA
    pre, gb, dqkv, gx, copy, sums2, sff, sums_qkv, sums1 = pl.pallas_call(
        functools.partial(bwd_kernel, chunk=chunk),
        in_specs=[vmem] * 3 + [hbm] * 14,
        out_specs=[hbm] * 5 + [vmem] * 4,
        out_shape=[sds(*k) for k in (tall, wide, three, wide, wide)]
        + [sds((8, d), F32), sds((1, ff), F32), sds((8, d), F32), sds((8, d), F32)],
        scratch_shapes=weight_scratch(d, ff)
        + [
            pltpu.VMEM(*k)
            for k in (flat, tall, three, lse, wide, wide, tall, wide, three, wide, flat, wide, flat)
        ]
        + [pltpu.VMEM((2 * chunk[1], 128), F32), dma((2, 2)), dma((5,)), dma((5,)), dma((FF_STEPS, 3))],
        compiler_params=params(),
        name="bwd",
    )(
        g, w["g2"], w["g1"], kept["mid"], kept["dg"], kept["qkv"], kept["lse"], x, kept["att"], *weights_of(w)
    )
    return (copy, pre, gb, dqkv, sums2, sff, sums_qkv, sums1, gx)


def wgrad_mlp_kernel(act, n2, pre, g, *refs, more):
    init, outs = refs[:more], refs[more:]
    j = pl.program_id(0)
    down, up = tn(act[...], g[...]), tn(n2[...], pre[...])
    for i in range(2):

        @pl.when(j // (WGRAD_STEPS // 2) == i)
        def _():
            for at, value in ((i, down), (2 + i, up)):
                if more:
                    value = value + init[at][...].astype(F32)
                outs[at][...] = value.astype(BF)


def wgrad_mlp(kept, back, init=()):
    n, d = back["g"].shape
    ff = kept["act"].shape[1]
    fb, last = ff // WGRAD_STEPS, WGRAD_STEPS // 2 - 1
    cols = pl.BlockSpec((n, fb), lambda j: (0, j))
    at = [lambda j: jnp.minimum(j, last), lambda j: jnp.maximum(j - last - 1, 0)]
    outs = [pl.BlockSpec((fb, d), lambda j, i=i: (at[i](j), 0)) for i in range(2)]
    outs += [pl.BlockSpec((d, fb), lambda j, i=i: (0, at[i](j))) for i in range(2)]
    return pl.pallas_call(
        functools.partial(wgrad_mlp_kernel, more=len(init)),
        grid=(WGRAD_STEPS,),
        in_specs=[cols, whole((n, d)), cols, whole((n, d))] + outs[: len(init)],
        out_specs=outs,
        out_shape=[sds((ff // 2, d), BF)] * 2 + [sds((d, ff // 2), BF)] * 2,
        compiler_params=params(),
        name="wgrad_mlp",
    )(kept["act"], kept["n2"], back["pre"], back["g"], *init)


def wgrad_attn_kernel(*refs, more):
    normed, dqkv, att, gb = refs[:4]
    init = refs[4 : 4 + more]
    outs = refs[4 + more :]
    s = pl.program_id(0)
    total = tn(normed[...], dqkv[0])
    half = outs[0].shape[-1]
    for i, value in enumerate((total[:, :half], total[:, half:])):
        if more:
            value += init[i][0].astype(F32)
        outs[i][0] = value.astype(BF)
    for i in range(2):

        @pl.when(s == i)
        def _():
            value = tn(att[...], gb[...])
            if more:
                value += init[2 + i][...].astype(F32)
            outs[2 + i][...] = value.astype(BF)


def wgrad_attn(kept, back, init=()):
    n, d = kept["normed"].shape
    half = d // 2
    part = pl.BlockSpec((1, d, half), lambda s: (s, 0, 0))
    outs = [part, part, whole((half, d)), whole((half, d))]
    return pl.pallas_call(
        functools.partial(wgrad_attn_kernel, more=len(init)),
        grid=(3,),
        in_specs=[
            whole((n, d)), pl.BlockSpec((1, n, d), lambda s: (s, 0, 0)),
            pl.BlockSpec((n, half), lambda s: (0, jnp.minimum(s, 1))), whole((n, d)),
        ]
        + outs[: len(init)],
        out_specs=outs,
        out_shape=[sds((3, d, half), BF)] * 2 + [sds((half, d), BF)] * 2,
        compiler_params=params(),
        name="wgrad_attn",
    )(kept["normed"], back["dqkv"], kept["att"], back["gb"], *init)


RING = 8
VEC_ROWS = 16


def items_of(d):
    return ((0, 0, 2 * d, 1), (1, 0, d, -1), (2, 2 * d, d, -1), (2, 0, 2 * d, 1), (3, 0, d // 2, -1))


def vector_block(sums):
    s1, s2, sq, ff = sums
    d = s1.shape[1]
    wide = lambda v: [v[:, i : i + d] for i in range(0, v.shape[1], d)]
    rows = [s1[:2], s2[:4], sq[0:1], sq[2:3]] + wide(ff)
    used = 8 + ff.shape[1] // d
    return jnp.concatenate(rows + [jnp.zeros((VEC_ROWS - used, d), F32)], axis=0)


def as_own(block, fold):
    half = block.shape[1] // 2
    qv = block[6:8]
    return jnp.concatenate(
        [
            block[:6], jnp.concatenate([qv[:, half:], qv[:, :half]], axis=1),
            block[8 + fold : 8 + 2 * fold], block[8 : 8 + fold], block[8 + 2 * fold :],
        ],
        axis=0,
    )


def ring_kernel(*refs, n, items, fold):
    sums = refs[12:20]
    at = 20
    results, vsum_ref = refs[at : at + n], refs[at + n]
    at += n + 1
    outs, theirs = refs[at : at + n], refs[at + n : at + 2 * n]
    at += 2 * n
    own_qkv, own_pw, gift_qkv, gift_pw = refs[at : at + 4]
    owns = refs[8:10] + (own_qkv, own_pw)
    gifts = refs[10:12] + (gift_qkv, gift_pw)
    at += 4
    m = len(items)
    slots = refs[at : at + m]
    vbuf, vother, vmine, vslot, send, recv, xsend, xrecv, flushed, vsend, vrecv, vxs, vxr, early_sem = refs[
        at + m : at + m + 14
    ]
    early = refs[at + m + 14 :]
    normed, dqkv, att, gb = early[:4]
    parts = early[4:]
    fetches = fetch(list(zip(refs[:8], early)), early_sem)
    for c in fetches:
        c.start()
    mesh_id = pl.DeviceIdType.MESH
    me = lax.axis_index("dp")
    partner = {"tensor": 1 - lax.axis_index("tensor")}
    z, x = me // 2, me % 2
    pos = z + x * (RING - 1 - 2 * z)

    def member(p):
        p = p % RING
        return {"dp": 2 * p + (p // (RING // 2)) * (2 * RING - 1 - 4 * p)}

    barrier = pltpu.get_barrier_semaphore()
    for k in range(1, RING):
        pl.semaphore_signal(barrier, inc=1, device_id=member(pos + k), device_id_type=mesh_id)
    pl.semaphore_signal(barrier, inc=1, device_id=partner, device_id_type=mesh_id)
    pl.semaphore_wait(barrier, RING)

    def part(arrays, a, chunk):
        i, first, rows, _ = items[a]
        rows = rows // RING
        return arrays[i].at[pl.ds(pl.multiple_of(first + (chunk % RING) * rows, rows), rows)]

    def chunk_at(a, step):
        return pos + 2 * RING - items[a][3] * step

    def exchange(a, step):
        return pltpu.make_async_remote_copy(
            src_ref=part(gifts, a, chunk_at(a, step)),
            dst_ref=part(theirs, a, chunk_at(a, step)),
            send_sem=xsend.at[a, step],
            recv_sem=xrecv.at[a, step],
            device_id=partner,
            device_id_type=mesh_id,
        )

    def mine(a, step):
        exchange(a, step).wait_recv()
        chunk = chunk_at(a, step)
        return part(owns, a, chunk)[...].astype(F32) + part(theirs, a, chunk)[...].astype(F32)

    def remote(src, dst, a, step):
        return pltpu.make_async_remote_copy(
            src_ref=src,
            dst_ref=dst,
            send_sem=send.at[a, step],
            recv_sem=recv.at[a, step],
            device_id=member(pos + items[a][3] + RING),
            device_id_type=mesh_id,
        )

    def flush(a, k):
        chunk = chunk_at(a, k - 1)
        return pltpu.make_async_copy(
            part(outs, a, chunk), part(results, a, chunk), flushed.at[a, k]
        )

    def vcopy(k):
        return pltpu.make_async_remote_copy(
            src_ref=vmine,
            dst_ref=vslot.at[k - 1],
            send_sem=vsend.at[k - 1],
            recv_sem=vrecv.at[k - 1],
            device_id=member(pos + k),
            device_id_type=mesh_id,
        )

    vexchange = pltpu.make_async_remote_copy(
        src_ref=vbuf, dst_ref=vother, send_sem=vxs, recv_sem=vxr,
        device_id=partner, device_id_type=mesh_id,
    )

    def begin(arrays):
        for step in range(2):
            for a in arrays:
                exchange(a, step).start()
        for a in arrays:
            slots[a][0] = mine(a, 0).astype(BF)
            remote(slots[a].at[0], slots[a].at[1], a, 0).start()

    begin(range(2))
    vbuf[...] = vector_block([sums[i][...] + sums[4 + i][...] for i in range(4)])
    vexchange.start()
    for c in fetches:
        c.wait()
    d = normed.shape[1]
    half = d // 2
    for s in range(3):
        total = tn(normed[...], dqkv[s])
        rows = slice(s * d, (s + 1) * d)
        own_qkv[rows] = (total[:, :half] + parts[0][s].astype(F32)).astype(BF)
        gift_qkv[rows] = (total[:, half:] + parts[1][s].astype(F32)).astype(BF)
    own_pw[...] = (tn(att[:, :half], gb[...]) + parts[2][...].astype(F32)).astype(BF)
    gift_pw[...] = (tn(att[:, half:], gb[...]) + parts[3][...].astype(F32)).astype(BF)
    begin(range(2, m))

    def scatter(s, carry):
        for a in range(m):
            exchange(a, s + 1).start()
        for a in range(m):
            here = slots[a].at[s]
            own = mine(a, s)
            remote(here, here, a, s - 1).wait_recv()
            here[...] = (here[...].astype(F32) + own).astype(BF)
            remote(here, slots[a].at[s + 1], a, s).start()
        return carry

    lax.fori_loop(1, RING - 1, scatter, 0)
    vexchange.wait()
    vmine[...] = vbuf[...] + as_own(vother[...], fold)
    for k in range(1, RING):
        vcopy(k).start()
    for a in range(m):
        last = slots[a].at[RING - 1]
        own = mine(a, RING - 1)
        remote(last, last, a, RING - 2).wait_recv()
        done = part(outs, a, chunk_at(a, RING - 1))
        done[...] = (last[...].astype(F32) + own).astype(BF)
        remote(done, done, a, RING - 1).start()
        flush(a, 0).start()

    def gather(t, carry):
        for a in range(m):
            here = part(outs, a, chunk_at(a, t - 1))
            remote(here, here, a, RING - 2 + t).wait_recv()
            remote(here, here, a, RING - 1 + t).start()
            flush(a, t).start()
        return carry

    lax.fori_loop(1, RING - 1, gather, 0)
    total = vmine[...]
    for k in range(1, RING):
        vcopy(k).wait()
        total += vslot[k - 1]
    vsum_ref[...] = total
    for a in range(m):
        here = part(outs, a, chunk_at(a, RING - 2))
        remote(here, here, a, 2 * RING - 3).wait_recv()
        flush(a, RING - 1).start()
    for a in range(m):
        for s in range(RING - 1):
            remote(slots[a].at[0], slots[a].at[0], a, s).wait_send()
            here = part(outs, a, pos)
            remote(here, here, a, RING - 1 + s).wait_send()
        for s in range(RING):
            exchange(a, s).wait_send()
            flush(a, s).wait()


def ring(mlp, kept, back, parts, sums):
    d = kept["normed"].shape[1]
    shapes = [mlp[0].shape, mlp[2].shape, (3 * d, d // 2), (d // 2, d)]
    n = len(shapes)
    items = items_of(d)
    m = len(items)
    vmem = pl.BlockSpec(memory_space=pltpu.VMEM)
    hbm = pl.BlockSpec(memory_space=pl.ANY)
    dma = pltpu.SemaphoreType.DMA
    vec = pltpu.VMEM((VEC_ROWS, d), F32)
    early = (kept["normed"], back["dqkv"], kept["att"], back["gb"], *parts)
    out = pl.pallas_call(
        functools.partial(ring_kernel, n=n, items=items, fold=sums[3].shape[1] // (2 * d)),
        in_specs=[hbm] * 8 + [vmem] * 2 + [hbm] * 2 + [vmem] * 8,
        out_specs=[hbm] * n + [vmem],
        out_shape=[sds(a, BF) for a in shapes] + [sds((VEC_ROWS, d), F32)],
        scratch_shapes=[pltpu.VMEM(a, BF) for a in 2 * shapes + 2 * shapes[2:]]
        + [pltpu.VMEM((RING, rows // RING, shapes[i][1]), BF) for i, _, rows, _ in items]
        + [
            vec, vec, vec, pltpu.VMEM((RING - 1, VEC_ROWS, d), F32),
            dma((m, 2 * RING - 2)), dma((m, 2 * RING - 2)), dma((m, RING)), dma((m, RING)),
            dma((m, RING)),
            dma((RING - 1,)), dma((RING - 1,)), dma, dma, dma((8,)),
        ]
        + [pltpu.VMEM(a.shape, BF) for a in early],
        compiler_params=params(collective_id=1, has_side_effects=True),
        name="ring",
    )(
        *early, mlp[0], mlp[2], mlp[1], mlp[3], *sums,
    )
    return out[:n], out[n]


def dp_sum(mlp, kept, back, parts, sums):
    if lax.axis_size("dp") == RING:
        return ring(mlp, kept, back, parts, sums)
    other = lambda array: lax.ppermute(array, "tensor", [(0, 1), (1, 0)])
    qkv_o, qkv_p, pw_o, pw_p = wgrad_attn(kept, back, parts)
    rows = lambda qkv: qkv.reshape(-1, qkv.shape[2])
    owns = [mlp[0], mlp[2], rows(qkv_o), pw_o]
    gifts = [mlp[1], mlp[3], rows(qkv_p), pw_p]
    fold = sums[3].shape[1] // (2 * pw_o.shape[1])
    block = vector_block([a + b for a, b in zip(sums[:4], sums[4:])])
    summed = [lax.psum(a + other(b), "dp") for a, b in zip(owns, gifts)]
    return summed, lax.psum(block + as_own(other(block), fold), "dp")


def finish_kernel(*refs, fold):
    grads, vec, outs = refs[:4], refs[4], refs[5:]
    for g, out in zip(grads, outs):
        out[0] = g[...].astype(F32)

    @pl.when(pl.program_id(0) == 0)
    def _():
        half = vec.shape[1] // 2
        for i in range(6):
            outs[4 + i][...] = vec[i : i + 1]
        outs[10][0] = vec[6:8, :half]
        outs[11][...] = jnp.concatenate([vec[8 + i : 9 + i] for i in range(fold)], axis=1)


def finish(grads, vec):
    d = vec.shape[1]
    fold = grads[1].shape[1] // d
    steps = 8
    rows_in = lambda a: pl.BlockSpec((a.shape[0] // steps, a.shape[1]), lambda j: (j, 0))
    rows_out = lambda a: pl.BlockSpec((1, a.shape[0] // steps, a.shape[1]), lambda j: (0, j, 0))
    small = [(1, d)] * 6 + [(1, 2, d // 2), (1, fold * d)]
    return pl.pallas_call(
        functools.partial(finish_kernel, fold=fold),
        grid=(steps,),
        in_specs=[rows_in(a) for a in grads] + [whole(vec.shape)],
        out_specs=[rows_out(a) for a in grads] + [whole(a) for a in small],
        out_shape=[sds((1,) + a.shape, F32) for a in grads] + [sds(a, F32) for a in small],
        compiler_params=params(),
        name="finish",
    )(*grads, vec)


def starts_of(place):
    slots = [j + (j >= place) for j in range(SMALL_MB)]
    return [place * LEN_SMALL] + [
        slot * LEN_SMALL + (LEN_LARGE - LEN_SMALL) * (slot > place) for slot in slots
    ]


def layout(place):
    at = 0
    starts = starts_of(place)
    for c, (nimg, plen, vlen) in enumerate(CHUNKS):
        for i in range(nimg):
            yield starts[at], c, i * plen, plen, vlen
            at += 1


def cut_kernel(meta_ref, x_ref, *refs):
    outs, flat = refs[:-1], refs[-1]
    rows = x_ref.shape[0]
    flat[:rows] = x_ref[...].astype(F32)
    flat[rows:] = jnp.zeros((flat.shape[0] - rows, flat.shape[1]), F32)
    for place in range(SMALL_MB + 1):

        @pl.when(meta_ref[1 + meta_ref[0]] == place)
        def _():
            for start, c, r0, plen, vlen in layout(place):
                value = flat[start : start + plen]
                row = lax.broadcasted_iota(jnp.int32, value.shape, 0)
                outs[c][r0 : r0 + plen] = jnp.where(row < vlen, value, 0.0).astype(BF)


def cut(array, meta):
    rows = LEN_LARGE + SMALL_MB * LEN_SMALL
    d = array.shape[1]
    block = d // 3
    return pl.pallas_call(
        cut_kernel,
        grid_spec=pltpu.PrefetchScalarGridSpec(
            num_scalar_prefetch=1,
            grid=(3,),
            in_specs=[pl.BlockSpec((rows, block), lambda j, m: (m[0], j))],
            out_specs=[pl.BlockSpec((k * p, block), lambda j, m: (0, j)) for k, p, _ in CHUNKS],
            scratch_shapes=[pltpu.VMEM((rows + 16, block), F32)],
        ),
        out_shape=[sds((k * p, d), BF) for k, p, _ in CHUNKS],
        compiler_params=params(),
        name="cut",
    )(meta, array)


def join_kernel(meta_ref, *refs):
    count = len(CHUNKS)
    mine, theirs, out_ref, flat = refs[:count], refs[count : 2 * count], refs[-2], refs[-1]
    rows = flat.shape[0]
    for lane in range(2):
        for place in range(SMALL_MB + 1):
            for own, source in ((True, mine), (False, theirs)):

                @pl.when((meta_ref[1 + lane] == place) & ((meta_ref[0] == lane) == own))
                def _():
                    for start, c, r0, plen, vlen in layout(place):
                        value = source[c][r0 : r0 + plen].astype(F32)
                        flat[start : start + vlen] = value[:vlen]

        out_ref[lane * rows : (lane + 1) * rows] = flat[...].astype(BF)


def join(mine, theirs, meta):
    rows = LEN_LARGE + SMALL_MB * LEN_SMALL
    d = mine[0].shape[1]
    block = d // 3
    return pl.pallas_call(
        join_kernel,
        grid_spec=pltpu.PrefetchScalarGridSpec(
            num_scalar_prefetch=1,
            grid=(3,),
            in_specs=[pl.BlockSpec((k * p, block), lambda j, m: (0, j)) for k, p, _ in CHUNKS] * 2,
            out_specs=pl.BlockSpec((2 * rows, block), lambda j, m: (0, j)),
            scratch_shapes=[pltpu.VMEM((rows, block), F32)],
        ),
        out_shape=sds((2 * rows, d), BF),
        compiler_params=params(),
        name="join",
    )(meta, *mine, *theirs)


def blank_kernel(*refs):
    pass


def blank(like):
    shapes = [sds(a.shape, a.dtype) for a in like]
    return tuple(
        pl.pallas_call(
            blank_kernel,
            out_shape=shapes,
            out_specs=[pl.BlockSpec(memory_space=pl.ANY) for _ in shapes],
            name="blank",
        )()
    )


KEPT = ("normed", "qkv", "att", "lse", "mid", "n2", "act", "dg", "out")
BACK = ("g", "pre", "gb", "dqkv", "sums2", "sff", "sums_qkv", "sums1", "gx")


def after(value, *earlier):
    return lax.optimization_barrier((value, earlier))[0]


def body(
    patches, out_grad, large_place, norm1_gain, norm1_bias, qkv_weight, qv_bias, proj_weight,
    proj_bias, norm2_gain, norm2_bias, up_weight, up_bias, down_weight, down_bias,
):
    d = patches.shape[1]
    half = qkv_weight.shape[-1]
    section = lax.axis_index("section")
    lane = lax.axis_index("tensor")
    both = [(0, 1), (1, 0)]
    other = lambda array: lax.ppermute(array, "tensor", both)

    wqkv, pw, up, dn = qkv_weight[0], proj_weight[0], up_weight[0], down_weight[0]
    meta = jnp.concatenate([lane[None], large_place])
    xs = cut(patches, meta)
    bias = jnp.concatenate([qv_bias.reshape(1, 2 * half), up_bias], axis=1)
    bias_parts = after((bias, other(bias)), xs)
    w = {
        "g1": norm1_gain, "b1": norm1_bias, "g2": norm2_gain, "b2": norm2_bias,
        "pb": proj_bias, "db": down_bias,
        "wqkv_o": wqkv, "wqkv_p": other(wqkv), "pw_o": pw, "pw_p": other(pw),
        "up_o": up, "up_p": other(up), "dn_o": dn, "dn_p": other(dn),
        **dict(zip(("bias_o", "bias_p"), bias_parts)),
    }


    large, smalls = 0, 1
    gs = cut(out_grad, meta)

    def pick(on, make, otherwise=None):
        like = jax.eval_shape(make)
        return lax.cond(
            section == on,
            lambda: tuple(make()),
            lambda: blank(like) if otherwise is None else tuple(otherwise),
        )

    def fwd(c, on, x, otherwise=None):
        return pick(on, lambda: forward(x, w, CHUNKS[c]), otherwise)

    def bwd(c, on, g, x, kept, otherwise=None):
        kept = dict(zip(KEPT, kept))
        return pick(on, lambda: backward(g, x, kept, w, CHUNKS[c]), otherwise)

    down = lambda array: lax.ppermute(array, "section", [(0, 1)])
    up_ = lambda array: lax.ppermute(array, "section", [(1, 0)])

    kept_s = fwd(smalls, 0, xs[smalls])
    in_s = down(kept_s[-1])
    x_l = after(xs[large], kept_s[-1])
    kept_l = fwd(large, 0, x_l)
    in_l = down(kept_l[-1])
    in_s = after(in_s, kept_l[-1])
    kept_s = fwd(smalls, 1, in_s, kept_s)
    back_s = bwd(smalls, 1, gs[smalls], in_s, kept_s)
    sent_s = up_(back_s[-1])
    in_l = after(in_l, back_s[-1])
    kept_l = fwd(large, 1, in_l, kept_l)
    back_l = bwd(large, 1, gs[large], in_l, kept_l)
    sent_l = up_(back_l[-1])
    back_s = bwd(smalls, 0, after(sent_s, back_l[-1]), xs[smalls], kept_s, back_s)
    named = lambda names, values: dict(zip(names, values))
    part_mlp = wgrad_mlp(named(KEPT, kept_s), named(BACK, back_s))
    part_attn = wgrad_attn(named(KEPT, kept_s), named(BACK, back_s))
    outs = [kept_l[-1], kept_s[-1]]
    outputs = join(outs, [other(a) for a in outs], meta)
    sent_l = after(sent_l, part_mlp, part_attn, outputs)
    back_l = bwd(large, 0, sent_l, xs[large], kept_l, back_l)
    mlp = wgrad_mlp(named(KEPT, kept_l), named(BACK, back_l), part_mlp)
    grads = [back_l[-1], back_s[-1]]
    input_grads = join(grads, [other(a) for a in grads], meta)

    sums = lambda back: [named(BACK, back)[k] for k in ("sums1", "sums2", "sums_qkv", "sff")]
    summed, vec = dp_sum(
        mlp, named(KEPT, kept_l), named(BACK, back_l), part_attn, sums(back_s) + sums(back_l)
    )
    g_dn, g_up, g_qkv, g_pw, g1, b1, g2, b2, pb, db, qv, ub = finish(summed, vec)
    return (
        outputs[None], input_grads[None], g1, b1, g_qkv.reshape(1, 3, d, half), qv, g_pw, pb,
        g2, b2, g_up, ub, g_dn, db,
    )


def solution(mesh):
    placed = (
        P("dp", None), P("dp", None), P("dp"), P("section", None), P("section", None),
        P("section", None, None, "tensor"), P("section", None, "tensor"),
        P("section", "tensor", None), P("section", None), P("section", None),
        P("section", None), P("section", None, "tensor"), P("section", "tensor"),
        P("section", "tensor", None), P("section", None),
    )
    return jax.shard_map(
        body,
        mesh=mesh,
        in_specs=placed,
        out_specs=(
            P("section", "dp", None), P("section", "dp", None), P("section", None),
            P("section", None), P("section", None, None, "tensor"), P("section", None, "tensor"),
            P("section", "tensor", None), P("section", None), P("section", None),
            P("section", None), P("section", None, "tensor"), P("section", "tensor"),
            P("section", "tensor", None), P("section", None),
        ),
        check_vma=False,
    )
```
